32 devices in a mesh: grp: 2 (over core), dom: 8 (over z, x), sub: 2 (over y).
Axes of the slice: x: 2, y: 2, z: 4, core: 2. Of those that a mesh axis runs over, the one named last changes fastest.
Arguments:
- positions: float32 [3, 8192], P(None, ('grp', 'dom', 'sub')), may hold values from 0 to 4
- charges: float32 [8192], P(('grp', 'dom', 'sub')), may hold values from -3 to 3
- polar: float32 [8192], P(('grp', 'dom', 'sub')), may hold values from 0.1 to 0.6
- features: bfloat16 [8192, 256], P(('grp', 'dom', 'sub')), may hold values from -6 to 6
- neighbours: int32 [8192, 32], P(('grp', 'dom', 'sub')), may hold values from 0 to 512, as said below
- send_rows: int32 [2, 4096], P(None, ('grp', 'dom', 'sub')), may hold values from 0 to 255
- blocks: int32 [128], P(('grp', 'dom', 'sub')), may hold values from 0 to 31
- radial_in: bfloat16 [2, 8, 64], replicated, may hold values from -2 to 2
- radial_mid: bfloat16 [2, 2, 64, 64], replicated, may hold values from -0.75 to 0.75
- radial_out: bfloat16 [2, 64, 256], replicated, may hold values from -0.75 to 0.75
- node_in: bfloat16 [2, 256, 256], replicated, may hold values from -0.375 to 0.375
- node_out: bfloat16 [2, 256, 256], replicated, may hold values from -0.375 to 0.375
- field_gain: float32 [256], replicated, may hold values from -3 to 3
- readout: bfloat16 [256, 2], replicated, may hold values from -0.375 to 0.375
Outputs:
- site_result: float32 [3, 8192], P(None, ('grp', 'dom', 'sub'))
- response: float32 [3, 8192], P(None, ('grp', 'dom', 'sub'))
The draws below stay inside these ranges and needn't reach their ends.
Inputs may be any that keep to these rules, and one draw needn't show every extreme that they name: `neighbours`: entries below 256 name the block's own sites, entries from 256 to 511 its lent sites, 512 an empty slot; empty slots follow the used ones. `blocks`: repeats may occur.
All inputs are finite; a program needn't handle non-finite values.
Results may differ from the reference program's by a relative error of at most 0.0022.
The reference program's roundings to bfloat16 on the way count: a program that leaves them out, or rounds other values in their place, can miss the bound.
Values may be sent and summed in bfloat16 or wider, within the bound.
A program may use at most 64 MiB of HBM per device.

```python
import math
import jax
import jax.numpy as jnp
from jax import lax

CHANNELS = 256
RADIAL = 64
BASIS = 8
NEIGHBOURS = 32
LAYERS = 2
SWEEPS = 4
ROWS = 256
HALO = 128
BLOCK = 128
LISTED = 4
SITES = 8192
RIMS = 4096
LISTS = 128
NBLOCKS = 32
N_DOM = 8
N_SUB = 2


def draw_neighbours(key, part):
    pick_key, count_key, rim_key, side_key = jax.random.split(jax.random.fold_in(key, 17), 4)
    own_pick = jax.random.randint(pick_key, (SITES, NEIGHBOURS), 0, ROWS)
    rim_pick = ROWS + jax.random.randint(rim_key, (SITES, NEIGHBOURS), 0, 2 * HALO)
    coin = jax.random.randint(side_key, (SITES, NEIGHBOURS), 0, 4)
    picked = jnp.where(coin < 3, rim_pick, own_pick)
    counts = jax.random.randint(count_key, (SITES, 1), NEIGHBOURS // 2, NEIGHBOURS + 1)
    slot_index = lax.broadcasted_iota(jnp.int32, (SITES, NEIGHBOURS), 1)
    return jnp.where(slot_index < counts, picked, ROWS + 2 * HALO).astype(jnp.int32)


def with_ends(result, stream_key, low, high):
    longest = result.shape.index(max(result.shape))
    spots = []
    for shift in (0, 1):
        where = [jax.random.randint(jax.random.fold_in(stream_key, axis), (), 0, length) for axis, length in enumerate(result.shape)]
        where[longest] = (where[longest] + shift) % result.shape[longest]
        spots.append(tuple(where))
    return result.at[spots[0]].set(low).at[spots[1]].set(high)


def block_scale(own_key, extent, pieces, smallest, top_value):
    level, own = 1.0, jax.random.fold_in(own_key, 6)
    for position, blocks in pieces:
        heights = jnp.exp(jax.random.uniform(jax.random.fold_in(own, position), (blocks,), jnp.float32, smallest / len(pieces), top_value / len(pieces)))
        level = level * jnp.repeat(heights, extent[position] // blocks).reshape([-1 if axis == position else 1 for axis in range(len(extent))])
    return level


def normal_values(own_key, extent, deviation, reach, pieces=(), kind=jnp.bfloat16):
    values = deviation * jax.random.normal(own_key, extent, jnp.float32)
    if pieces:
        values = values * block_scale(own_key, extent, pieces, -0.22, 0.18)
    return jnp.clip(values, -reach, reach).astype(kind)


def setup_inputs(seed: int = 0) -> dict:
    keys = jax.random.split(jax.random.key(seed), 15)
    return {
        "positions": jnp.clip(4.0 * jax.random.uniform(keys[0], (3, SITES), jnp.float32) ** block_scale(keys[0], (3, SITES), ((1, 32),), -0.2, 0.2), 0.0, 4.0),
        "charges": normal_values(keys[1], (SITES,), 0.5, 3.0, ((0, 32),), jnp.float32),
        "polar": jnp.clip(jnp.exp(math.log(0.6) - 1.7917595 * jax.random.uniform(keys[2], (SITES,), jnp.float32) ** block_scale(keys[2], (SITES,), ((0, 32),), -0.2, 0.2)), 0.1, 0.6),
        "features": normal_values(keys[3], (SITES, CHANNELS), 1.0, 6.0, ((0, 32),)),
        "neighbours": draw_neighbours(jax.random.fold_in(keys[14], 71), 0),
        "send_rows": with_ends(jax.random.randint(keys[5], (2, RIMS), 0, ROWS), jax.random.fold_in(keys[5], 1), 0, ROWS - 1).astype(jnp.int32),
        "blocks": with_ends(jax.random.randint(keys[6], (LISTS,), 0, NBLOCKS), jax.random.fold_in(keys[6], 1), 0, NBLOCKS - 1).astype(jnp.int32),
        "radial_in": normal_values(keys[7], (LAYERS, BASIS, RADIAL), BASIS ** -0.5, 2.0),
        "radial_mid": normal_values(keys[8], (LAYERS, 2, RADIAL, RADIAL), RADIAL ** -0.5, 0.75),
        "radial_out": normal_values(keys[9], (LAYERS, RADIAL, CHANNELS), RADIAL ** -0.5, 0.75),
        "node_in": normal_values(keys[10], (LAYERS, CHANNELS, CHANNELS), CHANNELS ** -0.5, 0.375),
        "node_out": normal_values(keys[11], (LAYERS, CHANNELS, CHANNELS), CHANNELS ** -0.5, 0.375),
        "field_gain": normal_values(keys[12], (CHANNELS,), 0.5, 3.0, (), jnp.float32),
        "readout": normal_values(keys[13], (CHANNELS, 2), CHANNELS ** -0.5, 0.375),
    }


SMOOTH = 1.0
GAMMA = 1.0
SPACING = 0.75

def field_at(target, source, charge, dipole):
    tile_count = target.shape[1] // BLOCK
    tiles = target.reshape(3, tile_count, BLOCK).transpose(1, 0, 2)

    def one_tile(target_tile):
        offset = target_tile[:, :, None] - source[:, None, :]
        dist_sq = lax.optimization_barrier(jnp.sum(offset * offset, axis=0)) + SMOOTH
        inverse = lax.rsqrt(dist_sq)
        inverse_cube = inverse * inverse * inverse
        inverse_fifth = inverse_cube * inverse * inverse
        projected = lax.optimization_barrier(jnp.sum(offset * dipole[:, None, :], axis=0))
        source_scale = charge[None, :] * inverse_cube + 3.0 * projected * inverse_fifth
        return lax.optimization_barrier(jnp.sum(offset * source_scale[None] - dipole[:, None, :] * inverse_cube[None], axis=2))
    return lax.map(one_tile, tiles).transpose(1, 0, 2).reshape(3, -1)

def edge_geometry(local_data, site_table, neighbour_list):
    source = site_table[:3][:, neighbour_list]
    offset = local_data[:3][:, :, None] - source
    dist_sq = lax.optimization_barrier(jnp.sum(offset * offset, axis=0)) + SMOOTH
    return (offset, dist_sq)

def pair_field(offset, dist_sq, source_charge, source_dipole):
    inverse = lax.rsqrt(dist_sq)
    inverse_cube = inverse * inverse * inverse
    inverse_fifth = inverse_cube * inverse * inverse
    projected = lax.optimization_barrier(jnp.sum(offset * source_dipole, axis=0))
    source_scale = source_charge * inverse_cube + 3.0 * projected * inverse_fifth
    return lax.optimization_barrier(jnp.sum(offset * source_scale[None] - source_dipole * inverse_cube[None], axis=2))

def message_update(hidden, lifted_table, radial_basis, neighbour_list, w_first, w_middle, w_last, w_node):
    row_count, channel_count = hidden.shape
    slot_count = neighbour_list.shape[1]
    tile_count = row_count // BLOCK
    basis_tiles = radial_basis.reshape(tile_count, BLOCK * slot_count, radial_basis.shape[2])
    index_tiles = neighbour_list.reshape(tile_count, BLOCK * slot_count)

    def one_tile(operands):
        basis_tile, index_tile = operands
        first_hidden = jax.nn.silu(jnp.dot(basis_tile, w_first, preferred_element_type=jnp.float32)).astype(jnp.bfloat16)
        second_hidden = jax.nn.silu(jnp.dot(first_hidden, w_middle[0], preferred_element_type=jnp.float32)).astype(jnp.bfloat16)
        third_hidden = jax.nn.silu(jnp.dot(second_hidden, w_middle[1], preferred_element_type=jnp.float32)).astype(jnp.bfloat16)
        edge_weight = jnp.dot(third_hidden, w_last, preferred_element_type=jnp.float32)
        source = lifted_table[index_tile].astype(jnp.float32)
        summed = lax.optimization_barrier(jnp.sum((edge_weight * source).reshape(BLOCK, slot_count, channel_count), axis=1))
        return summed / slot_count
    message = lax.map(one_tile, (basis_tiles, index_tiles)).reshape(row_count, channel_count).astype(jnp.bfloat16)
    update = jax.nn.silu(jnp.dot(message, w_node, preferred_element_type=jnp.float32))
    return (hidden.astype(jnp.float32) + update).astype(jnp.bfloat16)

def rim_cols(values, rim_lists):
    to_next = jax.vmap(lambda v, s: v[:, s[0]])(values, rim_lists)
    to_prev = jax.vmap(lambda v, s: v[:, s[1]])(values, rim_lists)
    missing = jnp.zeros_like(to_next[:1])
    lower = jnp.concatenate([missing, to_next[:-1]], 0)
    upper = jnp.concatenate([to_prev[1:], missing], 0)
    empty_entry = jnp.zeros(values.shape[:-1] + (1,), values.dtype)
    return jnp.concatenate([values, lower, upper, empty_entry], -1)

def rim_rows(values, rim_lists):
    to_next = jax.vmap(lambda v, s: v[s[0]])(values, rim_lists)
    to_prev = jax.vmap(lambda v, s: v[s[1]])(values, rim_lists)
    missing = jnp.zeros_like(to_next[:1])
    lower = jnp.concatenate([missing, to_next[:-1]], 0)
    upper = jnp.concatenate([to_prev[1:], missing], 0)
    empty_entry = jnp.zeros((values.shape[0], 1) + values.shape[2:], values.dtype)
    return jnp.concatenate([values, lower, upper, empty_entry], 1)

def reference(positions, charges, polar, features, neighbours, send_rows, blocks, radial_in, radial_mid, radial_out, node_in, node_out, field_gain, readout):
    groups = N_DOM * N_SUB
    local_data = jnp.concatenate([positions, charges[None], polar[None]], 0).reshape(5, 2 * groups, ROWS).transpose(1, 0, 2)
    neighbour_lists = neighbours.reshape(2 * groups, ROWS, NEIGHBOURS)
    rim_lists = send_rows.reshape(2, 2 * groups, HALO).transpose(1, 0, 2)
    block_lists = blocks.reshape(2 * groups, LISTED)
    by_group = local_data.reshape(2, groups, 5, ROWS).transpose(0, 2, 1, 3).reshape(2, 5, groups * ROWS)

    def pick(other, listed):
        return jnp.take(other.reshape(5, -1, BLOCK), listed, axis=1).reshape(5, -1)
    near_learned = jax.vmap(lambda l: pick(by_group[1], l))(block_lists[:groups])
    near_solvent = jax.vmap(lambda l: pick(by_group[0], l))(block_lists[groups:])
    near_sites = jnp.concatenate([near_learned, near_solvent], 0)
    outside = lax.map(lambda a: field_at(a[0][:3], a[1][:3], a[1][3], jnp.zeros_like(a[1][:3])), (local_data, near_sites))
    site_tables = jnp.concatenate([rim_cols(local_data[:groups], rim_lists[:groups]), rim_cols(local_data[groups:], rim_lists[groups:])], 0)
    strength = jnp.sqrt(1.0 + lax.optimization_barrier(jnp.sum(outside * outside, axis=1)))
    learned_offset, learned_dist = jax.vmap(edge_geometry)(local_data[:groups], site_tables[:groups], neighbour_lists[:groups])
    centres = jnp.arange(BASIS, dtype=jnp.float32) * SPACING
    radial_basis = jnp.exp(-GAMMA * (jnp.sqrt(learned_dist)[..., None] - centres) ** 2).astype(jnp.bfloat16)
    initial = features.reshape(2 * groups, ROWS, CHANNELS)[:groups].astype(jnp.float32)
    hidden = (initial + strength[:groups, :, None] * field_gain[None, None, :]).astype(jnp.bfloat16)
    for layer_index in range(LAYERS):
        lifted = lax.map(lambda h: jnp.dot(h, node_in[layer_index], preferred_element_type=jnp.float32).astype(jnp.bfloat16), hidden)
        lifted_tables = rim_rows(lifted, rim_lists[:groups])
        hidden = lax.map(lambda a: message_update(a[0], a[1], a[2], a[3], radial_in[layer_index], radial_mid[layer_index], radial_out[layer_index], node_out[layer_index]), (hidden, lifted_tables, radial_basis, neighbour_lists[:groups]))
    readouts = lax.map(lambda h: jnp.dot(h, readout, preferred_element_type=jnp.float32), hidden)
    solvent_offset, solvent_dist = jax.vmap(edge_geometry)(local_data[groups:], site_tables[groups:], neighbour_lists[groups:])
    source_charge = jax.vmap(lambda t, n: t[3][n])(site_tables[groups:], neighbour_lists[groups:])
    fixed_field = outside[groups:] + jax.vmap(pair_field)(solvent_offset, solvent_dist, source_charge, jnp.zeros_like(solvent_offset))
    polar_rows = local_data[groups:, 4]
    dipole = polar_rows[:, None, :] * fixed_field
    for sweep_index in range(SWEEPS):
        dipole_tables = rim_cols(dipole, rim_lists[groups:])
        gathered = jax.vmap(lambda t, n: t[:, n])(dipole_tables, neighbour_lists[groups:])
        induced = jax.vmap(pair_field)(solvent_offset, solvent_dist, jnp.zeros_like(solvent_dist), gathered)
        dipole = polar_rows[:, None, :] * (fixed_field + induced)
    learned_charge = readouts[:, :, 0]
    source_q = jnp.concatenate([learned_charge, jnp.zeros_like(learned_charge)], 0)
    source_d = jnp.concatenate([jnp.zeros_like(dipole), dipole], 0)
    terms = lax.map(lambda a: field_at(a[0][:3], a[1][:3], a[2], a[3]), (near_sites, local_data, source_q, source_d))

    def collect(part_terms, part_lists):
        flat_terms = part_terms.reshape(groups, 3, LISTED, BLOCK).transpose(1, 0, 2, 3).reshape(3, groups * LISTED, BLOCK)
        summed = jnp.zeros((3, NBLOCKS, BLOCK), jnp.float32).at[:, part_lists.reshape(-1)].add(flat_terms)
        return summed.reshape(3, -1)
    from_learned = collect(terms[:groups], block_lists[:groups])
    from_solvent = collect(terms[groups:], block_lists[groups:])
    response = jnp.concatenate([from_solvent, from_learned], 1)
    learned_rows = jnp.stack([readouts[:, :, 0], readouts[:, :, 1], strength[:groups]], 1)
    site_result = jnp.concatenate([learned_rows, dipole], 0).transpose(1, 0, 2).reshape(3, -1)
    return (site_result, response)
```

```python
import functools

import jax
import jax.numpy as jnp
from jax import lax
from jax.experimental import pallas as pl
from jax.experimental.pallas import tpu as pltpu
from jax.sharding import PartitionSpec as P

SWEEPS = 4
BLOCK = 128
SMOOTH = 1.0
SPACING = 0.75
MESH = pl.DeviceIdType.MESH
INPUTS = 14
STRIP = 16
F32 = jnp.float32
BF16 = jnp.bfloat16


def silu_of_half(half):
    return half + half * jnp.tanh(half)


def lane_pick(rows, index):
    shape = index.shape
    return jnp.take_along_axis(
        jnp.broadcast_to(rows, shape), index, axis=1, mode="promise_in_bounds"
    )


def table_gather(pieces, local, chunk):
    total = jnp.zeros(local.shape, F32)
    for number, rows in pieces:
        total = jnp.where(chunk == number, lane_pick(rows, local), total)
    return total


def kernel(
    n_dom,
    n_sub,
    *refs,
):
    sources = refs[:INPUTS]
    (
    both,
    positions,
    charges,
    polar,
    features,
    neighbours,
    send_rows,
    blocks,
    radial_in,
    radial_mid,
    radial_out,
    node_in,
    node_out,
    field_gain,
    readout,
    in_sem,
    packet,
    everyone,
    near_rows,
    near_cols,
    own_rows,
    own_cols,
    extra_cols,
    rim_out,
    rim_in,
    geometry,
    hot,
    pick,
    wave,
    stage,
    third,
    edge_weight,
    wide_in,
    wide_mid,
    wide_out,
    tables,
    lent,
    hidden_ref,
    acc,
    outside,
    pairs,
    terms,
    term_out,
    term_in,
    all_send,
    all_recv,
    rim_send,
    rim_recv,
    lift_send,
    lift_recv,
    term_send,
    term_recv,
    ) = refs[INPUTS:]
    g = lax.axis_index("grp")
    p = lax.axis_index("dom") * n_sub + lax.axis_index("sub")
    site_result, response = both.at[0], both.at[1]
    n = n_dom * n_sub
    rows = positions.shape[1]
    own_blocks = rows // BLOCK
    slots = neighbours.shape[0]
    listed = blocks.shape[0]
    layers, basis, radial = radial_in.shape
    channels = features.shape[1]
    rim = send_rows.shape[1]
    pack = channels // radial
    groups = slots // pack
    strips = rows // STRIP
    other = 1 - g
    held = (
        positions,
        charges,
        polar,
        features,
        neighbours,
        send_rows,
        blocks,
        radial_in,
        radial_mid,
        radial_out,
        node_in,
        node_out,
        field_gain,
        readout,
    )
    early = (0, 1, 2, 4, 5, 6)
    late = (7, 8, 9, 3, 10, 11, 12, 13)

    def load(number):
        return pltpu.make_async_copy(sources[number], held[number], in_sem.at[number])

    for number in early:
        load(number).start()

    def place(group, q):
        return (group, lax.div(q, n_sub), lax.rem(q, n_sub))

    def peer(i):
        return lax.rem(p + i, n)

    barrier = pltpu.get_barrier_semaphore()

    @pl.loop(0, n)
    def _(i):
        pl.semaphore_signal(barrier, inc=1, device_id=place(other, peer(i)), device_id_type=MESH)

    @pl.when(p > 0)
    def _():
        pl.semaphore_signal(barrier, inc=1, device_id=place(g, p - 1), device_id_type=MESH)

    @pl.when(p < n - 1)
    def _():
        pl.semaphore_signal(barrier, inc=1, device_id=place(g, p + 1), device_id_type=MESH)

    @pl.when(g == 0)
    def _():
        for number in late:
            load(number).start()

    own_rows[...] = jnp.zeros_like(own_rows)
    for number in early:
        load(number).wait()
    own_rows[0:3, :] = positions[...]
    own_rows[3:4, :] = charges[...]
    own = own_rows[...]
    for b in range(own_blocks):
        packet[b] = own[:, b * BLOCK : (b + 1) * BLOCK]

    def fill_rims(step, values):
        for side in range(2):
            index = jnp.broadcast_to(send_rows[side : side + 1, :], (8, rim))
            rim_out[step, side] = table_gather(
                [(c, values[:, c * BLOCK : (c + 1) * BLOCK]) for c in range(own_blocks)],
                index & (BLOCK - 1),
                lax.shift_right_logical(index, 7),
            )

    def side_copy(src, dst, send, recv, step, side, q):
        return pltpu.make_async_remote_copy(
            src_ref=src,
            dst_ref=dst,
            send_sem=send.at[step, side],
            recv_sem=recv.at[step, side],
            device_id=place(g, q),
            device_id_type=MESH,
        )

    def rim_copy(step, side, q):
        return side_copy(
            rim_out.at[step, side], rim_in.at[step, side], rim_send, rim_recv, step, side, q
        )

    def lift_copy(layer, side, q):
        return side_copy(
            lent.at[layer, side],
            tables.at[layer, pl.ds(rows + side * rim, rim)],
            lift_send,
            lift_recv,
            layer,
            side,
            q,
        )

    def start(copy, step):
        @pl.when(p < n - 1)
        def _():
            copy(step, 0, p + 1).start()

        @pl.when(p > 0)
        def _():
            copy(step, 1, p - 1).start()

    def arrive(copy, step):
        @pl.when(p > 0)
        def _():
            copy(step, 0, p - 1).wait_recv()

        @pl.when(p < n - 1)
        def _():
            copy(step, 1, p + 1).wait_recv()

    def gone(copy, step):
        @pl.when(p < n - 1)
        def _():
            copy(step, 0, p + 1).wait_send()

        @pl.when(p > 0)
        def _():
            copy(step, 1, p - 1).wait_send()

    def prepare():
        width = rows + 2 * rim
        lane = lax.broadcasted_iota(jnp.int32, (rows, width), 1).astype(jnp.int16)
        listing = jnp.concatenate(
            [neighbours[...].astype(F32), jnp.zeros((BLOCK - slots, rows), F32)], axis=0
        ).T.astype(jnp.int32)
        one, none = jnp.ones((rows, width), BF16), jnp.zeros((rows, width), BF16)
        for k in range(slots):
            entry = jnp.broadcast_to(listing[:, k : k + 1], (rows, BLOCK)).astype(jnp.int16)
            entry = jnp.concatenate([entry] * (width // BLOCK), axis=1)
            mark = jnp.where(entry == lane, one, none)
            hot[k % pack, :, k // pack] = mark.reshape(strips, STRIP, width)
        lists = jnp.concatenate(
            [send_rows[...].astype(F32), jnp.zeros((6, rim), F32)], axis=0
        ).T.astype(jnp.int32)
        site = lax.broadcasted_iota(jnp.int32, (rim, rows), 1)
        for side in range(2):
            pick[side * rim : (side + 1) * rim, :] = jnp.where(
                lists[:, side : side + 1] == site, 1.0, 0.0
            ).astype(BF16)
        for number in late[:3]:
            load(number).wait()
        spread_r = (
            lax.broadcasted_iota(jnp.int32, (channels, radial), 0) % radial
            == lax.broadcasted_iota(jnp.int32, (channels, radial), 1)
        ).astype(F32).astype(BF16)
        spread_c = (
            lax.broadcasted_iota(jnp.int32, (radial, channels), 1) % radial
            == lax.broadcasted_iota(jnp.int32, (radial, channels), 0)
        ).astype(F32).astype(BF16)
        same_in = (
            lax.broadcasted_iota(jnp.int32, (pack * basis, channels), 0) // basis
            == lax.broadcasted_iota(jnp.int32, (pack * basis, channels), 1) // radial
        )
        same_mid = (
            lax.broadcasted_iota(jnp.int32, (channels, channels), 0) // radial
            == lax.broadcasted_iota(jnp.int32, (channels, channels), 1) // radial
        )
        for layer in range(layers):
            flat = jnp.dot(radial_in[layer], spread_c, preferred_element_type=F32)
            wide_in[layer] = jnp.where(
                same_in, jnp.concatenate([0.5 * flat] * pack, axis=0), 0.0
            ).astype(BF16)
            for m in range(2):
                flat = jnp.dot(
                    jnp.dot(spread_r, radial_mid[layer, m], preferred_element_type=F32).astype(
                        BF16
                    ),
                    spread_c,
                    preferred_element_type=F32,
                )
                wide_mid[layer, m] = jnp.where(same_mid, 0.5 * flat, 0.0).astype(BF16)
            for j in range(pack):
                wide_out[layer, j] = jnp.zeros((channels, channels), BF16)
                wide_out[layer, j, j * radial : (j + 1) * radial, :] = radial_out[layer]

    fill_rims(0, own)

    @pl.when(p == 0)
    def _():
        for step in range(1 + SWEEPS):
            rim_in[step, 0] = jnp.zeros((8, rim), F32)
        for layer in range(layers):
            tables[layer, rows : rows + rim] = jnp.zeros((rim, channels), BF16)

    @pl.when(p == n - 1)
    def _():
        for step in range(1 + SWEEPS):
            rim_in[step, 1] = jnp.zeros((8, rim), F32)
        for layer in range(layers):
            tables[layer, rows + rim :] = jnp.zeros((rim, channels), BF16)

    @pl.when(g == 0)
    def _():
        prepare()

    pl.semaphore_wait(barrier, n + (p > 0).astype(jnp.int32) + (p < n - 1).astype(jnp.int32))

    def packet_copy(i):
        return pltpu.make_async_remote_copy(
            src_ref=packet,
            dst_ref=everyone.at[pl.ds(p * own_blocks, own_blocks)],
            send_sem=all_send,
            recv_sem=all_recv,
            device_id=place(other, peer(i)),
            device_id_type=MESH,
        )

    start(rim_copy, 0)

    @pl.loop(0, n)
    def _(i):
        packet_copy(i).start()

    own_cols[...] = own.T

    def field(targets, source_cols, count, charge, dipole):
        x, y, z = (targets[c : c + 1, :] for c in range(3))
        width = targets.shape[1]

        def step(i, sums):
            at = pl.ds(pl.multiple_of(i * 8, 8), 8)
            source = source_cols[at, :]
            rx = x - source[:, 0:1]
            ry = y - source[:, 1:2]
            rz = z - source[:, 2:3]
            w = lax.rsqrt(rx * rx + ry * ry + rz * rz + SMOOTH)
            w2 = w * w
            w3 = w2 * w
            if not dipole:
                s = charge(at, source) * w3
                return (sums[0] + rx * s, sums[1] + ry * s, sums[2] + rz * s)
            d = extra_cols[at, :]
            dx, dy, dz = d[:, 0:1], d[:, 1:2], d[:, 2:3]
            s = 3.0 * (rx * dx + ry * dy + rz * dz) * (w3 * w2)
            return (
                sums[0] + (rx * s - dx * w3),
                sums[1] + (ry * s - dy * w3),
                sums[2] + (rz * s - dz * w3),
            )

        zero = jnp.zeros((8, width), F32)
        sums = lax.fori_loop(0, count // 8, step, (zero, zero, zero), unroll=16)
        return [jnp.sum(s, axis=0, keepdims=True) for s in sums]

    def edges():
        arrive(rim_copy, 0)
        for tile in range(own_blocks):
            at = slice(tile * BLOCK, (tile + 1) * BLOCK)
            index = neighbours[:, at]
            local = index & (BLOCK - 1)
            chunk = lax.shift_right_logical(index, 7)
            picked = []
            for c in range(4):
                pieces = [
                    (b, own_rows[c : c + 1, b * BLOCK : (b + 1) * BLOCK])
                    for b in range(own_blocks)
                ] + [(own_blocks + side, rim_in[0, side, c : c + 1, :]) for side in range(2)]
                picked.append(table_gather(pieces, local, chunk))
            ox, oy, oz = (own_rows[c : c + 1, at] - picked[c] for c in range(3))
            dist_sq = ox * ox + oy * oy + oz * oz + SMOOTH
            yield at, (ox, oy, oz), dist_sq, picked[3], local, chunk

    def send_terms(charge, dipole):
        width = listed * BLOCK
        for half in range(0, width, 2 * BLOCK):
            out = field(
                near_rows[:, half : half + 2 * BLOCK], own_cols, rows, charge, dipole
            )
            for c in range(3):
                terms[c : c + 1, half : half + 2 * BLOCK] = out[c]

    centre = lax.broadcasted_iota(jnp.int32, (basis, rows), 0).astype(F32) * SPACING

    def radial_net():
        half = groups // 2
        spans = [range(half), range(half, groups)]
        for q in range(groups):
            parts = []
            for j in range(pack):
                away = jnp.broadcast_to(geometry[0, q * pack + j : q * pack + j + 1, :], (basis, rows))
                away = away - centre
                parts.append(jnp.exp(-(away * away)))
            turned = jnp.concatenate(parts, axis=0).T
            wave[q * rows : (q + 1) * rows, :] = turned.astype(BF16)
        for layer in range(layers):
            for step in range(3):
                for part, span in enumerate(spans):
                    at = slice(span[0] * rows, (span[-1] + 1) * rows)
                    if step == 0:
                        source, weight = wave[at, :], wide_in[layer]
                    else:
                        source, weight = stage[layer, step - 1, at, :], wide_mid[layer, step - 1]
                    h = silu_of_half(jnp.dot(source, weight, preferred_element_type=F32)).astype(BF16)
                    if step < 2:
                        stage[layer, step, at, :] = h
                    else:
                        for i, q in enumerate(span):
                            third[layer, :, q] = h[i * rows : (i + 1) * rows].reshape(
                                strips, STRIP, channels
                            )

    def own_part(layer):
        for j in range(pack):
            edge_weight[j] = jnp.dot(
                third[layer].reshape(groups * rows, channels),
                wide_out[layer, j],
                preferred_element_type=F32,
            ).reshape(strips, groups, STRIP, channels)
            gather_part(layer, j, 0, rows)

    def rim_part(layer):
        for j in range(pack):
            gather_part(layer, j, rows, 2 * rim)

    def gather_part(layer, j, first, count):
        source = jnp.dot(
            hot[j, :, :, :, first : first + count].reshape(groups * rows, count),
            tables[layer, first : first + count],
            preferred_element_type=F32,
        )
        product = edge_weight[j] * source.reshape(strips, groups, STRIP, channels)
        total = jnp.sum(product, axis=1)
        if first or j:
            total = acc[...] + total
        acc[...] = total

    @pl.when(g == 0)
    def _():
        for at, _, dist_sq, _, _, _ in edges():
            geometry[0, :, at] = jnp.sqrt(dist_sq)
        radial_net()

    @pl.when(g == 1)
    def _():
        for at, offset, dist_sq, source_charge, _, _ in edges():
            w = lax.rsqrt(dist_sq)
            w2 = w * w
            w3 = w2 * w
            s = source_charge * w3
            for c in range(3):
                geometry[c, :, at] = offset[c]
                extra = jnp.sum(offset[c] * s, axis=0, keepdims=True)
                pairs[c : c + 1, at] = extra
            geometry[3, :, at] = w3
            geometry[4, :, at] = 3.0 * (w3 * w2)

    pltpu.make_async_copy(everyone, everyone, all_recv).wait()
    for l in range(listed):
        tile = everyone[blocks[l]]
        near_rows[:, l * BLOCK : (l + 1) * BLOCK] = tile
        near_cols[l * BLOCK : (l + 1) * BLOCK, :] = tile.T

    out = field(own, near_cols, listed * BLOCK, lambda at, source: source[:, 3:4], False)
    for c in range(3):
        outside[c : c + 1, :] = out[c]

    @pl.when(g == 0)
    def _():
        for number in late[3:]:
            load(number).wait()
        fx, fy, fz = out
        strength = jnp.sqrt(1.0 + fx * fx + fy * fy + fz * fz)
        site_result[2:3, :] = strength
        strength_col = jnp.broadcast_to(strength, (8, rows)).T[:, 0:1]
        hidden_ref[...] = (features[...].astype(F32) + strength_col * field_gain[...]).astype(BF16)

        def lift(layer):
            lifted = jnp.dot(
                hidden_ref[...], node_in[layer], preferred_element_type=F32
            ).astype(BF16)
            picked = jnp.dot(pick[...], lifted, preferred_element_type=F32).astype(BF16)
            lent[layer] = picked.reshape(2, rim, channels)
            start(lift_copy, layer)
            tables[layer, 0:rows] = lifted

        for layer in range(layers):
            lift(layer)
            own_part(layer)
            arrive(lift_copy, layer)
            rim_part(layer)
            message = (acc[...].reshape(rows, channels) * (1.0 / slots)).astype(BF16)
            update = silu_of_half(
                0.5 * jnp.dot(message, node_out[layer], preferred_element_type=F32)
            )
            hidden_ref[...] = (hidden_ref[...].astype(F32) + update).astype(BF16)

        across = (((1,), (1,)), ((), ()))
        extra_cols[:, 0:2] = lax.dot_general(
            hidden_ref[...], readout[...], across, preferred_element_type=F32
        )
        site_result[0:2, :] = lax.dot_general(
            readout[...], hidden_ref[...], across, preferred_element_type=F32
        )
        send_terms(lambda at, source: extra_cols[at, 0:1], False)
        for layer in range(layers):
            gone(lift_copy, layer)

    @pl.when(g == 1)
    def _():
        gain = polar[...]
        outside[...] = outside[...] + pairs[...]
        dipole = [gain * outside[c : c + 1, :] for c in range(3)]
        for sweep in range(SWEEPS):
            step = 1 + sweep
            stacked = jnp.concatenate(dipole + [jnp.zeros((5, rows), F32)], axis=0)
            fill_rims(step, stacked)
            start(rim_copy, step)
            arrive(rim_copy, step)
            fresh = [[], [], []]
            for tile in range(own_blocks):
                at = slice(tile * BLOCK, (tile + 1) * BLOCK)
                index = neighbours[:, at]
                local = index & (BLOCK - 1)
                chunk = lax.shift_right_logical(index, 7)
                d = []
                for c in range(3):
                    pieces = [
                        (b, dipole[c][:, b * BLOCK : (b + 1) * BLOCK]) for b in range(own_blocks)
                    ] + [
                        (own_blocks + side, rim_in[step, side, c : c + 1, :]) for side in range(2)
                    ]
                    d.append(table_gather(pieces, local, chunk))
                r = [geometry[c, :, at] for c in range(3)]
                w3 = geometry[3, :, at]
                s = (r[0] * d[0] + r[1] * d[1] + r[2] * d[2]) * geometry[4, :, at]
                for c in range(3):
                    total = jnp.sum(r[c] * s - d[c] * w3, axis=0, keepdims=True)
                    fresh[c].append(gain[:, at] * (outside[c : c + 1, at] + total))
            dipole = [jnp.concatenate(f, axis=1) for f in fresh]
        for c in range(3):
            site_result[c : c + 1, :] = dipole[c]
        stacked = jnp.concatenate(dipole + [jnp.zeros((5, rows), F32)], axis=0)
        extra_cols[...] = stacked.T
        send_terms(None, True)
        for sweep in range(SWEEPS):
            gone(rim_copy, 1 + sweep)

    @pl.loop(0, n)
    def _(q):
        for b in range(own_blocks):
            total = jnp.zeros((3, BLOCK), F32)
            for l in range(listed):
                total = total + jnp.where(
                    blocks[l] == q * own_blocks + b, terms[:, l * BLOCK : (l + 1) * BLOCK], 0.0
                )
            term_out[q, b * 3 : (b + 1) * 3, :] = total

    def term_copy(i):
        return pltpu.make_async_remote_copy(
            src_ref=term_out.at[peer(i)],
            dst_ref=term_in.at[p],
            send_sem=term_send,
            recv_sem=term_recv,
            device_id=place(other, peer(i)),
            device_id_type=MESH,
        )

    @pl.loop(0, n)
    def _(i):
        term_copy(i).start()

    gone(rim_copy, 0)
    pltpu.make_async_copy(everyone, everyone, all_send).wait()
    pltpu.make_async_copy(term_in, term_in, term_recv).wait()

    total = jnp.sum(term_in[...], axis=0)
    for b in range(own_blocks):
        response[:, b * BLOCK : (b + 1) * BLOCK] = total[b * 3 : (b + 1) * 3, :]
    pltpu.make_async_copy(term_in, term_in, term_send).wait()


def local(n_dom, n_sub, *args):
    (
        positions,
        charges,
        polar,
        features,
        neighbours,
        send_rows,
        blocks,
        radial_in,
        radial_mid,
        radial_out,
        node_in,
        node_out,
        field_gain,
        readout,
    ) = args
    n = n_dom * n_sub
    rows = positions.shape[1]
    own_blocks = rows // BLOCK
    slots = neighbours.shape[1]
    listed = blocks.shape[0]
    layers, basis, radial = radial_in.shape
    channels = features.shape[1]
    rim = send_rows.shape[1]
    pack = channels // radial
    dma = pltpu.SemaphoreType.DMA
    operands = (
        positions,
        charges.reshape(1, -1),
        polar.reshape(1, -1),
        features,
        neighbours.T,
        send_rows,
        blocks,
        radial_in,
        radial_mid,
        radial_out,
        node_in,
        node_out,
        field_gain.reshape(1, -1),
        readout.T,
    )
    spaces = [pltpu.VMEM] * INPUTS
    spaces[6] = pltpu.SMEM
    both = pl.pallas_call(
        functools.partial(kernel, n_dom, n_sub),
        out_shape=jax.ShapeDtypeStruct((2, 3, rows), F32),
        in_specs=[pl.BlockSpec(memory_space=pl.ANY)] * INPUTS,
        out_specs=pl.BlockSpec(memory_space=pltpu.VMEM),
        scratch_shapes=[space(a.shape, a.dtype) for space, a in zip(spaces, operands)]
        + [
            dma((INPUTS,)),
            pltpu.VMEM((own_blocks, 8, BLOCK), F32),
            pltpu.VMEM((n * own_blocks, 8, BLOCK), F32),
            pltpu.VMEM((8, listed * BLOCK), F32),
            pltpu.VMEM((listed * BLOCK, 8), F32),
            pltpu.VMEM((8, rows), F32),
            pltpu.VMEM((rows, 8), F32),
            pltpu.VMEM((rows, 8), F32),
            pltpu.VMEM((1 + SWEEPS, 2, 8, rim), F32),
            pltpu.VMEM((1 + SWEEPS, 2, 8, rim), F32),
            pltpu.VMEM((5, slots, rows), F32),
            pltpu.VMEM((pack, rows // STRIP, slots // pack, STRIP, rows + 2 * rim), BF16),
            pltpu.VMEM((2 * rim, rows), BF16),
            pltpu.VMEM((slots // pack * rows, pack * basis), BF16),
            pltpu.VMEM((layers, 2, slots // pack * rows, channels), BF16),
            pltpu.VMEM((layers, rows // STRIP, slots // pack, STRIP, channels), BF16),
            pltpu.VMEM((pack, rows // STRIP, slots // pack, STRIP, channels), F32),
            pltpu.VMEM((layers, pack * basis, channels), BF16),
            pltpu.VMEM((layers, 2, channels, channels), BF16),
            pltpu.VMEM((layers, pack, channels, channels), BF16),
            pltpu.VMEM((layers, rows + 2 * rim, channels), BF16),
            pltpu.VMEM((layers, 2, rim, channels), BF16),
            pltpu.VMEM((rows, channels), BF16),
            pltpu.VMEM((rows // STRIP, STRIP, channels), F32),
            pltpu.VMEM((3, rows), F32),
            pltpu.VMEM((3, rows), F32),
            pltpu.VMEM((3, listed * BLOCK), F32),
            pltpu.VMEM((n, own_blocks * 3, BLOCK), F32),
            pltpu.VMEM((n, own_blocks * 3, BLOCK), F32),
            dma(()),
            dma(()),
            dma((1 + SWEEPS, 2)),
            dma((1 + SWEEPS, 2)),
            dma((layers, 2)),
            dma((layers, 2)),
            dma(()),
            dma(()),
        ],
        compiler_params=pltpu.CompilerParams(
            collective_id=0, has_side_effects=True, vmem_limit_bytes=56 * 2**20
        ),
    )(*operands)
    return both[0], both[1]


def solution(mesh):
    sites = ("grp", "dom", "sub")
    in_specs = (
        P(None, sites),
        P(sites),
        P(sites),
        P(sites, None),
        P(sites, None),
        P(None, sites),
        P(sites),
    ) + (P(),) * 7
    out_specs = (P(None, sites), P(None, sites))
    body = functools.partial(local, mesh.shape["dom"], mesh.shape["sub"])
    return jax.shard_map(body, mesh=mesh, in_specs=in_specs, out_specs=out_specs, check_vma=False)
```

```python
import functools

import jax
import jax.numpy as jnp
from jax import lax
from jax.experimental import pallas as pl
from jax.experimental.pallas import tpu as pltpu
from jax.sharding import PartitionSpec as P

SWEEPS = 4
BLOCK = 128
SMOOTH = 1.0
SPACING = 0.75
MESH = pl.DeviceIdType.MESH
INPUTS = 14
STRIP = 16
F32 = jnp.float32
BF16 = jnp.bfloat16


def silu_of_half(half):
    return half + half * jnp.tanh(half)


def lane_pick(rows, index):
    shape = index.shape
    return jnp.take_along_axis(
        jnp.broadcast_to(rows, shape), index, axis=1, mode="promise_in_bounds"
    )


def table_gather(pieces, local, chunk):
    total = jnp.zeros(local.shape, F32)
    for number, rows in pieces:
        total = jnp.where(chunk == number, lane_pick(rows, local), total)
    return total


def kernel(
    n_dom,
    n_sub,
    *refs,
):
    sources = refs[:INPUTS]
    (
    both,
    positions,
    charges,
    polar,
    features,
    neighbours,
    send_rows,
    blocks,
    radial_in,
    radial_mid,
    radial_out,
    node_in,
    node_out,
    field_gain,
    readout,
    in_sem,
    packet,
    everyone,
    near_rows,
    near_cols,
    own_rows,
    own_cols,
    extra_cols,
    rim_out,
    rim_in,
    geometry,
    hot,
    pick,
    wave,
    stage,
    third,
    edge_weight,
    wide_in,
    wide_mid,
    wide_out,
    tables,
    lent,
    hidden_ref,
    acc,
    outside,
    pairs,
    terms,
    term_out,
    term_in,
    all_send,
    all_recv,
    rim_send,
    rim_recv,
    lift_send,
    lift_recv,
    term_send,
    term_recv,
    ) = refs[INPUTS:]
    g = lax.axis_index("grp")
    p = lax.axis_index("dom") * n_sub + lax.axis_index("sub")
    site_result, response = both.at[0], both.at[1]
    n = n_dom * n_sub
    rows = positions.shape[1]
    own_blocks = rows // BLOCK
    slots = neighbours.shape[0]
    listed = blocks.shape[0]
    layers, basis, radial = radial_in.shape
    channels = features.shape[1]
    rim = send_rows.shape[1]
    pack = channels // radial
    groups = slots // pack
    strips = rows // STRIP
    other = 1 - g
    held = (
        positions,
        charges,
        polar,
        features,
        neighbours,
        send_rows,
        blocks,
        radial_in,
        radial_mid,
        radial_out,
        node_in,
        node_out,
        field_gain,
        readout,
    )
    early = (0, 1, 2, 4, 5, 6)
    late = (7, 8, 9, 3, 10, 11, 12, 13)

    def load(number):
        return pltpu.make_async_copy(sources[number], held[number], in_sem.at[number])

    for number in early:
        load(number).start()

    def place(group, q):
        return (group, lax.div(q, n_sub), lax.rem(q, n_sub))

    def peer(i):
        return lax.rem(p + i, n)

    barrier = pltpu.get_barrier_semaphore()

    @pl.loop(0, n)
    def _(i):
        pl.semaphore_signal(barrier, inc=1, device_id=place(other, peer(i)), device_id_type=MESH)

    @pl.when(p > 0)
    def _():
        pl.semaphore_signal(barrier, inc=1, device_id=place(g, p - 1), device_id_type=MESH)

    @pl.when(p < n - 1)
    def _():
        pl.semaphore_signal(barrier, inc=1, device_id=place(g, p + 1), device_id_type=MESH)

    @pl.when(g == 0)
    def _():
        for number in late:
            load(number).start()

    own_rows[...] = jnp.zeros_like(own_rows)
    for number in early:
        load(number).wait()
    own_rows[0:3, :] = positions[...]
    own_rows[3:4, :] = charges[...]
    own = own_rows[...]
    for b in range(own_blocks):
        packet[b] = own[0:4, b * BLOCK : (b + 1) * BLOCK]

    def fill_rims(step, values):
        for side in range(2):
            index = jnp.broadcast_to(send_rows[side : side + 1, :], (4, rim))
            rim_out[step, side] = table_gather(
                [(c, values[:, c * BLOCK : (c + 1) * BLOCK]) for c in range(own_blocks)],
                index & (BLOCK - 1),
                lax.shift_right_logical(index, 7),
            )

    def side_copy(src, dst, send, recv, step, side, q):
        return pltpu.make_async_remote_copy(
            src_ref=src,
            dst_ref=dst,
            send_sem=send.at[step, side],
            recv_sem=recv.at[step, side],
            device_id=place(g, q),
            device_id_type=MESH,
        )

    def rim_copy(step, side, q):
        return side_copy(
            rim_out.at[step, side], rim_in.at[step, side], rim_send, rim_recv, step, side, q
        )

    def lift_copy(layer, side, q):
        return side_copy(
            lent.at[layer, side],
            tables.at[layer, pl.ds(rows + side * rim, rim)],
            lift_send,
            lift_recv,
            layer,
            side,
            q,
        )

    def start(copy, step):
        @pl.when(p < n - 1)
        def _():
            copy(step, 0, p + 1).start()

        @pl.when(p > 0)
        def _():
            copy(step, 1, p - 1).start()

    def arrive(copy, step):
        @pl.when(p > 0)
        def _():
            copy(step, 0, p - 1).wait_recv()

        @pl.when(p < n - 1)
        def _():
            copy(step, 1, p + 1).wait_recv()

    def gone(copy, step):
        @pl.when(p < n - 1)
        def _():
            copy(step, 0, p + 1).wait_send()

        @pl.when(p > 0)
        def _():
            copy(step, 1, p - 1).wait_send()

    def prepare():
        width = rows + 2 * rim
        lane = lax.broadcasted_iota(jnp.int32, (rows, width), 1).astype(jnp.int16)
        listing = jnp.concatenate(
            [neighbours[...].astype(F32), jnp.zeros((BLOCK - slots, rows), F32)], axis=0
        ).T.astype(jnp.int32)
        one, none = jnp.ones((rows, width), BF16), jnp.zeros((rows, width), BF16)
        for k in range(slots):
            entry = jnp.broadcast_to(listing[:, k : k + 1], (rows, BLOCK)).astype(jnp.int16)
            entry = jnp.concatenate([entry] * (width // BLOCK), axis=1)
            mark = jnp.where(entry == lane, one, none)
            hot[k % pack, :, k // pack] = mark.reshape(strips, STRIP, width)
        lists = jnp.concatenate(
            [send_rows[...].astype(F32), jnp.zeros((6, rim), F32)], axis=0
        ).T.astype(jnp.int32)
        site = lax.broadcasted_iota(jnp.int32, (rim, rows), 1)
        for side in range(2):
            pick[side * rim : (side + 1) * rim, :] = jnp.where(
                lists[:, side : side + 1] == site, 1.0, 0.0
            ).astype(BF16)

    def spread():
        for number in late[:3]:
            load(number).wait()
        spread_r = (
            lax.broadcasted_iota(jnp.int32, (channels, radial), 0) % radial
            == lax.broadcasted_iota(jnp.int32, (channels, radial), 1)
        ).astype(F32).astype(BF16)
        spread_c = (
            lax.broadcasted_iota(jnp.int32, (radial, channels), 1) % radial
            == lax.broadcasted_iota(jnp.int32, (radial, channels), 0)
        ).astype(F32).astype(BF16)
        same_in = (
            lax.broadcasted_iota(jnp.int32, (pack * basis, channels), 0) // basis
            == lax.broadcasted_iota(jnp.int32, (pack * basis, channels), 1) // radial
        )
        same_mid = (
            lax.broadcasted_iota(jnp.int32, (channels, channels), 0) // radial
            == lax.broadcasted_iota(jnp.int32, (channels, channels), 1) // radial
        )
        for layer in range(layers):
            flat = jnp.dot(radial_in[layer], spread_c, preferred_element_type=F32)
            wide_in[layer] = jnp.where(
                same_in, jnp.concatenate([0.5 * flat] * pack, axis=0), 0.0
            ).astype(BF16)
            for m in range(2):
                flat = jnp.dot(
                    jnp.dot(spread_r, radial_mid[layer, m], preferred_element_type=F32).astype(
                        BF16
                    ),
                    spread_c,
                    preferred_element_type=F32,
                )
                wide_mid[layer, m] = jnp.where(same_mid, 0.5 * flat, 0.0).astype(BF16)
            for j in range(pack):
                wide_out[layer, j] = jnp.zeros((channels, channels), BF16)
                wide_out[layer, j, j * radial : (j + 1) * radial, :] = radial_out[layer]

    fill_rims(0, own[0:4])

    @pl.when(p == 0)
    def _():
        for step in range(1 + SWEEPS):
            rim_in[step, 0] = jnp.zeros((4, rim), F32)
        for layer in range(layers):
            tables[layer, rows : rows + rim] = jnp.zeros((rim, channels), BF16)

    @pl.when(p == n - 1)
    def _():
        for step in range(1 + SWEEPS):
            rim_in[step, 1] = jnp.zeros((4, rim), F32)
        for layer in range(layers):
            tables[layer, rows + rim :] = jnp.zeros((rim, channels), BF16)

    @pl.when(g == 0)
    def _():
        prepare()

    pl.semaphore_wait(barrier, n + (p > 0).astype(jnp.int32) + (p < n - 1).astype(jnp.int32))

    def packet_copy(i):
        return pltpu.make_async_remote_copy(
            src_ref=packet,
            dst_ref=everyone.at[pl.ds(p * own_blocks, own_blocks)],
            send_sem=all_send,
            recv_sem=all_recv,
            device_id=place(other, peer(i)),
            device_id_type=MESH,
        )

    start(rim_copy, 0)

    @pl.loop(0, n, unroll=4)
    def _(i):
        packet_copy(i).start()

    @pl.when(g == 0)
    def _():
        spread()

    own_cols[...] = own.T

    def field(targets, source_cols, count, charge, dipole):
        x, y, z = (targets[c : c + 1, :] for c in range(3))
        width = targets.shape[1]

        def step(i, sums):
            at = pl.ds(pl.multiple_of(i * 8, 8), 8)
            source = source_cols[at, :]
            rx = x - source[:, 0:1]
            ry = y - source[:, 1:2]
            rz = z - source[:, 2:3]
            w = lax.rsqrt(rx * rx + ry * ry + rz * rz + SMOOTH)
            w2 = w * w
            w3 = w2 * w
            if not dipole:
                s = charge(at, source) * w3
                return (sums[0] + rx * s, sums[1] + ry * s, sums[2] + rz * s)
            d = extra_cols[at, :]
            dx, dy, dz = d[:, 0:1], d[:, 1:2], d[:, 2:3]
            s = 3.0 * (rx * dx + ry * dy + rz * dz) * (w3 * w2)
            return (
                sums[0] + (rx * s - dx * w3),
                sums[1] + (ry * s - dy * w3),
                sums[2] + (rz * s - dz * w3),
            )

        zero = jnp.zeros((8, width), F32)
        sums = lax.fori_loop(0, count // 8, step, (zero, zero, zero), unroll=16)
        return [jnp.sum(s, axis=0, keepdims=True) for s in sums]

    def edges():
        arrive(rim_copy, 0)
        for tile in range(own_blocks):
            at = slice(tile * BLOCK, (tile + 1) * BLOCK)
            index = neighbours[:, at]
            local = index & (BLOCK - 1)
            chunk = lax.shift_right_logical(index, 7)
            picked = []
            for c in range(4):
                pieces = [
                    (b, own_rows[c : c + 1, b * BLOCK : (b + 1) * BLOCK])
                    for b in range(own_blocks)
                ] + [(own_blocks + side, rim_in[0, side, c : c + 1, :]) for side in range(2)]
                picked.append(table_gather(pieces, local, chunk))
            ox, oy, oz = (own_rows[c : c + 1, at] - picked[c] for c in range(3))
            dist_sq = ox * ox + oy * oy + oz * oz + SMOOTH
            yield at, (ox, oy, oz), dist_sq, picked[3], local, chunk

    def send_terms(charge, dipole):
        width = listed * BLOCK
        for half in range(0, width, 2 * BLOCK):
            out = field(
                near_rows[:, half : half + 2 * BLOCK], own_cols, rows, charge, dipole
            )
            for c in range(3):
                terms[c : c + 1, half : half + 2 * BLOCK] = out[c]

    centre = lax.broadcasted_iota(jnp.int32, (basis, rows), 0).astype(F32) * SPACING

    def radial_net():
        half = groups // 2
        spans = [range(half), range(half, groups)]
        for q in range(groups):
            parts = []
            for j in range(pack):
                away = jnp.broadcast_to(geometry[0, q * pack + j : q * pack + j + 1, :], (basis, rows))
                away = away - centre
                parts.append(jnp.exp(-(away * away)))
            turned = jnp.concatenate(parts, axis=0).T
            wave[q * rows : (q + 1) * rows, :] = turned.astype(BF16)
        for layer in range(layers):
            for step in range(3):
                for part, span in enumerate(spans):
                    at = slice(span[0] * rows, (span[-1] + 1) * rows)
                    if step == 0:
                        source, weight = wave[at, :], wide_in[layer]
                    else:
                        source, weight = stage[layer, step - 1, at, :], wide_mid[layer, step - 1]
                    h = silu_of_half(jnp.dot(source, weight, preferred_element_type=F32)).astype(BF16)
                    if step < 2:
                        stage[layer, step, at, :] = h
                    else:
                        for i, q in enumerate(span):
                            third[layer, :, q] = h[i * rows : (i + 1) * rows].reshape(
                                strips, STRIP, channels
                            )

    def own_part(layer):
        for j in range(pack):
            edge_weight[j] = jnp.dot(
                third[layer].reshape(groups * rows, channels),
                wide_out[layer, j],
                preferred_element_type=F32,
            ).reshape(strips, groups, STRIP, channels)
            gather_part(layer, j, 0, rows)

    def rim_part(layer):
        for j in range(pack):
            gather_part(layer, j, rows, 2 * rim)

    def gather_part(layer, j, first, count):
        source = jnp.dot(
            hot[j, :, :, :, first : first + count].reshape(groups * rows, count),
            tables[layer, first : first + count],
            preferred_element_type=F32,
        )
        product = edge_weight[j] * source.reshape(strips, groups, STRIP, channels)
        total = jnp.sum(product, axis=1)
        if first or j:
            total = acc[...] + total
        acc[...] = total

    @pl.when(g == 0)
    def _():
        for at, _, dist_sq, _, _, _ in edges():
            geometry[0, :, at] = jnp.sqrt(dist_sq)
        radial_net()

    @pl.when(g == 1)
    def _():
        for at, offset, dist_sq, source_charge, _, _ in edges():
            w = lax.rsqrt(dist_sq)
            w2 = w * w
            w3 = w2 * w
            s = source_charge * w3
            for c in range(3):
                geometry[c, :, at] = offset[c]
                extra = jnp.sum(offset[c] * s, axis=0, keepdims=True)
                pairs[c : c + 1, at] = extra
            geometry[3, :, at] = w3
            geometry[4, :, at] = 3.0 * (w3 * w2)

    pltpu.make_async_copy(everyone, everyone, all_recv).wait()
    for l in range(listed):
        tile = everyone[blocks[l]]
        near_rows[:, l * BLOCK : (l + 1) * BLOCK] = tile
        near_cols[l * BLOCK : (l + 1) * BLOCK, :] = jnp.concatenate(
            [tile, jnp.zeros_like(tile)], axis=0
        ).T

    out = field(own, near_cols, listed * BLOCK, lambda at, source: source[:, 3:4], False)
    for c in range(3):
        outside[c : c + 1, :] = out[c]

    @pl.when(g == 0)
    def _():
        for number in late[3:]:
            load(number).wait()
        fx, fy, fz = out
        strength = jnp.sqrt(1.0 + fx * fx + fy * fy + fz * fz)
        site_result[2:3, :] = strength
        strength_col = jnp.broadcast_to(strength, (8, rows)).T[:, 0:1]
        hidden_ref[...] = (features[...].astype(F32) + strength_col * field_gain[...]).astype(BF16)

        def lift(layer):
            lifted = jnp.dot(
                hidden_ref[...], node_in[layer], preferred_element_type=F32
            ).astype(BF16)
            picked = jnp.dot(pick[...], lifted, preferred_element_type=F32).astype(BF16)
            lent[layer] = picked.reshape(2, rim, channels)
            start(lift_copy, layer)
            tables[layer, 0:rows] = lifted

        for layer in range(layers):
            lift(layer)
            own_part(layer)
            arrive(lift_copy, layer)
            rim_part(layer)
            message = (acc[...].reshape(rows, channels) * (1.0 / slots)).astype(BF16)
            update = silu_of_half(
                0.5 * jnp.dot(message, node_out[layer], preferred_element_type=F32)
            )
            hidden_ref[...] = (hidden_ref[...].astype(F32) + update).astype(BF16)

        across = (((1,), (1,)), ((), ()))
        extra_cols[:, 0:2] = lax.dot_general(
            hidden_ref[...], readout[...], across, preferred_element_type=F32
        )
        site_result[0:2, :] = lax.dot_general(
            readout[...], hidden_ref[...], across, preferred_element_type=F32
        )
        send_terms(lambda at, source: extra_cols[at, 0:1], False)
        for layer in range(layers):
            gone(lift_copy, layer)

    @pl.when(g == 1)
    def _():
        gain = polar[...]
        outside[...] = outside[...] + pairs[...]
        dipole = [gain * outside[c : c + 1, :] for c in range(3)]
        for sweep in range(SWEEPS):
            step = 1 + sweep
            fill_rims(step, jnp.concatenate(dipole + [jnp.zeros((1, rows), F32)], axis=0))
            start(rim_copy, step)
            arrive(rim_copy, step)
            fresh = [[], [], []]
            for tile in range(own_blocks):
                at = slice(tile * BLOCK, (tile + 1) * BLOCK)
                index = neighbours[:, at]
                local = index & (BLOCK - 1)
                chunk = lax.shift_right_logical(index, 7)
                d = []
                for c in range(3):
                    pieces = [
                        (b, dipole[c][:, b * BLOCK : (b + 1) * BLOCK]) for b in range(own_blocks)
                    ] + [
                        (own_blocks + side, rim_in[step, side, c : c + 1, :]) for side in range(2)
                    ]
                    d.append(table_gather(pieces, local, chunk))
                r = [geometry[c, :, at] for c in range(3)]
                w3 = geometry[3, :, at]
                s = (r[0] * d[0] + r[1] * d[1] + r[2] * d[2]) * geometry[4, :, at]
                for c in range(3):
                    total = jnp.sum(r[c] * s - d[c] * w3, axis=0, keepdims=True)
                    fresh[c].append(gain[:, at] * (outside[c : c + 1, at] + total))
            dipole = [jnp.concatenate(f, axis=1) for f in fresh]
        for c in range(3):
            site_result[c : c + 1, :] = dipole[c]
        stacked = jnp.concatenate(dipole + [jnp.zeros((5, rows), F32)], axis=0)
        extra_cols[...] = stacked.T
        send_terms(None, True)
        for sweep in range(SWEEPS):
            gone(rim_copy, 1 + sweep)

    @pl.loop(0, n, unroll=4)
    def _(q):
        for b in range(own_blocks):
            total = jnp.zeros((3, BLOCK), F32)
            for l in range(listed):
                total = total + jnp.where(
                    blocks[l] == q * own_blocks + b, terms[:, l * BLOCK : (l + 1) * BLOCK], 0.0
                )
            term_out[q, b * 3 : (b + 1) * 3, :] = total

    def term_copy(i):
        return pltpu.make_async_remote_copy(
            src_ref=term_out.at[peer(i)],
            dst_ref=term_in.at[p],
            send_sem=term_send,
            recv_sem=term_recv,
            device_id=place(other, peer(i)),
            device_id_type=MESH,
        )

    @pl.loop(0, n, unroll=4)
    def _(i):
        term_copy(i).start()

    gone(rim_copy, 0)
    pltpu.make_async_copy(everyone, everyone, all_send).wait()
    pltpu.make_async_copy(term_in, term_in, term_recv).wait()

    total = jnp.sum(term_in[...], axis=0)
    for b in range(own_blocks):
        response[:, b * BLOCK : (b + 1) * BLOCK] = total[b * 3 : (b + 1) * 3, :]
    pltpu.make_async_copy(term_in, term_in, term_send).wait()


def local(n_dom, n_sub, *args):
    (
        positions,
        charges,
        polar,
        features,
        neighbours,
        send_rows,
        blocks,
        radial_in,
        radial_mid,
        radial_out,
        node_in,
        node_out,
        field_gain,
        readout,
    ) = args
    n = n_dom * n_sub
    rows = positions.shape[1]
    own_blocks = rows // BLOCK
    slots = neighbours.shape[1]
    listed = blocks.shape[0]
    layers, basis, radial = radial_in.shape
    channels = features.shape[1]
    rim = send_rows.shape[1]
    pack = channels // radial
    dma = pltpu.SemaphoreType.DMA
    operands = (
        positions,
        charges.reshape(1, -1),
        polar.reshape(1, -1),
        features,
        neighbours.T,
        send_rows,
        blocks,
        radial_in,
        radial_mid,
        radial_out,
        node_in,
        node_out,
        field_gain.reshape(1, -1),
        readout.T,
    )
    spaces = [pltpu.VMEM] * INPUTS
    spaces[6] = pltpu.SMEM
    both = pl.pallas_call(
        functools.partial(kernel, n_dom, n_sub),
        out_shape=jax.ShapeDtypeStruct((2, 3, rows), F32),
        in_specs=[pl.BlockSpec(memory_space=pl.ANY)] * INPUTS,
        out_specs=pl.BlockSpec(memory_space=pltpu.VMEM),
        scratch_shapes=[space(a.shape, a.dtype) for space, a in zip(spaces, operands)]
        + [
            dma((INPUTS,)),
            pltpu.VMEM((own_blocks, 4, BLOCK), F32),
            pltpu.VMEM((n * own_blocks, 4, BLOCK), F32),
            pltpu.VMEM((4, listed * BLOCK), F32),
            pltpu.VMEM((listed * BLOCK, 8), F32),
            pltpu.VMEM((8, rows), F32),
            pltpu.VMEM((rows, 8), F32),
            pltpu.VMEM((rows, 8), F32),
            pltpu.VMEM((1 + SWEEPS, 2, 4, rim), F32),
            pltpu.VMEM((1 + SWEEPS, 2, 4, rim), F32),
            pltpu.VMEM((5, slots, rows), F32),
            pltpu.VMEM((pack, rows // STRIP, slots // pack, STRIP, rows + 2 * rim), BF16),
            pltpu.VMEM((2 * rim, rows), BF16),
            pltpu.VMEM((slots // pack * rows, pack * basis), BF16),
            pltpu.VMEM((layers, 2, slots // pack * rows, channels), BF16),
            pltpu.VMEM((layers, rows // STRIP, slots // pack, STRIP, channels), BF16),
            pltpu.VMEM((pack, rows // STRIP, slots // pack, STRIP, channels), F32),
            pltpu.VMEM((layers, pack * basis, channels), BF16),
            pltpu.VMEM((layers, 2, channels, channels), BF16),
            pltpu.VMEM((layers, pack, channels, channels), BF16),
            pltpu.VMEM((layers, rows + 2 * rim, channels), BF16),
            pltpu.VMEM((layers, 2, rim, channels), BF16),
            pltpu.VMEM((rows, channels), BF16),
            pltpu.VMEM((rows // STRIP, STRIP, channels), F32),
            pltpu.VMEM((3, rows), F32),
            pltpu.VMEM((3, rows), F32),
            pltpu.VMEM((3, listed * BLOCK), F32),
            pltpu.VMEM((n, own_blocks * 3, BLOCK), F32),
            pltpu.VMEM((n, own_blocks * 3, BLOCK), F32),
            dma(()),
            dma(()),
            dma((1 + SWEEPS, 2)),
            dma((1 + SWEEPS, 2)),
            dma((layers, 2)),
            dma((layers, 2)),
            dma(()),
            dma(()),
        ],
        compiler_params=pltpu.CompilerParams(
            collective_id=0, has_side_effects=True, vmem_limit_bytes=40 * 2**20
        ),
    )(*(pltpu.with_memory_space_constraint(a, pltpu.HBM) for a in operands))
    return both[0], both[1]


def solution(mesh):
    sites = ("grp", "dom", "sub")
    in_specs = (
        P(None, sites),
        P(sites),
        P(sites),
        P(sites, None),
        P(sites, None),
        P(None, sites),
        P(sites),
    ) + (P(),) * 7
    out_specs = (P(None, sites), P(None, sites))
    body = functools.partial(local, mesh.shape["dom"], mesh.shape["sub"])
    return jax.shard_map(body, mesh=mesh, in_specs=in_specs, out_specs=out_specs, check_vma=False)
```

```python
import functools

import jax
import jax.numpy as jnp
from jax import lax
from jax.experimental import pallas as pl
from jax.experimental.pallas import tpu as pltpu
from jax.sharding import PartitionSpec as P

SWEEPS = 4
BLOCK = 128
SMOOTH = 1.0
SPACING = 0.75
MESH = pl.DeviceIdType.MESH
INPUTS = 14
STRIP = 16
F32 = jnp.float32
BF16 = jnp.bfloat16


def silu_of_half(half):
    return half + half * jnp.tanh(half)


def lane_pick(rows, index):
    shape = index.shape
    return jnp.take_along_axis(
        jnp.broadcast_to(rows, shape), index, axis=1, mode="promise_in_bounds"
    )


def table_gather(pieces, local, chunk, total=None):
    if total is None:
        total = jnp.zeros(local.shape, F32)
    for number, rows in pieces:
        total = jnp.where(chunk == number, lane_pick(rows, local), total)
    return total


def kernel(
    n_dom,
    n_sub,
    *refs,
):
    sources = refs[:INPUTS]
    (
    both,
    positions,
    charges,
    polar,
    features,
    neighbours,
    send_rows,
    blocks,
    radial_in,
    radial_mid,
    radial_out,
    node_in,
    node_out,
    field_gain,
    readout,
    in_sem,
    packet,
    everyone,
    near_rows,
    near_cols,
    own_rows,
    own_cols,
    extra_cols,
    rim_out,
    rim_in,
    geometry,
    hot,
    pick,
    wave,
    stage,
    third,
    edge_weight,
    wide_in,
    wide_mid,
    wide_out,
    tables,
    lent,
    lent_cols,
    reach,
    hidden_ref,
    acc,
    outside,
    pairs,
    terms,
    term_out,
    term_in,
    all_send,
    all_recv,
    rim_send,
    rim_recv,
    lift_send,
    lift_recv,
    term_send,
    term_recv,
    ) = refs[INPUTS:]
    g = lax.axis_index("grp")
    p = lax.axis_index("dom") * n_sub + lax.axis_index("sub")
    site_result, response = both.at[0], both.at[1]
    n = n_dom * n_sub
    rows = positions.shape[1]
    own_blocks = rows // BLOCK
    slots = neighbours.shape[0]
    listed = blocks.shape[0]
    layers, basis, radial = radial_in.shape
    channels = features.shape[1]
    rim = send_rows.shape[1]
    pack = channels // radial
    groups = slots // pack
    strips = rows // STRIP
    other = 1 - g
    held = (
        positions,
        charges,
        polar,
        features,
        neighbours,
        send_rows,
        blocks,
        radial_in,
        radial_mid,
        radial_out,
        node_in,
        node_out,
        field_gain,
        readout,
    )
    early = (0, 1, 2, 4, 5, 6)
    late = (7, 8, 9, 3, 10, 11, 12, 13)
    spread_needs = 4

    def load(number):
        target = held[number]
        if number == 3:
            target = target.at[pl.ds(0, rows)]
        return pltpu.make_async_copy(sources[number], target, in_sem.at[number])

    for number in early:
        load(number).start()

    def place(group, q):
        return (group, lax.div(q, n_sub), lax.rem(q, n_sub))

    def peer(i):
        return lax.rem(p + i, n)

    barrier = pltpu.get_barrier_semaphore()

    @pl.loop(0, n)
    def _(i):
        pl.semaphore_signal(barrier, inc=1, device_id=place(other, peer(i)), device_id_type=MESH)

    @pl.when(p > 0)
    def _():
        pl.semaphore_signal(barrier, inc=1, device_id=place(g, p - 1), device_id_type=MESH)

    @pl.when(p < n - 1)
    def _():
        pl.semaphore_signal(barrier, inc=1, device_id=place(g, p + 1), device_id_type=MESH)

    @pl.when(g == 0)
    def _():
        for number in late:
            load(number).start()

    own_rows[...] = jnp.zeros_like(own_rows)
    for number in early:
        load(number).wait()
    own_rows[0:3, :] = positions[...]
    own_rows[3:4, :] = charges[...]
    own = own_rows[...]
    for b in range(own_blocks):
        packet[b] = own[0:4, b * BLOCK : (b + 1) * BLOCK]

    def fill_rims(step, values):
        for side in range(2):
            index = jnp.broadcast_to(send_rows[side : side + 1, :], (4, rim))
            rim_out[step, side] = table_gather(
                [(c, values[:, c * BLOCK : (c + 1) * BLOCK]) for c in range(own_blocks)],
                index & (BLOCK - 1),
                lax.shift_right_logical(index, 7),
            )

    def side_copy(src, dst, send, recv, step, side, q):
        return pltpu.make_async_remote_copy(
            src_ref=src,
            dst_ref=dst,
            send_sem=send.at[step, side],
            recv_sem=recv.at[step, side],
            device_id=place(g, q),
            device_id_type=MESH,
        )

    def rim_copy(step, side, q):
        return side_copy(
            rim_out.at[step, side], rim_in.at[step, side], rim_send, rim_recv, step, side, q
        )

    def lift_copy(layer, side, q):
        target = tables.at[layer] if layer else features
        return side_copy(
            lent.at[layer, side],
            target.at[pl.ds(rows + side * rim, rim)],
            lift_send,
            lift_recv,
            layer,
            side,
            q,
        )

    def start(copy, step):
        @pl.when(p < n - 1)
        def _():
            copy(step, 0, p + 1).start()

        @pl.when(p > 0)
        def _():
            copy(step, 1, p - 1).start()

    def arrive(copy, step):
        @pl.when(p > 0)
        def _():
            copy(step, 0, p - 1).wait_recv()

        @pl.when(p < n - 1)
        def _():
            copy(step, 1, p + 1).wait_recv()

    def gone(copy, step):
        @pl.when(p < n - 1)
        def _():
            copy(step, 0, p + 1).wait_send()

        @pl.when(p > 0)
        def _():
            copy(step, 1, p - 1).wait_send()

    def prepare():
        width = rows + 2 * rim
        lane = lax.broadcasted_iota(jnp.int32, (rows, width), 1).astype(jnp.int16)
        listing = jnp.concatenate(
            [neighbours[...].astype(F32), jnp.zeros((BLOCK - slots, rows), F32)], axis=0
        ).T.astype(jnp.int32)
        one, none = jnp.ones((rows, width), BF16), jnp.zeros((rows, width), BF16)
        for k in range(slots):
            entry = jnp.broadcast_to(listing[:, k : k + 1], (rows, BLOCK)).astype(jnp.int16)
            entry = jnp.concatenate([entry] * (width // BLOCK), axis=1)
            mark = jnp.where(entry == lane, one, none)
            hot[k % pack, :, k // pack] = mark.reshape(strips, STRIP, width)
        lists = jnp.concatenate(
            [send_rows[...].astype(F32), jnp.zeros((6, rim), F32)], axis=0
        ).T.astype(jnp.int32)
        site = lax.broadcasted_iota(jnp.int32, (rim, rows), 1)
        for side in range(2):
            pick[side * rim : (side + 1) * rim, :] = jnp.where(
                lists[:, side : side + 1] == site, 1.0, 0.0
            ).astype(BF16)

    def spread():
        for number in late[:spread_needs]:
            load(number).wait()
        spread_r = (
            lax.broadcasted_iota(jnp.int32, (channels, radial), 0) % radial
            == lax.broadcasted_iota(jnp.int32, (channels, radial), 1)
        ).astype(F32).astype(BF16)
        spread_c = (
            lax.broadcasted_iota(jnp.int32, (radial, channels), 1) % radial
            == lax.broadcasted_iota(jnp.int32, (radial, channels), 0)
        ).astype(F32).astype(BF16)
        same_in = (
            lax.broadcasted_iota(jnp.int32, (pack * basis, channels), 0) // basis
            == lax.broadcasted_iota(jnp.int32, (pack * basis, channels), 1) // radial
        )
        same_mid = (
            lax.broadcasted_iota(jnp.int32, (channels, channels), 0) // radial
            == lax.broadcasted_iota(jnp.int32, (channels, channels), 1) // radial
        )
        for layer in range(layers):
            flat = jnp.dot(radial_in[layer], spread_c, preferred_element_type=F32)
            wide_in[layer] = jnp.where(
                same_in, jnp.concatenate([0.5 * flat] * pack, axis=0), 0.0
            ).astype(BF16)
            for m in range(2):
                flat = jnp.dot(
                    jnp.dot(spread_r, radial_mid[layer, m], preferred_element_type=F32).astype(
                        BF16
                    ),
                    spread_c,
                    preferred_element_type=F32,
                )
                wide_mid[layer, m] = jnp.where(same_mid, 0.5 * flat, 0.0).astype(BF16)
            for j in range(pack):
                wide_out[layer, j] = jnp.zeros((channels, channels), BF16)
                wide_out[layer, j, j * radial : (j + 1) * radial, :] = radial_out[layer]

    def lend(layer, values):
        picked = jnp.dot(pick[...], values, preferred_element_type=F32).astype(BF16)
        lent[layer] = picked.reshape(2, rim, channels)

    fill_rims(0, own[0:4])

    @pl.when(g == 0)
    def _():
        spot = lax.broadcasted_iota(jnp.int32, (1, rim), 1)
        names = jnp.zeros((1, rim), F32)
        for l in range(listed):
            names = jnp.where(spot == l, blocks[l].astype(F32), names)
        for side in range(2):
            rim_out[0, side, 3:4, :] = names

    @pl.when(p == 0)
    def _():
        for step in range(1 + SWEEPS):
            rim_in[step, 0] = jnp.zeros((4, rim), F32)
        features[rows : rows + rim] = jnp.zeros((rim, channels), BF16)
        for layer in range(1, layers):
            tables[layer, rows : rows + rim] = jnp.zeros((rim, channels), BF16)

    @pl.when(p == n - 1)
    def _():
        for step in range(1 + SWEEPS):
            rim_in[step, 1] = jnp.zeros((4, rim), F32)
        features[rows + rim :] = jnp.zeros((rim, channels), BF16)
        for layer in range(1, layers):
            tables[layer, rows + rim :] = jnp.zeros((rim, channels), BF16)

    @pl.when(g == 0)
    def _():
        prepare()

    pl.semaphore_wait(barrier, n + (p > 0).astype(jnp.int32) + (p < n - 1).astype(jnp.int32))

    def packet_copy(i):
        return pltpu.make_async_remote_copy(
            src_ref=packet,
            dst_ref=everyone.at[pl.ds(p * own_blocks, own_blocks)],
            send_sem=all_send,
            recv_sem=all_recv,
            device_id=place(other, peer(i)),
            device_id_type=MESH,
        )

    start(rim_copy, 0)

    @pl.loop(0, n, unroll=4)
    def _(i):
        packet_copy(i).start()

    @pl.when(g == 0)
    def _():
        spread()
        lend(0, features[0:rows])

    own_cols[...] = own.T

    def field(targets, source_cols, count):
        x, y, z = (targets[c : c + 1, :] for c in range(3))

        def step(i, sums):
            source = source_cols[pl.ds(pl.multiple_of(i * 8, 8), 8), :]
            rx = x - source[:, 0:1]
            ry = y - source[:, 1:2]
            rz = z - source[:, 2:3]
            w = lax.rsqrt(rx * rx + ry * ry + rz * rz + SMOOTH)
            s = source[:, 3:4] * (w * w * w)
            return (sums[0] + rx * s, sums[1] + ry * s, sums[2] + rz * s)

        zero = jnp.zeros((8, targets.shape[1]), F32)
        sums = lax.fori_loop(0, count // 8, step, (zero, zero, zero), unroll=True)
        return [jnp.sum(s, axis=0, keepdims=True) for s in sums]

    def term_geometry(dipole):
        x, y, z = (near_rows[c : c + 1, :] for c in range(3))

        @pl.loop(0, rows // 8, unroll=8)
        def _(i):
            at = pl.ds(pl.multiple_of(i * 8, 8), 8)
            source = own_cols[at, :]
            r = (x - source[:, 0:1], y - source[:, 1:2], z - source[:, 2:3])
            w = lax.rsqrt(r[0] * r[0] + r[1] * r[1] + r[2] * r[2] + SMOOTH)
            w2 = w * w
            w3 = w2 * w
            for c in range(3):
                reach[c, at, :] = r[c] if dipole else r[c] * w3
            if dipole:
                reach[3, at, :] = w3
                reach[4, at, :] = 3.0 * (w3 * w2)

    def send_terms(dipole):
        def step(i, sums):
            at = pl.ds(pl.multiple_of(i * 8, 8), 8)
            d = extra_cols[at, :]
            r = [reach[c, at, :] for c in range(3)]
            if not dipole:
                return tuple(sums[c] + r[c] * d[:, 0:1] for c in range(3))
            w3 = reach[3, at, :]
            d = [d[:, c : c + 1] for c in range(3)]
            s = (r[0] * d[0] + r[1] * d[1] + r[2] * d[2]) * reach[4, at, :]
            return tuple(sums[c] + (r[c] * s - d[c] * w3) for c in range(3))

        zero = jnp.zeros((8, listed * BLOCK), F32)
        sums = lax.fori_loop(0, rows // 8, step, (zero, zero, zero), unroll=True)
        for c in range(3):
            terms[c : c + 1, :] = jnp.sum(sums[c], axis=0, keepdims=True)

    def edges():
        for tile in range(own_blocks):
            at = slice(tile * BLOCK, (tile + 1) * BLOCK)
            index = neighbours[:, at]
            local = index & (BLOCK - 1)
            chunk = lax.shift_right_logical(index, 7)
            picked = []
            for c in range(4):
                pieces = [
                    (b, own_rows[c : c + 1, b * BLOCK : (b + 1) * BLOCK])
                    for b in range(own_blocks)
                ] + [(own_blocks + side, rim_in[0, side, c : c + 1, :]) for side in range(2)]
                picked.append(table_gather(pieces, local, chunk))
            ox, oy, oz = (own_rows[c : c + 1, at] - picked[c] for c in range(3))
            dist_sq = ox * ox + oy * oy + oz * oz + SMOOTH
            yield at, (ox, oy, oz), dist_sq, picked[3], local, chunk

    centre = lax.broadcasted_iota(jnp.int32, (basis, rows), 0).astype(F32) * SPACING

    def waves():
        for q in range(groups):
            parts = []
            for j in range(pack):
                away = jnp.broadcast_to(geometry[0, q * pack + j : q * pack + j + 1, :], (basis, rows))
                away = away - centre
                parts.append(jnp.exp(-(away * away)))
            turned = jnp.concatenate(parts, axis=0).T
            wave[q * rows : (q + 1) * rows, :] = turned.astype(BF16)

    def radial_net(layer):
        half = groups // 2
        spans = [range(half), range(half, groups)]
        for step in range(3):
            for part, span in enumerate(spans):
                at = slice(span[0] * rows, (span[-1] + 1) * rows)
                if step == 0:
                    source, weight = wave[at, :], wide_in[layer]
                else:
                    source, weight = stage[step - 1, at, :], wide_mid[layer, step - 1]
                h = silu_of_half(jnp.dot(source, weight, preferred_element_type=F32)).astype(BF16)
                if step < 2:
                    stage[step, at, :] = h
                else:
                    for i, q in enumerate(span):
                        third[layer, :, q] = h[i * rows : (i + 1) * rows].reshape(
                            strips, STRIP, channels
                        )

    def own_part(layer, beside):
        for j in range(pack):
            beside(j)
            edge_weight[j] = jnp.dot(
                third[layer].reshape(groups * rows, channels),
                wide_out[layer, j],
                preferred_element_type=F32,
            ).reshape(strips, groups, STRIP, channels)
            gather_part(layer, j, 0, rows)

    def rim_part(layer):
        for j in range(pack):
            gather_part(layer, j, rows, 2 * rim)

    def gather_part(layer, j, first, count):
        source = jnp.dot(
            hot[j, :, :, :, first : first + count].reshape(groups * rows, count),
            tables[layer, first : first + count],
            preferred_element_type=F32,
        )
        product = edge_weight[j] * source.reshape(strips, groups, STRIP, channels)
        total = jnp.sum(product, axis=1)
        if first or j:
            total = acc[...] + total
        acc[...] = total

    @pl.when(g == 0)
    def _():
        arrive(rim_copy, 0)
        start(lift_copy, 0)
        for at, _, dist_sq, _, _, _ in edges():
            geometry[0, :, at] = jnp.sqrt(dist_sq)
        waves()
        radial_net(0)

    @pl.when(g == 1)
    def _():
        arrive(rim_copy, 0)
        for at, offset, dist_sq, source_charge, _, _ in edges():
            w = lax.rsqrt(dist_sq)
            w2 = w * w
            w3 = w2 * w
            s = source_charge * w3
            for c in range(3):
                geometry[c, :, at] = offset[c]
                extra = jnp.sum(offset[c] * s, axis=0, keepdims=True)
                pairs[c : c + 1, at] = extra
            geometry[3, :, at] = w3
            geometry[4, :, at] = 3.0 * (w3 * w2)

    pltpu.make_async_copy(everyone, everyone, all_recv).wait()
    for l in range(listed):
        tile = everyone[blocks[l]]
        near_rows[:, l * BLOCK : (l + 1) * BLOCK] = tile
        near_cols[l * BLOCK : (l + 1) * BLOCK, :] = jnp.concatenate(
            [tile, jnp.zeros_like(tile)], axis=0
        ).T

    def lent_near():
        names = [
            [jnp.broadcast_to(rim_in[0, side, 3:4, l : l + 1], (4, BLOCK)) for l in range(listed)]
            for side in range(2)
        ]

        def step(b, found):
            tile = everyone[b]
            return tuple(
                tuple(
                    jnp.where(names[side][l] == b.astype(F32), tile, found[side][l])
                    for l in range(listed)
                )
                for side in range(2)
            )

        blank = jnp.zeros((4, BLOCK), F32)
        found = lax.fori_loop(
            0, n * own_blocks, step, ((blank,) * listed,) * 2, unroll=max(8, min(32, n * own_blocks))
        )
        for side in range(2):
            for l in range(listed):
                lent_cols[side, l * BLOCK : (l + 1) * BLOCK, :] = jnp.concatenate(
                    [found[side][l], blank], axis=0
                ).T

    @pl.when(g == 0)
    def _():
        for number in late[spread_needs:]:
            load(number).wait()

        def strength_of(fields):
            fx, fy, fz = fields
            return jnp.sqrt(1.0 + fx * fx + fy * fy + fz * fz)

        def embed(strength, at):
            column = jnp.broadcast_to(strength, (8, strength.shape[1])).T[:, 0:1]
            return (features[at].astype(F32) + column * field_gain[...]).astype(BF16)

        def lent_field(side):
            return field(rim_in[0, side], lent_cols.at[side], listed * BLOCK)

        strength = strength_of(field(own, near_cols, listed * BLOCK))
        site_result[2:3, :] = strength
        hidden_ref[...] = embed(strength, slice(0, rows))
        tables[0, 0:rows] = jnp.dot(
            hidden_ref[...], node_in[0], preferred_element_type=F32
        ).astype(BF16)
        fields = []

        def lent_lift(j):
            if j == 0:
                lent_near()
            if j < 2:
                fields.append(lent_field(j))
            if j == pack - 1:
                arrive(lift_copy, 0)
                ends = (p > 0, p < n - 1)
                for side in range(2):
                    at = slice(rows + side * rim, rows + (side + 1) * rim)
                    hidden = embed(strength_of(fields[side]), at)
                    lifted = jnp.dot(hidden, node_in[0], preferred_element_type=F32)
                    tables[0, at] = jnp.where(ends[side], lifted, 0.0).astype(BF16)

        def lift(layer):
            lifted = jnp.dot(
                hidden_ref[...], node_in[layer], preferred_element_type=F32
            ).astype(BF16)
            lend(layer, lifted)
            start(lift_copy, layer)
            tables[layer, 0:rows] = lifted

        for layer in range(layers):
            if layer:
                lift(layer)
                radial_net(layer)
            own_part(layer, (lambda j: None) if layer else lent_lift)
            if layer == layers - 1:
                term_geometry(False)
            if layer:
                arrive(lift_copy, layer)
            rim_part(layer)
            message = (acc[...].reshape(rows, channels) * (1.0 / slots)).astype(BF16)
            update = silu_of_half(
                0.5 * jnp.dot(message, node_out[layer], preferred_element_type=F32)
            )
            hidden_ref[...] = (hidden_ref[...].astype(F32) + update).astype(BF16)

        across = (((1,), (1,)), ((), ()))
        extra_cols[:, 0:2] = lax.dot_general(
            hidden_ref[...], readout[...], across, preferred_element_type=F32
        )
        site_result[0:2, :] = lax.dot_general(
            readout[...], hidden_ref[...], across, preferred_element_type=F32
        )
        send_terms(False)
        for layer in range(layers):
            gone(lift_copy, layer)

    @pl.when(g == 1)
    def _():
        out = field(own, near_cols, listed * BLOCK)
        for c in range(3):
            outside[c : c + 1, :] = out[c]
        gain = polar[...]
        outside[...] = outside[...] + pairs[...]
        dipole = [gain * outside[c : c + 1, :] for c in range(3)]
        for sweep in range(SWEEPS):
            step = 1 + sweep
            fill_rims(step, jnp.concatenate(dipole + [jnp.zeros((1, rows), F32)], axis=0))
            start(rim_copy, step)
            near_part = []
            for tile in range(own_blocks):
                index = neighbours[:, tile * BLOCK : (tile + 1) * BLOCK]
                local = index & (BLOCK - 1)
                chunk = lax.shift_right_logical(index, 7)
                near_part.append([
                    table_gather(
                        [(b, dipole[c][:, b * BLOCK : (b + 1) * BLOCK]) for b in range(own_blocks)],
                        local,
                        chunk,
                    )
                    for c in range(3)
                ])
            if sweep == 0:
                term_geometry(True)
            arrive(rim_copy, step)
            fresh = [[], [], []]
            for tile in range(own_blocks):
                at = slice(tile * BLOCK, (tile + 1) * BLOCK)
                index = neighbours[:, at]
                local = index & (BLOCK - 1)
                chunk = lax.shift_right_logical(index, 7)
                d = [
                    table_gather(
                        [(own_blocks + side, rim_in[step, side, c : c + 1, :]) for side in range(2)],
                        local,
                        chunk,
                        near_part[tile][c],
                    )
                    for c in range(3)
                ]
                r = [geometry[c, :, at] for c in range(3)]
                w3 = geometry[3, :, at]
                s = (r[0] * d[0] + r[1] * d[1] + r[2] * d[2]) * geometry[4, :, at]
                for c in range(3):
                    total = jnp.sum(r[c] * s - d[c] * w3, axis=0, keepdims=True)
                    fresh[c].append(gain[:, at] * (outside[c : c + 1, at] + total))
            dipole = [jnp.concatenate(f, axis=1) for f in fresh]
        for c in range(3):
            site_result[c : c + 1, :] = dipole[c]
        stacked = jnp.concatenate(dipole + [jnp.zeros((5, rows), F32)], axis=0)
        extra_cols[...] = stacked.T
        send_terms(True)
        for sweep in range(SWEEPS):
            gone(rim_copy, 1 + sweep)

    @pl.loop(0, n, unroll=4)
    def _(q):
        for b in range(own_blocks):
            total = jnp.zeros((3, BLOCK), F32)
            for l in range(listed):
                total = total + jnp.where(
                    blocks[l] == q * own_blocks + b, terms[:, l * BLOCK : (l + 1) * BLOCK], 0.0
                )
            term_out[q, b * 3 : (b + 1) * 3, :] = total

    def term_copy(i):
        return pltpu.make_async_remote_copy(
            src_ref=term_out.at[peer(i)],
            dst_ref=term_in.at[p],
            send_sem=term_send,
            recv_sem=term_recv,
            device_id=place(other, peer(i)),
            device_id_type=MESH,
        )

    @pl.loop(0, n, unroll=4)
    def _(i):
        term_copy(i).start()

    gone(rim_copy, 0)
    pltpu.make_async_copy(everyone, everyone, all_send).wait()
    pltpu.make_async_copy(term_in, term_in, term_recv).wait()

    total = jnp.sum(term_in[...], axis=0)
    for b in range(own_blocks):
        response[:, b * BLOCK : (b + 1) * BLOCK] = total[b * 3 : (b + 1) * 3, :]
    pltpu.make_async_copy(term_in, term_in, term_send).wait()


def local(n_dom, n_sub, *args):
    (
        positions,
        charges,
        polar,
        features,
        neighbours,
        send_rows,
        blocks,
        radial_in,
        radial_mid,
        radial_out,
        node_in,
        node_out,
        field_gain,
        readout,
    ) = args
    n = n_dom * n_sub
    rows = positions.shape[1]
    own_blocks = rows // BLOCK
    slots = neighbours.shape[1]
    listed = blocks.shape[0]
    layers, basis, radial = radial_in.shape
    channels = features.shape[1]
    rim = send_rows.shape[1]
    pack = channels // radial
    dma = pltpu.SemaphoreType.DMA
    operands = (
        positions,
        charges.reshape(1, -1),
        polar.reshape(1, -1),
        features,
        neighbours.T,
        send_rows,
        blocks,
        radial_in,
        radial_mid,
        radial_out,
        node_in,
        node_out,
        field_gain.reshape(1, -1),
        readout.T,
    )
    spaces = [pltpu.VMEM] * INPUTS
    spaces[6] = pltpu.SMEM
    shapes = [a.shape for a in operands]
    shapes[3] = (rows + 2 * rim, channels)
    both = pl.pallas_call(
        functools.partial(kernel, n_dom, n_sub),
        out_shape=jax.ShapeDtypeStruct((2, 3, rows), F32),
        in_specs=[pl.BlockSpec(memory_space=pl.ANY)] * INPUTS,
        out_specs=pl.BlockSpec(memory_space=pltpu.VMEM),
        scratch_shapes=[space(shape, a.dtype) for space, shape, a in zip(spaces, shapes, operands)]
        + [
            dma((INPUTS,)),
            pltpu.VMEM((own_blocks, 4, BLOCK), F32),
            pltpu.VMEM((n * own_blocks, 4, BLOCK), F32),
            pltpu.VMEM((4, listed * BLOCK), F32),
            pltpu.VMEM((listed * BLOCK, 8), F32),
            pltpu.VMEM((8, rows), F32),
            pltpu.VMEM((rows, 8), F32),
            pltpu.VMEM((rows, 8), F32),
            pltpu.VMEM((1 + SWEEPS, 2, 4, rim), F32),
            pltpu.VMEM((1 + SWEEPS, 2, 4, rim), F32),
            pltpu.VMEM((5, slots, rows), F32),
            pltpu.VMEM((pack, rows // STRIP, slots // pack, STRIP, rows + 2 * rim), BF16),
            pltpu.VMEM((2 * rim, rows), BF16),
            pltpu.VMEM((slots // pack * rows, pack * basis), BF16),
            pltpu.VMEM((2, slots // pack * rows, channels), BF16),
            pltpu.VMEM((layers, rows // STRIP, slots // pack, STRIP, channels), BF16),
            pltpu.VMEM((pack, rows // STRIP, slots // pack, STRIP, channels), F32),
            pltpu.VMEM((layers, pack * basis, channels), BF16),
            pltpu.VMEM((layers, 2, channels, channels), BF16),
            pltpu.VMEM((layers, pack, channels, channels), BF16),
            pltpu.VMEM((layers, rows + 2 * rim, channels), BF16),
            pltpu.VMEM((layers, 2, rim, channels), BF16),
            pltpu.VMEM((2, listed * BLOCK, 8), F32),
            pltpu.VMEM((5, rows, listed * BLOCK), F32),
            pltpu.VMEM((rows, channels), BF16),
            pltpu.VMEM((rows // STRIP, STRIP, channels), F32),
            pltpu.VMEM((3, rows), F32),
            pltpu.VMEM((3, rows), F32),
            pltpu.VMEM((3, listed * BLOCK), F32),
            pltpu.VMEM((n, own_blocks * 3, BLOCK), F32),
            pltpu.VMEM((n, own_blocks * 3, BLOCK), F32),
            dma(()),
            dma(()),
            dma((1 + SWEEPS, 2)),
            dma((1 + SWEEPS, 2)),
            dma((layers, 2)),
            dma((layers, 2)),
            dma(()),
            dma(()),
        ],
        compiler_params=pltpu.CompilerParams(
            collective_id=0, has_side_effects=True, vmem_limit_bytes=40 * 2**20
        ),
    )(*(pltpu.with_memory_space_constraint(a, pltpu.HBM) for a in operands))
    return both[0], both[1]


def solution(mesh):
    sites = ("grp", "dom", "sub")
    in_specs = (
        P(None, sites),
        P(sites),
        P(sites),
        P(sites, None),
        P(sites, None),
        P(None, sites),
        P(sites),
    ) + (P(),) * 7
    out_specs = (P(None, sites), P(None, sites))
    body = functools.partial(local, mesh.shape["dom"], mesh.shape["sub"])
    return jax.shard_map(body, mesh=mesh, in_specs=in_specs, out_specs=out_specs, check_vma=False)
```

```python
import functools

import jax
import jax.numpy as jnp
from jax import lax
from jax.experimental import pallas as pl
from jax.experimental.pallas import tpu as pltpu
from jax.sharding import PartitionSpec as P

SWEEPS = 4
BLOCK = 128
SMOOTH = 1.0
SPACING = 0.75
MESH = pl.DeviceIdType.MESH
INPUTS = 14
STRIP = 16
EARLY = 2
F32 = jnp.float32
BF16 = jnp.bfloat16


def silu_of_half(half):
    return half + half * jnp.tanh(half)


def lane_pick(rows, index):
    shape = index.shape
    return jnp.take_along_axis(
        jnp.broadcast_to(rows, shape), index, axis=1, mode="promise_in_bounds"
    )


def table_gather(pieces, local, chunk, total=None):
    if total is None:
        total = jnp.zeros(local.shape, F32)
    for number, rows in pieces:
        total = jnp.where(chunk == number, lane_pick(rows, local), total)
    return total


def kernel(
    n_dom,
    n_sub,
    *refs,
):
    sources = refs[:INPUTS]
    (
    both,
    positions,
    charges,
    polar,
    features,
    neighbours,
    send_rows,
    blocks,
    radial_in,
    radial_mid,
    radial_out,
    node_in,
    node_out,
    field_gain,
    readout,
    in_sem,
    packet,
    everyone,
    near_rows,
    near_cols,
    own_rows,
    own_cols,
    extra_cols,
    rim_out,
    rim_in,
    geometry,
    hot,
    pick,
    wave,
    stage,
    third,
    edge_weight,
    wide_in,
    wide_mid,
    wide_out,
    tables,
    lent,
    lent_cols,
    reach,
    hidden_ref,
    acc,
    outside,
    pairs,
    terms,
    term_out,
    term_in,
    all_send,
    all_recv,
    rim_send,
    rim_recv,
    lift_send,
    lift_recv,
    term_send,
    term_recv,
    ) = refs[INPUTS:]
    g = lax.axis_index("grp")
    p = lax.axis_index("dom") * n_sub + lax.axis_index("sub")
    site_result, response = both.at[0], both.at[1]
    n = n_dom * n_sub
    rows = positions.shape[1]
    own_blocks = rows // BLOCK
    slots = neighbours.shape[0]
    listed = blocks.shape[0]
    layers, basis, radial = radial_in.shape
    channels = features.shape[1]
    rim = send_rows.shape[1]
    pack = channels // radial
    groups = slots // pack
    strips = rows // STRIP
    other = 1 - g
    held = (
        positions,
        charges,
        polar,
        features,
        neighbours,
        send_rows,
        blocks,
        radial_in,
        radial_mid,
        radial_out,
        node_in,
        node_out,
        field_gain,
        readout,
    )
    early = (0, 1, 2, 4, 5, 6)
    late = (7, 8, 9, 3, 10, 11, 12, 13)
    spread_needs = 4

    def load(number):
        target = held[number]
        if number == 3:
            target = target.at[pl.ds(0, rows)]
        return pltpu.make_async_copy(sources[number], target, in_sem.at[number])

    for number in early:
        load(number).start()

    def place(group, q):
        return (group, lax.div(q, n_sub), lax.rem(q, n_sub))

    def peer(i):
        if n % 4:
            return lax.rem(p + i, n)
        quarter = n // 4
        second = lax.div(2 * p, n)
        turn = lax.div(i, quarter)
        far = second * turn + (1 - second) * (3 - turn)
        return far * quarter + lax.rem(p + i, quarter)

    barrier = pltpu.get_barrier_semaphore()

    @pl.loop(0, n)
    def _(i):
        pl.semaphore_signal(barrier, inc=1, device_id=place(other, peer(i)), device_id_type=MESH)

    @pl.when(p > 0)
    def _():
        pl.semaphore_signal(barrier, inc=1, device_id=place(g, p - 1), device_id_type=MESH)

    @pl.when(p < n - 1)
    def _():
        pl.semaphore_signal(barrier, inc=1, device_id=place(g, p + 1), device_id_type=MESH)

    @pl.when(g == 0)
    def _():
        for number in late:
            load(number).start()

    own_rows[...] = jnp.zeros_like(own_rows)
    for number in early:
        load(number).wait()
    own_rows[0:3, :] = positions[...]
    own_rows[3:4, :] = charges[...]
    own = own_rows[...]
    for b in range(own_blocks):
        packet[b] = own[0:4, b * BLOCK : (b + 1) * BLOCK]

    def fill_rims(step, values):
        for side in range(2):
            index = jnp.broadcast_to(send_rows[side : side + 1, :], (4, rim))
            rim_out[step, side] = table_gather(
                [(c, values[:, c * BLOCK : (c + 1) * BLOCK]) for c in range(own_blocks)],
                index & (BLOCK - 1),
                lax.shift_right_logical(index, 7),
            )

    def side_copy(src, dst, send, recv, step, side, q):
        return pltpu.make_async_remote_copy(
            src_ref=src,
            dst_ref=dst,
            send_sem=send.at[step, side],
            recv_sem=recv.at[step, side],
            device_id=place(g, q),
            device_id_type=MESH,
        )

    def rim_copy(step, side, q):
        return side_copy(
            rim_out.at[step, side], rim_in.at[step, side], rim_send, rim_recv, step, side, q
        )

    def lift_copy(layer, side, q):
        target = tables.at[layer] if layer else features
        return side_copy(
            lent.at[layer, side],
            target.at[pl.ds(rows + side * rim, rim)],
            lift_send,
            lift_recv,
            layer,
            side,
            q,
        )

    def start(copy, step):
        @pl.when(p < n - 1)
        def _():
            copy(step, 0, p + 1).start()

        @pl.when(p > 0)
        def _():
            copy(step, 1, p - 1).start()

    def arrive(copy, step):
        @pl.when(p > 0)
        def _():
            copy(step, 0, p - 1).wait_recv()

        @pl.when(p < n - 1)
        def _():
            copy(step, 1, p + 1).wait_recv()

    def gone(copy, step):
        @pl.when(p < n - 1)
        def _():
            copy(step, 0, p + 1).wait_send()

        @pl.when(p > 0)
        def _():
            copy(step, 1, p - 1).wait_send()

    def prepare():
        width = rows + 2 * rim
        lane = lax.broadcasted_iota(jnp.int32, (rows, width), 1).astype(jnp.int16)
        listing = jnp.concatenate(
            [neighbours[...].astype(F32), jnp.zeros((BLOCK - slots, rows), F32)], axis=0
        ).T.astype(jnp.int32)
        one, none = jnp.ones((rows, width), BF16), jnp.zeros((rows, width), BF16)
        for k in range(slots):
            entry = jnp.broadcast_to(listing[:, k : k + 1], (rows, BLOCK)).astype(jnp.int16)
            entry = jnp.concatenate([entry] * (width // BLOCK), axis=1)
            mark = jnp.where(entry == lane, one, none)
            hot[k % pack, :, k // pack] = mark.reshape(strips, STRIP, width)
        lists = jnp.concatenate(
            [send_rows[...].astype(F32), jnp.zeros((6, rim), F32)], axis=0
        ).T.astype(jnp.int32)
        site = lax.broadcasted_iota(jnp.int32, (rim, rows), 1)
        for side in range(2):
            pick[side * rim : (side + 1) * rim, :] = jnp.where(
                lists[:, side : side + 1] == site, 1.0, 0.0
            ).astype(BF16)

    def spread():
        for number in late[:spread_needs]:
            load(number).wait()
        spread_r = (
            lax.broadcasted_iota(jnp.int32, (channels, radial), 0) % radial
            == lax.broadcasted_iota(jnp.int32, (channels, radial), 1)
        ).astype(F32).astype(BF16)
        spread_c = (
            lax.broadcasted_iota(jnp.int32, (radial, channels), 1) % radial
            == lax.broadcasted_iota(jnp.int32, (radial, channels), 0)
        ).astype(F32).astype(BF16)
        same_in = (
            lax.broadcasted_iota(jnp.int32, (pack * basis, channels), 0) // basis
            == lax.broadcasted_iota(jnp.int32, (pack * basis, channels), 1) // radial
        )
        same_mid = (
            lax.broadcasted_iota(jnp.int32, (channels, channels), 0) // radial
            == lax.broadcasted_iota(jnp.int32, (channels, channels), 1) // radial
        )
        for layer in range(layers):
            flat = jnp.dot(radial_in[layer], spread_c, preferred_element_type=F32)
            wide_in[layer] = jnp.where(
                same_in, jnp.concatenate([0.5 * flat] * pack, axis=0), 0.0
            ).astype(BF16)
            for m in range(2):
                flat = jnp.dot(
                    jnp.dot(spread_r, radial_mid[layer, m], preferred_element_type=F32).astype(
                        BF16
                    ),
                    spread_c,
                    preferred_element_type=F32,
                )
                wide_mid[layer, m] = jnp.where(same_mid, 0.5 * flat, 0.0).astype(BF16)
            for j in range(pack):
                wide_out[layer, j] = jnp.zeros((channels, channels), BF16)
                wide_out[layer, j, j * radial : (j + 1) * radial, :] = radial_out[layer]

    def lend(layer, values):
        picked = jnp.dot(pick[...], values, preferred_element_type=F32).astype(BF16)
        lent[layer] = picked.reshape(2, rim, channels)

    fill_rims(0, own[0:4])

    @pl.when(g == 0)
    def _():
        spot = lax.broadcasted_iota(jnp.int32, (1, rim), 1)
        names = jnp.zeros((1, rim), F32)
        for l in range(listed):
            names = jnp.where(spot == l, blocks[l].astype(F32), names)
        for side in range(2):
            rim_out[0, side, 3:4, :] = names

    @pl.when(p == 0)
    def _():
        for step in range(1 + SWEEPS):
            rim_in[step, 0] = jnp.zeros((4, rim), F32)
        features[rows : rows + rim] = jnp.zeros((rim, channels), BF16)
        for layer in range(1, layers):
            tables[layer, rows : rows + rim] = jnp.zeros((rim, channels), BF16)

    @pl.when(p == n - 1)
    def _():
        for step in range(1 + SWEEPS):
            rim_in[step, 1] = jnp.zeros((4, rim), F32)
        features[rows + rim :] = jnp.zeros((rim, channels), BF16)
        for layer in range(1, layers):
            tables[layer, rows + rim :] = jnp.zeros((rim, channels), BF16)

    @pl.when(g == 0)
    def _():
        prepare()

    pl.semaphore_wait(barrier, n + (p > 0).astype(jnp.int32) + (p < n - 1).astype(jnp.int32))

    def packet_copy(i):
        return pltpu.make_async_remote_copy(
            src_ref=packet,
            dst_ref=everyone.at[pl.ds(p * own_blocks, own_blocks)],
            send_sem=all_send,
            recv_sem=all_recv,
            device_id=place(other, peer(i)),
            device_id_type=MESH,
        )

    start(rim_copy, 0)

    @pl.loop(0, n, unroll=4)
    def _(i):
        packet_copy(i).start()

    @pl.when(g == 0)
    def _():
        spread()
        lend(0, features[0:rows])

    own_cols[...] = own.T

    def field(targets, source_cols, count):
        x, y, z = (targets[c : c + 1, :] for c in range(3))

        def step(i, sums):
            source = source_cols[pl.ds(pl.multiple_of(i * 8, 8), 8), :]
            rx = x - source[:, 0:1]
            ry = y - source[:, 1:2]
            rz = z - source[:, 2:3]
            w = lax.rsqrt(rx * rx + ry * ry + rz * rz + SMOOTH)
            s = source[:, 3:4] * (w * w * w)
            return (sums[0] + rx * s, sums[1] + ry * s, sums[2] + rz * s)

        zero = jnp.zeros((8, targets.shape[1]), F32)
        sums = lax.fori_loop(0, count // 8, step, (zero, zero, zero), unroll=True)
        return [jnp.sum(s, axis=0, keepdims=True) for s in sums]

    def term_geometry(dipole, part, parts):
        x, y, z = (near_rows[c : c + 1, :] for c in range(3))
        for i in range(part * rows // 8 // parts, (part + 1) * rows // 8 // parts):
            at = slice(i * 8, i * 8 + 8)
            source = own_cols[at, :]
            r = (x - source[:, 0:1], y - source[:, 1:2], z - source[:, 2:3])
            w = lax.rsqrt(r[0] * r[0] + r[1] * r[1] + r[2] * r[2] + SMOOTH)
            w2 = w * w
            w3 = w2 * w
            for c in range(3):
                reach[c, at, :] = r[c] if dipole else r[c] * w3
            if dipole:
                reach[3, at, :] = w3
                reach[4, at, :] = 3.0 * (w3 * w2)

    def send_terms(dipole):
        def step(i, sums):
            at = pl.ds(pl.multiple_of(i * 8, 8), 8)
            d = extra_cols[at, :]
            r = [reach[c, at, :] for c in range(3)]
            if not dipole:
                return tuple(sums[c] + r[c] * d[:, 0:1] for c in range(3))
            w3 = reach[3, at, :]
            d = [d[:, c : c + 1] for c in range(3)]
            s = (r[0] * d[0] + r[1] * d[1] + r[2] * d[2]) * reach[4, at, :]
            return tuple(sums[c] + (r[c] * s - d[c] * w3) for c in range(3))

        zero = jnp.zeros((8, listed * BLOCK), F32)
        sums = lax.fori_loop(0, rows // 8, step, (zero, zero, zero), unroll=True)
        for c in range(3):
            terms[c : c + 1, :] = jnp.sum(sums[c], axis=0, keepdims=True)

    def edges():
        for tile in range(own_blocks):
            at = slice(tile * BLOCK, (tile + 1) * BLOCK)
            index = neighbours[:, at]
            local = index & (BLOCK - 1)
            chunk = lax.shift_right_logical(index, 7)
            picked = []
            for c in range(4):
                pieces = [
                    (b, own_rows[c : c + 1, b * BLOCK : (b + 1) * BLOCK])
                    for b in range(own_blocks)
                ] + [(own_blocks + side, rim_in[0, side, c : c + 1, :]) for side in range(2)]
                picked.append(table_gather(pieces, local, chunk))
            ox, oy, oz = (own_rows[c : c + 1, at] - picked[c] for c in range(3))
            dist_sq = ox * ox + oy * oy + oz * oz + SMOOTH
            yield at, (ox, oy, oz), dist_sq, picked[3], local, chunk

    centre = lax.broadcasted_iota(jnp.int32, (basis, rows), 0).astype(F32) * SPACING

    def waves():
        for q in range(groups):
            parts = []
            for j in range(pack):
                away = jnp.broadcast_to(geometry[0, q * pack + j : q * pack + j + 1, :], (basis, rows))
                away = away - centre
                parts.append(jnp.exp(-(away * away)))
            turned = jnp.concatenate(parts, axis=0).T
            wave[q * rows : (q + 1) * rows, :] = turned.astype(BF16)

    def radial_net(layer):
        half = groups // 2
        spans = [range(half), range(half, groups)]
        for step in range(3):
            for part, span in enumerate(spans):
                at = slice(span[0] * rows, (span[-1] + 1) * rows)
                if step == 0:
                    source, weight = wave[at, :], wide_in[layer]
                else:
                    source, weight = stage[step - 1, at, :], wide_mid[layer, step - 1]
                h = silu_of_half(jnp.dot(source, weight, preferred_element_type=F32)).astype(BF16)
                if step < 2:
                    stage[step, at, :] = h
                else:
                    for i, q in enumerate(span):
                        third[layer, :, q] = h[i * rows : (i + 1) * rows].reshape(
                            strips, STRIP, channels
                        )

    def edge_part(layer, j):
        edge_weight[j] = jnp.dot(
            third[layer].reshape(groups * rows, channels),
            wide_out[layer, j],
            preferred_element_type=F32,
        ).reshape(strips, groups, STRIP, channels)

    def own_part(layer, beside):
        for j in range(pack):
            beside(j)
            if layer or j >= EARLY:
                edge_part(layer, j)
            gather_part(layer, j, 0, rows)

    def rim_part(layer):
        for j in range(pack):
            gather_part(layer, j, rows, 2 * rim)

    def gather_part(layer, j, first, count):
        source = jnp.dot(
            hot[j, :, :, :, first : first + count].reshape(groups * rows, count),
            tables[layer, first : first + count],
            preferred_element_type=F32,
        )
        product = edge_weight[j] * source.reshape(strips, groups, STRIP, channels)
        total = jnp.sum(product, axis=1)
        if first or j:
            total = acc[...] + total
        acc[...] = total

    @pl.when(g == 0)
    def _():
        arrive(rim_copy, 0)
        start(lift_copy, 0)
        for at, _, dist_sq, _, _, _ in edges():
            geometry[0, :, at] = jnp.sqrt(dist_sq)
        waves()
        radial_net(0)
        for j in range(EARLY):
            edge_part(0, j)

    @pl.when(g == 1)
    def _():
        arrive(rim_copy, 0)
        for at, offset, dist_sq, source_charge, _, _ in edges():
            w = lax.rsqrt(dist_sq)
            w2 = w * w
            w3 = w2 * w
            s = source_charge * w3
            for c in range(3):
                geometry[c, :, at] = offset[c]
                extra = jnp.sum(offset[c] * s, axis=0, keepdims=True)
                pairs[c : c + 1, at] = extra
            geometry[3, :, at] = w3
            geometry[4, :, at] = 3.0 * (w3 * w2)

    pltpu.make_async_copy(everyone, everyone, all_recv).wait()
    for l in range(listed):
        tile = everyone[blocks[l]]
        near_rows[:, l * BLOCK : (l + 1) * BLOCK] = tile
        near_cols[l * BLOCK : (l + 1) * BLOCK, :] = jnp.concatenate(
            [tile, jnp.zeros_like(tile)], axis=0
        ).T

    def lent_near():
        names = [
            [jnp.broadcast_to(rim_in[0, side, 3:4, l : l + 1], (4, BLOCK)) for l in range(listed)]
            for side in range(2)
        ]

        def step(b, found):
            tile = everyone[b]
            return tuple(
                tuple(
                    jnp.where(names[side][l] == b.astype(F32), tile, found[side][l])
                    for l in range(listed)
                )
                for side in range(2)
            )

        blank = jnp.zeros((4, BLOCK), F32)
        found = lax.fori_loop(
            0, n * own_blocks, step, ((blank,) * listed,) * 2, unroll=max(8, min(32, n * own_blocks))
        )
        for side in range(2):
            for l in range(listed):
                lent_cols[side, l * BLOCK : (l + 1) * BLOCK, :] = jnp.concatenate(
                    [found[side][l], blank], axis=0
                ).T

    @pl.when(g == 0)
    def _():
        for number in late[spread_needs:]:
            load(number).wait()

        def strength_of(fields):
            fx, fy, fz = fields
            return jnp.sqrt(1.0 + fx * fx + fy * fy + fz * fz)

        def column_of(strength):
            return jnp.broadcast_to(strength, (8, strength.shape[1])).T[:, 0:1]

        def embed(column, at):
            return (features[at].astype(F32) + column * field_gain[...]).astype(BF16)

        def lent_field(side):
            return field(rim_in[0, side], lent_cols.at[side], listed * BLOCK)

        strength = strength_of(field(own, near_cols, listed * BLOCK))
        site_result[2:3, :] = strength
        hidden_ref[...] = embed(column_of(strength), slice(0, rows))
        tables[0, 0:rows] = jnp.dot(
            hidden_ref[...], node_in[0], preferred_element_type=F32
        ).astype(BF16)
        fields, columns = [], []

        def lent_lift(j):
            if j == 0:
                lent_near()
            if j < 2:
                fields.append(lent_field(j))
            if j == 2:
                columns.extend(column_of(strength_of(part)) for part in fields)
            if j == pack - 1:
                arrive(lift_copy, 0)
                ends = (p > 0, p < n - 1)
                for side in range(2):
                    at = slice(rows + side * rim, rows + (side + 1) * rim)
                    hidden = embed(columns[side], at)
                    lifted = jnp.dot(hidden, node_in[0], preferred_element_type=F32)
                    tables[0, at] = jnp.where(ends[side], lifted, 0.0).astype(BF16)

        def lift(layer):
            lifted = jnp.dot(
                hidden_ref[...], node_in[layer], preferred_element_type=F32
            ).astype(BF16)
            lend(layer, lifted)
            start(lift_copy, layer)
            tables[layer, 0:rows] = lifted

        for layer in range(layers):
            def beside(j, layer=layer):
                if layer == layers - 1:
                    term_geometry(False, j, pack)

            if layer:
                lift(layer)
                radial_net(layer)
            own_part(layer, beside if layer else lent_lift)
            if layer:
                arrive(lift_copy, layer)
            rim_part(layer)
            message = (acc[...].reshape(rows, channels) * (1.0 / slots)).astype(BF16)
            update = silu_of_half(
                0.5 * jnp.dot(message, node_out[layer], preferred_element_type=F32)
            )
            hidden_ref[...] = (hidden_ref[...].astype(F32) + update).astype(BF16)

        across = (((1,), (1,)), ((), ()))
        extra_cols[:, 0:2] = lax.dot_general(
            hidden_ref[...], readout[...], across, preferred_element_type=F32
        )
        site_result[0:2, :] = lax.dot_general(
            readout[...], hidden_ref[...], across, preferred_element_type=F32
        )
        send_terms(False)
        for layer in range(layers):
            gone(lift_copy, layer)

    @pl.when(g == 1)
    def _():
        out = field(own, near_cols, listed * BLOCK)
        for c in range(3):
            outside[c : c + 1, :] = out[c]
        gain = polar[...]
        outside[...] = outside[...] + pairs[...]
        dipole = [gain * outside[c : c + 1, :] for c in range(3)]
        for sweep in range(SWEEPS):
            step = 1 + sweep
            fill_rims(step, jnp.concatenate(dipole + [jnp.zeros((1, rows), F32)], axis=0))
            start(rim_copy, step)
            near_part = []
            for tile in range(own_blocks):
                index = neighbours[:, tile * BLOCK : (tile + 1) * BLOCK]
                local = index & (BLOCK - 1)
                chunk = lax.shift_right_logical(index, 7)
                near_part.append([
                    table_gather(
                        [(b, dipole[c][:, b * BLOCK : (b + 1) * BLOCK]) for b in range(own_blocks)],
                        local,
                        chunk,
                    )
                    for c in range(3)
                ])
            if sweep == 0:
                term_geometry(True, 0, 1)
            arrive(rim_copy, step)
            fresh = [[], [], []]
            for tile in range(own_blocks):
                at = slice(tile * BLOCK, (tile + 1) * BLOCK)
                index = neighbours[:, at]
                local = index & (BLOCK - 1)
                chunk = lax.shift_right_logical(index, 7)
                d = [
                    table_gather(
                        [(own_blocks + side, rim_in[step, side, c : c + 1, :]) for side in range(2)],
                        local,
                        chunk,
                        near_part[tile][c],
                    )
                    for c in range(3)
                ]
                r = [geometry[c, :, at] for c in range(3)]
                w3 = geometry[3, :, at]
                s = (r[0] * d[0] + r[1] * d[1] + r[2] * d[2]) * geometry[4, :, at]
                for c in range(3):
                    total = jnp.sum(r[c] * s - d[c] * w3, axis=0, keepdims=True)
                    fresh[c].append(gain[:, at] * (outside[c : c + 1, at] + total))
            dipole = [jnp.concatenate(f, axis=1) for f in fresh]
        for c in range(3):
            site_result[c : c + 1, :] = dipole[c]
        stacked = jnp.concatenate(dipole + [jnp.zeros((5, rows), F32)], axis=0)
        extra_cols[...] = stacked.T
        send_terms(True)
        for sweep in range(SWEEPS):
            gone(rim_copy, 1 + sweep)

    @pl.loop(0, n, unroll=min(n, 16))
    def _(q):
        for b in range(own_blocks):
            total = jnp.zeros((3, BLOCK), F32)
            for l in range(listed):
                total = total + jnp.where(
                    blocks[l] == q * own_blocks + b, terms[:, l * BLOCK : (l + 1) * BLOCK], 0.0
                )
            term_out[q, b * 3 : (b + 1) * 3, :] = total

    def term_copy(i):
        return pltpu.make_async_remote_copy(
            src_ref=term_out.at[peer(i)],
            dst_ref=term_in.at[p],
            send_sem=term_send,
            recv_sem=term_recv,
            device_id=place(other, peer(i)),
            device_id_type=MESH,
        )

    @pl.loop(0, n, unroll=4)
    def _(i):
        term_copy(i).start()

    gone(rim_copy, 0)
    pltpu.make_async_copy(everyone, everyone, all_send).wait()
    pltpu.make_async_copy(term_in, term_in, term_recv).wait()

    total = jnp.sum(term_in[...], axis=0)
    for b in range(own_blocks):
        response[:, b * BLOCK : (b + 1) * BLOCK] = total[b * 3 : (b + 1) * 3, :]
    pltpu.make_async_copy(term_in, term_in, term_send).wait()


def local(n_dom, n_sub, *args):
    (
        positions,
        charges,
        polar,
        features,
        neighbours,
        send_rows,
        blocks,
        radial_in,
        radial_mid,
        radial_out,
        node_in,
        node_out,
        field_gain,
        readout,
    ) = args
    n = n_dom * n_sub
    rows = positions.shape[1]
    own_blocks = rows // BLOCK
    slots = neighbours.shape[1]
    listed = blocks.shape[0]
    layers, basis, radial = radial_in.shape
    channels = features.shape[1]
    rim = send_rows.shape[1]
    pack = channels // radial
    dma = pltpu.SemaphoreType.DMA
    operands = (
        positions,
        charges.reshape(1, -1),
        polar.reshape(1, -1),
        features,
        neighbours.T,
        send_rows,
        blocks,
        radial_in,
        radial_mid,
        radial_out,
        node_in,
        node_out,
        field_gain.reshape(1, -1),
        readout.T,
    )
    spaces = [pltpu.VMEM] * INPUTS
    spaces[6] = pltpu.SMEM
    shapes = [a.shape for a in operands]
    shapes[3] = (rows + 2 * rim, channels)
    both = pl.pallas_call(
        functools.partial(kernel, n_dom, n_sub),
        out_shape=jax.ShapeDtypeStruct((2, 3, rows), F32),
        in_specs=[pl.BlockSpec(memory_space=pl.ANY)] * INPUTS,
        out_specs=pl.BlockSpec(memory_space=pltpu.VMEM),
        scratch_shapes=[space(shape, a.dtype) for space, shape, a in zip(spaces, shapes, operands)]
        + [
            dma((INPUTS,)),
            pltpu.VMEM((own_blocks, 4, BLOCK), F32),
            pltpu.VMEM((n * own_blocks, 4, BLOCK), F32),
            pltpu.VMEM((4, listed * BLOCK), F32),
            pltpu.VMEM((listed * BLOCK, 8), F32),
            pltpu.VMEM((8, rows), F32),
            pltpu.VMEM((rows, 8), F32),
            pltpu.VMEM((rows, 8), F32),
            pltpu.VMEM((1 + SWEEPS, 2, 4, rim), F32),
            pltpu.VMEM((1 + SWEEPS, 2, 4, rim), F32),
            pltpu.VMEM((5, slots, rows), F32),
            pltpu.VMEM((pack, rows // STRIP, slots // pack, STRIP, rows + 2 * rim), BF16),
            pltpu.VMEM((2 * rim, rows), BF16),
            pltpu.VMEM((slots // pack * rows, pack * basis), BF16),
            pltpu.VMEM((2, slots // pack * rows, channels), BF16),
            pltpu.VMEM((layers, rows // STRIP, slots // pack, STRIP, channels), BF16),
            pltpu.VMEM((pack, rows // STRIP, slots // pack, STRIP, channels), F32),
            pltpu.VMEM((layers, pack * basis, channels), BF16),
            pltpu.VMEM((layers, 2, channels, channels), BF16),
            pltpu.VMEM((layers, pack, channels, channels), BF16),
            pltpu.VMEM((layers, rows + 2 * rim, channels), BF16),
            pltpu.VMEM((layers, 2, rim, channels), BF16),
            pltpu.VMEM((2, listed * BLOCK, 8), F32),
            pltpu.VMEM((5, rows, listed * BLOCK), F32),
            pltpu.VMEM((rows, channels), BF16),
            pltpu.VMEM((rows // STRIP, STRIP, channels), F32),
            pltpu.VMEM((3, rows), F32),
            pltpu.VMEM((3, rows), F32),
            pltpu.VMEM((3, listed * BLOCK), F32),
            pltpu.VMEM((n, own_blocks * 3, BLOCK), F32),
            pltpu.VMEM((n, own_blocks * 3, BLOCK), F32),
            dma(()),
            dma(()),
            dma((1 + SWEEPS, 2)),
            dma((1 + SWEEPS, 2)),
            dma((layers, 2)),
            dma((layers, 2)),
            dma(()),
            dma(()),
        ],
        compiler_params=pltpu.CompilerParams(
            collective_id=0, has_side_effects=True, vmem_limit_bytes=40 * 2**20
        ),
    )(*(pltpu.with_memory_space_constraint(a, pltpu.HBM) for a in operands))
    return both[0], both[1]


def solution(mesh):
    sites = ("grp", "dom", "sub")
    in_specs = (
        P(None, sites),
        P(sites),
        P(sites),
        P(sites, None),
        P(sites, None),
        P(None, sites),
        P(sites),
    ) + (P(),) * 7
    out_specs = (P(None, sites), P(None, sites))
    body = functools.partial(local, mesh.shape["dom"], mesh.shape["sub"])
    return jax.shard_map(body, mesh=mesh, in_specs=in_specs, out_specs=out_specs, check_vma=False)
```

```python
import functools

import jax
import jax.numpy as jnp
from jax import lax
from jax.experimental import pallas as pl
from jax.experimental.pallas import tpu as pltpu
from jax.sharding import PartitionSpec as P

SWEEPS = 4
ROUNDS = SWEEPS // 2
BLOCK = 128
SMOOTH = 1.0
SPACING = 0.75
MESH = pl.DeviceIdType.MESH
INPUTS = 14
STRIP = 16
EARLY = 2
F32 = jnp.float32
BF16 = jnp.bfloat16


def silu_of_half(half):
    return half + half * jnp.tanh(half)


def lane_pick(rows, index):
    shape = index.shape
    return jnp.take_along_axis(
        jnp.broadcast_to(rows, shape), index, axis=1, mode="promise_in_bounds"
    )


def table_gather(pieces, local, chunk, total=None):
    if total is None:
        total = jnp.zeros(local.shape, pieces[0][1].dtype)
    for number, rows in pieces:
        total = jnp.where(chunk == number, lane_pick(rows, local), total)
    return total


def kernel(
    n_dom,
    n_sub,
    *refs,
):
    sources = refs[:INPUTS]
    (
    both,
    positions,
    charges,
    polar,
    features,
    neighbours,
    send_rows,
    blocks,
    radial_in,
    radial_mid,
    radial_out,
    node_in,
    node_out,
    field_gain,
    readout,
    in_sem,
    packet,
    everyone,
    near_rows,
    near_cols,
    own_rows,
    own_cols,
    extra_cols,
    rim_out,
    rim_in,
    flat_out,
    flat_in,
    far_in,
    lists_out,
    lists_in,
    fixed_out,
    fixed_in,
    geometry,
    hot,
    pick,
    wave,
    stage,
    third,
    edge_weight,
    wide_in,
    wide_mid,
    wide_out,
    tables,
    lent,
    lent_cols,
    reach,
    hidden_ref,
    acc,
    outside,
    pairs,
    terms,
    term_out,
    term_in,
    all_send,
    all_recv,
    rim_send,
    rim_recv,
    lift_send,
    lift_recv,
    term_send,
    term_recv,
    flat_send,
    flat_recv,
    far_send,
    far_recv,
    list_send,
    list_recv,
    fixed_send,
    fixed_recv,
    ) = refs[INPUTS:]
    g = lax.axis_index("grp")
    p = lax.axis_index("dom") * n_sub + lax.axis_index("sub")
    site_result, response = both.at[0], both.at[1]
    n = n_dom * n_sub
    rows = positions.shape[1]
    own_blocks = rows // BLOCK
    slots = neighbours.shape[0]
    listed = blocks.shape[0]
    layers, basis, radial = radial_in.shape
    channels = features.shape[1]
    rim = send_rows.shape[1]
    pack = channels // radial
    groups = slots // pack
    strips = rows // STRIP
    other = 1 - g
    held = (
        positions,
        charges,
        polar,
        features,
        neighbours,
        send_rows,
        blocks,
        radial_in,
        radial_mid,
        radial_out,
        node_in,
        node_out,
        field_gain,
        readout,
    )
    early = (0, 1, 2, 4, 5, 6)
    late = (7, 8, 9, 3, 10, 11, 12, 13)
    spread_needs = 4

    def load(number):
        target = held[number]
        if number == 3:
            target = target.at[pl.ds(0, rows)]
        return pltpu.make_async_copy(sources[number], target, in_sem.at[number])

    for number in early:
        load(number).start()

    def place(group, q):
        return (group, lax.div(q, n_sub), lax.rem(q, n_sub))

    def peer(i):
        if n % 4:
            return lax.rem(p + i, n)
        quarter = n // 4
        second = lax.div(2 * p, n)
        turn = lax.div(i, quarter)
        far = second * turn + (1 - second) * (3 - turn)
        return far * quarter + lax.rem(p + i, quarter)

    barrier = pltpu.get_barrier_semaphore()

    @pl.loop(0, n)
    def _(i):
        pl.semaphore_signal(barrier, inc=1, device_id=place(other, peer(i)), device_id_type=MESH)

    @pl.when(p > 0)
    def _():
        pl.semaphore_signal(barrier, inc=1, device_id=place(g, p - 1), device_id_type=MESH)

    @pl.when(p < n - 1)
    def _():
        pl.semaphore_signal(barrier, inc=1, device_id=place(g, p + 1), device_id_type=MESH)

    @pl.when(p > 1)
    def _():
        pl.semaphore_signal(barrier, inc=1, device_id=place(g, p - 2), device_id_type=MESH)

    @pl.when(p < n - 2)
    def _():
        pl.semaphore_signal(barrier, inc=1, device_id=place(g, p + 2), device_id_type=MESH)

    @pl.when(g == 0)
    def _():
        for number in late:
            load(number).start()

    own_rows[...] = jnp.zeros_like(own_rows)
    for number in early:
        load(number).wait()
    own_rows[0:3, :] = positions[...]
    own_rows[3:4, :] = charges[...]
    own = own_rows[...]
    for b in range(own_blocks):
        packet[b] = own[0:4, b * BLOCK : (b + 1) * BLOCK]

    def fill(target, values):
        for side in range(2):
            index = jnp.broadcast_to(send_rows[side : side + 1, :], (values.shape[0], rim))
            target[side] = table_gather(
                [(c, values[:, c * BLOCK : (c + 1) * BLOCK]) for c in range(own_blocks)],
                index & (BLOCK - 1),
                lax.shift_right_logical(index, 7),
            )

    def fill_rims(step, values):
        fill(rim_out.at[step], values)

    def side_copy(src, dst, send, recv, step, side, q):
        return pltpu.make_async_remote_copy(
            src_ref=src,
            dst_ref=dst,
            send_sem=send.at[step, side],
            recv_sem=recv.at[step, side],
            device_id=place(g, q),
            device_id_type=MESH,
        )

    def rim_copy(step, side, q):
        return side_copy(
            rim_out.at[step, side], rim_in.at[step, side], rim_send, rim_recv, step, side, q
        )

    def lift_copy(layer, side, q):
        target = tables.at[layer] if layer else features
        return side_copy(
            lent.at[layer, side],
            target.at[pl.ds(rows + side * rim, rim)],
            lift_send,
            lift_recv,
            layer,
            side,
            q,
        )

    def flat_copy(step, side, q):
        return side_copy(
            flat_out.at[step], flat_in.at[step, side], flat_send, flat_recv, step, side, q
        )

    def far_copy(step, side, q):
        return side_copy(
            rim_out.at[step, side], far_in.at[step, side], far_send, far_recv, step, side, q
        )

    def list_copy(step, side, q):
        return side_copy(
            lists_out.at[side], lists_in.at[side], list_send, list_recv, step, side, q
        )

    def fixed_copy(step, side, q):
        return side_copy(
            fixed_out.at[side], fixed_in.at[side], fixed_send, fixed_recv, step, side, q
        )

    def start(copy, step, away=1):
        @pl.when(p < n - away)
        def _():
            copy(step, 0, p + away).start()

        @pl.when(p > away - 1)
        def _():
            copy(step, 1, p - away).start()

    def arrive(copy, step, away=1):
        @pl.when(p > away - 1)
        def _():
            copy(step, 0, p - away).wait_recv()

        @pl.when(p < n - away)
        def _():
            copy(step, 1, p + away).wait_recv()

    def gone(copy, step, away=1):
        @pl.when(p < n - away)
        def _():
            copy(step, 0, p + away).wait_send()

        @pl.when(p > away - 1)
        def _():
            copy(step, 1, p - away).wait_send()

    def prepare():
        width = rows + 2 * rim
        lane = lax.broadcasted_iota(jnp.int32, (rows, width), 1).astype(jnp.int16)
        listing = jnp.concatenate(
            [neighbours[...].astype(F32), jnp.zeros((BLOCK - slots, rows), F32)], axis=0
        ).T.astype(jnp.int32)
        one, none = jnp.ones((rows, width), BF16), jnp.zeros((rows, width), BF16)
        for k in range(slots):
            entry = jnp.broadcast_to(listing[:, k : k + 1], (rows, BLOCK)).astype(jnp.int16)
            entry = jnp.concatenate([entry] * (width // BLOCK), axis=1)
            mark = jnp.where(entry == lane, one, none)
            hot[k % pack, :, k // pack] = mark.reshape(strips, STRIP, width)
        lists = jnp.concatenate(
            [send_rows[...].astype(F32), jnp.zeros((6, rim), F32)], axis=0
        ).T.astype(jnp.int32)
        site = lax.broadcasted_iota(jnp.int32, (rim, rows), 1)
        for side in range(2):
            pick[side * rim : (side + 1) * rim, :] = jnp.where(
                lists[:, side : side + 1] == site, 1.0, 0.0
            ).astype(BF16)

    def spread():
        for number in late[:spread_needs]:
            load(number).wait()
        spread_r = (
            lax.broadcasted_iota(jnp.int32, (channels, radial), 0) % radial
            == lax.broadcasted_iota(jnp.int32, (channels, radial), 1)
        ).astype(F32).astype(BF16)
        spread_c = (
            lax.broadcasted_iota(jnp.int32, (radial, channels), 1) % radial
            == lax.broadcasted_iota(jnp.int32, (radial, channels), 0)
        ).astype(F32).astype(BF16)
        same_in = (
            lax.broadcasted_iota(jnp.int32, (pack * basis, channels), 0) // basis
            == lax.broadcasted_iota(jnp.int32, (pack * basis, channels), 1) // radial
        )
        same_mid = (
            lax.broadcasted_iota(jnp.int32, (channels, channels), 0) // radial
            == lax.broadcasted_iota(jnp.int32, (channels, channels), 1) // radial
        )
        for layer in range(layers):
            flat = jnp.dot(radial_in[layer], spread_c, preferred_element_type=F32)
            wide_in[layer] = jnp.where(
                same_in, jnp.concatenate([0.5 * flat] * pack, axis=0), 0.0
            ).astype(BF16)
            for m in range(2):
                flat = jnp.dot(
                    jnp.dot(spread_r, radial_mid[layer, m], preferred_element_type=F32).astype(
                        BF16
                    ),
                    spread_c,
                    preferred_element_type=F32,
                )
                wide_mid[layer, m] = jnp.where(same_mid, 0.5 * flat, 0.0).astype(BF16)
            for j in range(pack):
                wide_out[layer, j] = jnp.zeros((channels, channels), BF16)
                wide_out[layer, j, j * radial : (j + 1) * radial, :] = radial_out[layer]

    def lend(layer, values):
        picked = jnp.dot(pick[...], values, preferred_element_type=F32).astype(BF16)
        lent[layer] = picked.reshape(2, rim, channels)

    fill_rims(0, own[0:4])

    @pl.when(g == 0)
    def _():
        spot = lax.broadcasted_iota(jnp.int32, (1, rim), 1)
        names = jnp.zeros((1, rim), F32)
        for l in range(listed):
            names = jnp.where(spot == l, blocks[l].astype(F32), names)
        for side in range(2):
            rim_out[0, side, 3:4, :] = names

    @pl.when(p == 0)
    def _():
        for step in range(1 + ROUNDS):
            rim_in[step, 0] = jnp.zeros((4, rim), F32)
        features[rows : rows + rim] = jnp.zeros((rim, channels), BF16)
        for layer in range(1, layers):
            tables[layer, rows : rows + rim] = jnp.zeros((rim, channels), BF16)

    @pl.when(p == n - 1)
    def _():
        for step in range(1 + ROUNDS):
            rim_in[step, 1] = jnp.zeros((4, rim), F32)
        features[rows + rim :] = jnp.zeros((rim, channels), BF16)
        for layer in range(1, layers):
            tables[layer, rows + rim :] = jnp.zeros((rim, channels), BF16)

    def clear(side, away):
        for step in range(1 + ROUNDS):
            far_in[step, side] = jnp.zeros((4, rim), F32)
            if away == 1:
                flat_in[step, side] = jnp.zeros((4, rows), F32)
        if away == 1:
            lists_in[side] = jnp.zeros((slots, rim), jnp.int32)
            fixed_in[side] = jnp.zeros((4, rim), F32)

    @pl.when(g == 1)
    def _():
        flat_out[0] = own[0:4]
        fill(lists_out, neighbours[...])
        for side, ends in enumerate(((0, 1), (n - 1, n - 2))):
            pl.when(p == ends[0])(functools.partial(clear, side, 1))
            pl.when(p == ends[1])(functools.partial(clear, side, 2))

    @pl.when(g == 0)
    def _():
        prepare()

    sides = [p > 0, p < n - 1, p > 1, p < n - 2]
    pl.semaphore_wait(barrier, n + sum(side.astype(jnp.int32) for side in sides))

    def packet_copy(i):
        return pltpu.make_async_remote_copy(
            src_ref=packet,
            dst_ref=everyone.at[pl.ds(p * own_blocks, own_blocks)],
            send_sem=all_send,
            recv_sem=all_recv,
            device_id=place(other, peer(i)),
            device_id_type=MESH,
        )

    start(rim_copy, 0)

    @pl.when(g == 1)
    def _():
        start(flat_copy, 0)
        start(far_copy, 0, 2)
        start(list_copy, 0)

    @pl.loop(0, n, unroll=4)
    def _(i):
        packet_copy(i).start()

    @pl.when(g == 0)
    def _():
        spread()
        lend(0, features[0:rows])

    own_cols[...] = own.T

    def field(targets, source_cols, count):
        x, y, z = (targets[c : c + 1, :] for c in range(3))

        def step(i, sums):
            source = source_cols[pl.ds(pl.multiple_of(i * 8, 8), 8), :]
            rx = x - source[:, 0:1]
            ry = y - source[:, 1:2]
            rz = z - source[:, 2:3]
            w = lax.rsqrt(rx * rx + ry * ry + rz * rz + SMOOTH)
            s = source[:, 3:4] * (w * w * w)
            return (sums[0] + rx * s, sums[1] + ry * s, sums[2] + rz * s)

        zero = jnp.zeros((8, targets.shape[1]), F32)
        sums = lax.fori_loop(0, count // 8, step, (zero, zero, zero), unroll=True)
        return [jnp.sum(s, axis=0, keepdims=True) for s in sums]

    def term_geometry(dipole, part, parts):
        x, y, z = (near_rows[c : c + 1, :] for c in range(3))
        for i in range(part * rows // 8 // parts, (part + 1) * rows // 8 // parts):
            at = slice(i * 8, i * 8 + 8)
            source = own_cols[at, :]
            r = (x - source[:, 0:1], y - source[:, 1:2], z - source[:, 2:3])
            w = lax.rsqrt(r[0] * r[0] + r[1] * r[1] + r[2] * r[2] + SMOOTH)
            w2 = w * w
            w3 = w2 * w
            for c in range(3):
                reach[c, at, :] = r[c] if dipole else r[c] * w3
            if dipole:
                reach[3, at, :] = w3
                reach[4, at, :] = 3.0 * (w3 * w2)

    def send_terms(dipole):
        def step(i, sums):
            at = pl.ds(pl.multiple_of(i * 8, 8), 8)
            d = extra_cols[at, :]
            r = [reach[c, at, :] for c in range(3)]
            if not dipole:
                return tuple(sums[c] + r[c] * d[:, 0:1] for c in range(3))
            w3 = reach[3, at, :]
            d = [d[:, c : c + 1] for c in range(3)]
            s = (r[0] * d[0] + r[1] * d[1] + r[2] * d[2]) * reach[4, at, :]
            return tuple(sums[c] + (r[c] * s - d[c] * w3) for c in range(3))

        zero = jnp.zeros((8, listed * BLOCK), F32)
        sums = lax.fori_loop(0, rows // 8, step, (zero, zero, zero), unroll=True)
        for c in range(3):
            terms[c : c + 1, :] = jnp.sum(sums[c], axis=0, keepdims=True)

    def lent_pieces(side, c, flat, mine, far):
        flat, mine, far = (rows_[c : c + 1, :] for rows_ in (flat, mine, far))
        rims = (far, mine) if side == 0 else (mine, far)
        return [(b, flat[:, b * BLOCK : (b + 1) * BLOCK]) for b in range(own_blocks)] + [
            (own_blocks + i, rims[i]) for i in range(2)
        ]

    def edges():
        for tile in range(own_blocks):
            at = slice(tile * BLOCK, (tile + 1) * BLOCK)
            index = neighbours[:, at]
            local = index & (BLOCK - 1)
            chunk = lax.shift_right_logical(index, 7)
            picked = []
            for c in range(4):
                pieces = [
                    (b, own_rows[c : c + 1, b * BLOCK : (b + 1) * BLOCK])
                    for b in range(own_blocks)
                ] + [(own_blocks + side, rim_in[0, side, c : c + 1, :]) for side in range(2)]
                picked.append(table_gather(pieces, local, chunk))
            ox, oy, oz = (own_rows[c : c + 1, at] - picked[c] for c in range(3))
            dist_sq = ox * ox + oy * oy + oz * oz + SMOOTH
            yield at, (ox, oy, oz), dist_sq, picked[3], local, chunk

    centre = lax.broadcasted_iota(jnp.int32, (basis, rows), 0).astype(F32) * SPACING

    def waves():
        for q in range(groups):
            parts = []
            for j in range(pack):
                away = jnp.broadcast_to(geometry[0, q * pack + j : q * pack + j + 1, 0:rows], (basis, rows))
                away = away - centre
                parts.append(jnp.exp(-(away * away)))
            turned = jnp.concatenate(parts, axis=0).T
            wave[q * rows : (q + 1) * rows, :] = turned.astype(BF16)

    def radial_net(layer):
        half = groups // 2
        spans = [range(half), range(half, groups)]
        for step in range(3):
            for part, span in enumerate(spans):
                at = slice(span[0] * rows, (span[-1] + 1) * rows)
                if step == 0:
                    source, weight = wave[at, :], wide_in[layer]
                else:
                    source, weight = stage[step - 1, at, :], wide_mid[layer, step - 1]
                h = silu_of_half(jnp.dot(source, weight, preferred_element_type=F32)).astype(BF16)
                if step < 2:
                    stage[step, at, :] = h
                else:
                    for i, q in enumerate(span):
                        third[layer, :, q] = h[i * rows : (i + 1) * rows].reshape(
                            strips, STRIP, channels
                        )

    def edge_part(layer, j):
        edge_weight[j] = jnp.dot(
            third[layer].reshape(groups * rows, channels),
            wide_out[layer, j],
            preferred_element_type=F32,
        ).reshape(strips, groups, STRIP, channels)

    def own_part(layer, beside):
        for j in range(pack):
            beside(j)
            if layer or j >= EARLY:
                edge_part(layer, j)
            gather_part(layer, j, 0, rows)

    def rim_part(layer):
        for j in range(pack):
            gather_part(layer, j, rows, 2 * rim)

    def gather_part(layer, j, first, count):
        source = jnp.dot(
            hot[j, :, :, :, first : first + count].reshape(groups * rows, count),
            tables[layer, first : first + count],
            preferred_element_type=F32,
        )
        product = edge_weight[j] * source.reshape(strips, groups, STRIP, channels)
        total = jnp.sum(product, axis=1)
        if first or j:
            total = acc[...] + total
        acc[...] = total

    @pl.when(g == 0)
    def _():
        arrive(rim_copy, 0)
        start(lift_copy, 0)
        for at, _, dist_sq, _, _, _ in edges():
            geometry[0, :, at] = jnp.sqrt(dist_sq)
        waves()
        radial_net(0)
        for j in range(EARLY):
            edge_part(0, j)

    @pl.when(g == 1)
    def _():
        arrive(rim_copy, 0)
        for at, offset, dist_sq, source_charge, _, _ in edges():
            w = lax.rsqrt(dist_sq)
            w2 = w * w
            w3 = w2 * w
            s = source_charge * w3
            for c in range(3):
                geometry[c, :, at] = offset[c]
                extra = jnp.sum(offset[c] * s, axis=0, keepdims=True)
                pairs[c : c + 1, at] = extra
            geometry[3, :, at] = w3
            geometry[4, :, at] = 3.0 * (w3 * w2)
        arrive(flat_copy, 0)
        arrive(far_copy, 0, 2)
        arrive(list_copy, 0)
        for side in range(2):
            at = slice(rows + side * rim, rows + (side + 1) * rim)
            index = lists_in[side]
            local = index & (BLOCK - 1)
            chunk = lax.shift_right_logical(index, 7)
            offset = [
                rim_in[0, side, c : c + 1, :]
                - table_gather(
                    lent_pieces(side, c, flat_in[0, side], rim_out[0, 1 - side], far_in[0, side]),
                    local,
                    chunk,
                )
                for c in range(3)
            ]
            w = lax.rsqrt(
                offset[0] * offset[0] + offset[1] * offset[1] + offset[2] * offset[2] + SMOOTH
            )
            w2 = w * w
            w3 = w2 * w
            for c in range(3):
                geometry[c, :, at] = offset[c]
            geometry[3, :, at] = w3
            geometry[4, :, at] = 3.0 * (w3 * w2)

    pltpu.make_async_copy(everyone, everyone, all_recv).wait()
    for l in range(listed):
        tile = everyone[blocks[l]]
        near_rows[:, l * BLOCK : (l + 1) * BLOCK] = tile
        near_cols[l * BLOCK : (l + 1) * BLOCK, :] = jnp.concatenate(
            [tile, jnp.zeros_like(tile)], axis=0
        ).T

    def lent_near():
        names = [
            [jnp.broadcast_to(rim_in[0, side, 3:4, l : l + 1], (4, BLOCK)) for l in range(listed)]
            for side in range(2)
        ]

        def step(b, found):
            tile = everyone[b]
            return tuple(
                tuple(
                    jnp.where(names[side][l] == b.astype(F32), tile, found[side][l])
                    for l in range(listed)
                )
                for side in range(2)
            )

        blank = jnp.zeros((4, BLOCK), F32)
        found = lax.fori_loop(
            0, n * own_blocks, step, ((blank,) * listed,) * 2, unroll=max(8, min(32, n * own_blocks))
        )
        for side in range(2):
            for l in range(listed):
                lent_cols[side, l * BLOCK : (l + 1) * BLOCK, :] = jnp.concatenate(
                    [found[side][l], blank], axis=0
                ).T

    @pl.when(g == 0)
    def _():
        for number in late[spread_needs:]:
            load(number).wait()

        def strength_of(fields):
            fx, fy, fz = fields
            return jnp.sqrt(1.0 + fx * fx + fy * fy + fz * fz)

        def column_of(strength):
            return jnp.broadcast_to(strength, (8, strength.shape[1])).T[:, 0:1]

        def embed(column, at):
            return (features[at].astype(F32) + column * field_gain[...]).astype(BF16)

        def lent_field(side):
            return field(rim_in[0, side], lent_cols.at[side], listed * BLOCK)

        strength = strength_of(field(own, near_cols, listed * BLOCK))
        site_result[2:3, :] = strength
        hidden_ref[...] = embed(column_of(strength), slice(0, rows))
        tables[0, 0:rows] = jnp.dot(
            hidden_ref[...], node_in[0], preferred_element_type=F32
        ).astype(BF16)
        fields, columns = [], []

        def lent_lift(j):
            if j == 0:
                lent_near()
            if j < 2:
                fields.append(lent_field(j))
            if j == 2:
                columns.extend(column_of(strength_of(part)) for part in fields)
            if j == pack - 1:
                arrive(lift_copy, 0)
                ends = (p > 0, p < n - 1)
                for side in range(2):
                    at = slice(rows + side * rim, rows + (side + 1) * rim)
                    hidden = embed(columns[side], at)
                    lifted = jnp.dot(hidden, node_in[0], preferred_element_type=F32)
                    tables[0, at] = jnp.where(ends[side], lifted, 0.0).astype(BF16)

        def lift(layer):
            lifted = jnp.dot(
                hidden_ref[...], node_in[layer], preferred_element_type=F32
            ).astype(BF16)
            lend(layer, lifted)
            start(lift_copy, layer)
            tables[layer, 0:rows] = lifted

        for layer in range(layers):
            def beside(j, layer=layer):
                if layer == layers - 1:
                    term_geometry(False, j, pack)

            if layer:
                lift(layer)
                radial_net(layer)
            own_part(layer, beside if layer else lent_lift)
            if layer:
                arrive(lift_copy, layer)
            rim_part(layer)
            message = (acc[...].reshape(rows, channels) * (1.0 / slots)).astype(BF16)
            update = silu_of_half(
                0.5 * jnp.dot(message, node_out[layer], preferred_element_type=F32)
            )
            hidden_ref[...] = (hidden_ref[...].astype(F32) + update).astype(BF16)

        across = (((1,), (1,)), ((), ()))
        extra_cols[:, 0:2] = lax.dot_general(
            hidden_ref[...], readout[...], across, preferred_element_type=F32
        )
        site_result[0:2, :] = lax.dot_general(
            readout[...], hidden_ref[...], across, preferred_element_type=F32
        )
        send_terms(False)
        for layer in range(layers):
            gone(lift_copy, layer)

    @pl.when(g == 1)
    def _():
        out = field(own, near_cols, listed * BLOCK)
        for c in range(3):
            outside[c : c + 1, :] = out[c]
        gain = polar[...]
        outside[...] = outside[...] + pairs[...]
        dipole = [gain * outside[c : c + 1, :] for c in range(3)]

        def induced(at, index, pieces, begun=(None, None, None)):
            local = index & (BLOCK - 1)
            chunk = lax.shift_right_logical(index, 7)
            d = [table_gather(pieces(c), local, chunk, begun[c]) for c in range(3)]
            r = [geometry[c, :, at] for c in range(3)]
            w3 = geometry[3, :, at]
            s = (r[0] * d[0] + r[1] * d[1] + r[2] * d[2]) * geometry[4, :, at]
            return [jnp.sum(r[c] * s - d[c] * w3, axis=0, keepdims=True) for c in range(3)]

        def own_pieces(c, values):
            return [(b, values[c][:, b * BLOCK : (b + 1) * BLOCK]) for b in range(own_blocks)]

        def own_sweep(values, rims, begun):
            fresh = [[], [], []]
            for tile in range(own_blocks):
                at = slice(tile * BLOCK, (tile + 1) * BLOCK)

                def pieces(c):
                    ends = [(own_blocks + side, rims(side, c)) for side in range(2)]
                    return ends if begun else own_pieces(c, values) + ends

                totals = induced(
                    at, neighbours[:, at], pieces, begun[tile] if begun else (None, None, None)
                )
                for c in range(3):
                    fresh[c].append(gain[:, at] * (outside[c : c + 1, at] + totals[c]))
            return [jnp.concatenate(f, axis=1) for f in fresh]

        for sweep in range(ROUNDS):
            step = 1 + sweep
            values = jnp.concatenate(dipole + [jnp.zeros((1, rows), F32)], axis=0)
            fill_rims(step, values)
            start(rim_copy, step)
            start(far_copy, step, 2)
            flat_out[step] = values
            start(flat_copy, step)
            if sweep == 0:
                fill(fixed_out, jnp.concatenate([outside[...], gain], axis=0))
                start(fixed_copy, 0)
            begun = []
            for tile in range(own_blocks):
                index = neighbours[:, tile * BLOCK : (tile + 1) * BLOCK]
                local = index & (BLOCK - 1)
                chunk = lax.shift_right_logical(index, 7)
                begun.append([table_gather(own_pieces(c, dipole), local, chunk) for c in range(3)])
            if sweep == 0:
                term_geometry(True, 0, 1)
            arrive(rim_copy, step)
            arrive(far_copy, step, 2)
            arrive(flat_copy, step)
            if sweep == 0:
                arrive(fixed_copy, 0)
            middle = own_sweep(
                dipole, lambda side, c: rim_in[step, side, c : c + 1, :], begun
            )
            lent_middle = []
            for side in range(2):
                at = slice(rows + side * rim, rows + (side + 1) * rim)
                totals = induced(
                    at,
                    lists_in[side],
                    lambda c: lent_pieces(
                        side, c, flat_in[step, side], rim_out[step, 1 - side], far_in[step, side]
                    ),
                )
                lent_middle.append([
                    fixed_in[side, 3:4, :] * (fixed_in[side, c : c + 1, :] + totals[c])
                    for c in range(3)
                ])
            dipole = own_sweep(middle, lambda side, c: lent_middle[side][c], None)
        for c in range(3):
            site_result[c : c + 1, :] = dipole[c]
        stacked = jnp.concatenate(dipole + [jnp.zeros((5, rows), F32)], axis=0)
        extra_cols[...] = stacked.T
        send_terms(True)
        for step in range(1 + ROUNDS):
            if step:
                gone(rim_copy, step)
            gone(far_copy, step, 2)
            gone(flat_copy, step)
        gone(list_copy, 0)
        gone(fixed_copy, 0)

    @pl.loop(0, n, unroll=min(n, 16))
    def _(q):
        for b in range(own_blocks):
            total = jnp.zeros((3, BLOCK), F32)
            for l in range(listed):
                total = total + jnp.where(
                    blocks[l] == q * own_blocks + b, terms[:, l * BLOCK : (l + 1) * BLOCK], 0.0
                )
            term_out[q, b * 3 : (b + 1) * 3, :] = total

    def term_copy(i):
        return pltpu.make_async_remote_copy(
            src_ref=term_out.at[peer(i)],
            dst_ref=term_in.at[p],
            send_sem=term_send,
            recv_sem=term_recv,
            device_id=place(other, peer(i)),
            device_id_type=MESH,
        )

    @pl.loop(0, n, unroll=4)
    def _(i):
        term_copy(i).start()

    gone(rim_copy, 0)
    pltpu.make_async_copy(everyone, everyone, all_send).wait()
    pltpu.make_async_copy(term_in, term_in, term_recv).wait()

    total = jnp.sum(term_in[...], axis=0)
    for b in range(own_blocks):
        response[:, b * BLOCK : (b + 1) * BLOCK] = total[b * 3 : (b + 1) * 3, :]
    pltpu.make_async_copy(term_in, term_in, term_send).wait()


def local(n_dom, n_sub, *args):
    (
        positions,
        charges,
        polar,
        features,
        neighbours,
        send_rows,
        blocks,
        radial_in,
        radial_mid,
        radial_out,
        node_in,
        node_out,
        field_gain,
        readout,
    ) = args
    n = n_dom * n_sub
    rows = positions.shape[1]
    own_blocks = rows // BLOCK
    slots = neighbours.shape[1]
    listed = blocks.shape[0]
    layers, basis, radial = radial_in.shape
    channels = features.shape[1]
    rim = send_rows.shape[1]
    pack = channels // radial
    dma = pltpu.SemaphoreType.DMA
    operands = (
        positions,
        charges.reshape(1, -1),
        polar.reshape(1, -1),
        features,
        neighbours.T,
        send_rows,
        blocks,
        radial_in,
        radial_mid,
        radial_out,
        node_in,
        node_out,
        field_gain.reshape(1, -1),
        readout.T,
    )
    spaces = [pltpu.VMEM] * INPUTS
    spaces[6] = pltpu.SMEM
    shapes = [a.shape for a in operands]
    shapes[3] = (rows + 2 * rim, channels)
    both = pl.pallas_call(
        functools.partial(kernel, n_dom, n_sub),
        out_shape=jax.ShapeDtypeStruct((2, 3, rows), F32),
        in_specs=[pl.BlockSpec(memory_space=pl.ANY)] * INPUTS,
        out_specs=pl.BlockSpec(memory_space=pltpu.VMEM),
        scratch_shapes=[space(shape, a.dtype) for space, shape, a in zip(spaces, shapes, operands)]
        + [
            dma((INPUTS,)),
            pltpu.VMEM((own_blocks, 4, BLOCK), F32),
            pltpu.VMEM((n * own_blocks, 4, BLOCK), F32),
            pltpu.VMEM((4, listed * BLOCK), F32),
            pltpu.VMEM((listed * BLOCK, 8), F32),
            pltpu.VMEM((8, rows), F32),
            pltpu.VMEM((rows, 8), F32),
            pltpu.VMEM((rows, 8), F32),
            pltpu.VMEM((1 + ROUNDS, 2, 4, rim), F32),
            pltpu.VMEM((1 + ROUNDS, 2, 4, rim), F32),
            pltpu.VMEM((1 + ROUNDS, 4, rows), F32),
            pltpu.VMEM((1 + ROUNDS, 2, 4, rows), F32),
            pltpu.VMEM((1 + ROUNDS, 2, 4, rim), F32),
            pltpu.VMEM((2, slots, rim), jnp.int32),
            pltpu.VMEM((2, slots, rim), jnp.int32),
            pltpu.VMEM((2, 4, rim), F32),
            pltpu.VMEM((2, 4, rim), F32),
            pltpu.VMEM((5, slots, rows + 2 * rim), F32),
            pltpu.VMEM((pack, rows // STRIP, slots // pack, STRIP, rows + 2 * rim), BF16),
            pltpu.VMEM((2 * rim, rows), BF16),
            pltpu.VMEM((slots // pack * rows, pack * basis), BF16),
            pltpu.VMEM((2, slots // pack * rows, channels), BF16),
            pltpu.VMEM((layers, rows // STRIP, slots // pack, STRIP, channels), BF16),
            pltpu.VMEM((pack, rows // STRIP, slots // pack, STRIP, channels), F32),
            pltpu.VMEM((layers, pack * basis, channels), BF16),
            pltpu.VMEM((layers, 2, channels, channels), BF16),
            pltpu.VMEM((layers, pack, channels, channels), BF16),
            pltpu.VMEM((layers, rows + 2 * rim, channels), BF16),
            pltpu.VMEM((layers, 2, rim, channels), BF16),
            pltpu.VMEM((2, listed * BLOCK, 8), F32),
            pltpu.VMEM((5, rows, listed * BLOCK), F32),
            pltpu.VMEM((rows, channels), BF16),
            pltpu.VMEM((rows // STRIP, STRIP, channels), F32),
            pltpu.VMEM((3, rows), F32),
            pltpu.VMEM((3, rows), F32),
            pltpu.VMEM((3, listed * BLOCK), F32),
            pltpu.VMEM((n, own_blocks * 3, BLOCK), F32),
            pltpu.VMEM((n, own_blocks * 3, BLOCK), F32),
            dma(()),
            dma(()),
            dma((1 + ROUNDS, 2)),
            dma((1 + ROUNDS, 2)),
            dma((layers, 2)),
            dma((layers, 2)),
            dma(()),
            dma(()),
            dma((1 + ROUNDS, 2)),
            dma((1 + ROUNDS, 2)),
            dma((1 + ROUNDS, 2)),
            dma((1 + ROUNDS, 2)),
            dma((1, 2)),
            dma((1, 2)),
            dma((1, 2)),
            dma((1, 2)),
        ],
        compiler_params=pltpu.CompilerParams(
            collective_id=0, has_side_effects=True, vmem_limit_bytes=40 * 2**20
        ),
    )(*(pltpu.with_memory_space_constraint(a, pltpu.HBM) for a in operands))
    return both[0], both[1]


def solution(mesh):
    sites = ("grp", "dom", "sub")
    in_specs = (
        P(None, sites),
        P(sites),
        P(sites),
        P(sites, None),
        P(sites, None),
        P(None, sites),
        P(sites),
    ) + (P(),) * 7
    out_specs = (P(None, sites), P(None, sites))
    body = functools.partial(local, mesh.shape["dom"], mesh.shape["sub"])
    return jax.shard_map(body, mesh=mesh, in_specs=in_specs, out_specs=out_specs, check_vma=False)
```

```python
import functools

import jax
import jax.numpy as jnp
from jax import lax
from jax.experimental import pallas as pl
from jax.experimental.pallas import tpu as pltpu
from jax.sharding import PartitionSpec as P

SWEEPS = 4
ROUNDS = SWEEPS // 2
BLOCK = 128
SMOOTH = 1.0
SPACING = 0.75
MESH = pl.DeviceIdType.MESH
INPUTS = 14
STRIP = 16
EARLY = 2
F32 = jnp.float32
BF16 = jnp.bfloat16


def silu_of_half(half):
    return half + half * jnp.tanh(half)


def lane_pick(rows, index):
    shape = index.shape
    return jnp.take_along_axis(
        jnp.broadcast_to(rows, shape), index, axis=1, mode="promise_in_bounds"
    )


def table_gather(pieces, local, chunk, total=None):
    if total is None:
        total = jnp.zeros(local.shape, pieces[0][1].dtype)
    for number, rows in pieces:
        total = jnp.where(chunk == number, lane_pick(rows, local), total)
    return total


def kernel(
    n_dom,
    n_sub,
    *refs,
):
    sources = refs[:INPUTS]
    (
    both,
    positions,
    charges,
    polar,
    features,
    neighbours,
    send_rows,
    blocks,
    radial_in,
    radial_mid,
    radial_out,
    node_in,
    node_out,
    field_gain,
    readout,
    in_sem,
    packet,
    everyone,
    near_rows,
    near_cols,
    own_rows,
    own_cols,
    extra_cols,
    rim_out,
    rim_in,
    flat_out,
    flat_in,
    far_in,
    lists_out,
    lists_in,
    fixed_out,
    fixed_in,
    geometry,
    hot,
    pick,
    wave,
    stage,
    third,
    edge_weight,
    wide_in,
    wide_mid,
    wide_out,
    tables,
    lent,
    lent_cols,
    reach,
    hidden_ref,
    acc,
    outside,
    pairs,
    terms,
    term_out,
    term_in,
    all_send,
    all_recv,
    rim_send,
    rim_recv,
    lift_send,
    lift_recv,
    term_send,
    term_recv,
    flat_send,
    flat_recv,
    far_send,
    far_recv,
    list_send,
    list_recv,
    fixed_send,
    fixed_recv,
    ) = refs[INPUTS:]
    g = lax.axis_index("grp")
    p = lax.axis_index("dom") * n_sub + lax.axis_index("sub")
    site_result, response = both.at[0], both.at[1]
    n = n_dom * n_sub
    rows = positions.shape[1]
    own_blocks = rows // BLOCK
    slots = neighbours.shape[0]
    listed = blocks.shape[0]
    layers, basis, radial = radial_in.shape
    channels = features.shape[1]
    rim = send_rows.shape[1]
    pack = channels // radial
    groups = slots // pack
    strips = rows // STRIP
    other = 1 - g
    held = (
        positions,
        charges,
        polar,
        features,
        neighbours,
        send_rows,
        blocks,
        radial_in,
        radial_mid,
        radial_out,
        node_in,
        node_out,
        field_gain,
        readout,
    )
    early = (0, 1, 2, 4, 5, 6)
    late = (7, 8, 9, 3, 10, 11, 12, 13)
    spread_needs = 4

    def load(number):
        target = held[number]
        if number == 3:
            target = target.at[pl.ds(0, rows)]
        return pltpu.make_async_copy(sources[number], target, in_sem.at[number])

    for number in early:
        load(number).start()

    def place(group, q):
        return (group, lax.div(q, n_sub), lax.rem(q, n_sub))

    def peer(i):
        if n % 4:
            return lax.rem(p + i, n)
        quarter = n // 4
        second = lax.div(2 * p, n)
        turn = lax.div(i, quarter)
        far = second * turn + (1 - second) * (3 - turn)
        return far * quarter + lax.rem(p + i, quarter)

    barrier = pltpu.get_barrier_semaphore()

    @pl.loop(0, n)
    def _(i):
        pl.semaphore_signal(barrier, inc=1, device_id=place(other, peer(i)), device_id_type=MESH)

    @pl.when(p > 0)
    def _():
        pl.semaphore_signal(barrier, inc=1, device_id=place(g, p - 1), device_id_type=MESH)

    @pl.when(p < n - 1)
    def _():
        pl.semaphore_signal(barrier, inc=1, device_id=place(g, p + 1), device_id_type=MESH)

    @pl.when(p > 1)
    def _():
        pl.semaphore_signal(barrier, inc=1, device_id=place(g, p - 2), device_id_type=MESH)

    @pl.when(p < n - 2)
    def _():
        pl.semaphore_signal(barrier, inc=1, device_id=place(g, p + 2), device_id_type=MESH)

    @pl.when(g == 0)
    def _():
        for number in late:
            load(number).start()

    own_rows[...] = jnp.zeros_like(own_rows)
    for number in early:
        load(number).wait()
    own_rows[0:3, :] = positions[...]
    own_rows[3:4, :] = charges[...]
    own = own_rows[...]
    for b in range(own_blocks):
        packet[b] = own[0:4, b * BLOCK : (b + 1) * BLOCK]

    def fill(target, values):
        for side in range(2):
            index = jnp.broadcast_to(send_rows[side : side + 1, :], (values.shape[0], rim))
            target[side] = table_gather(
                [(c, values[:, c * BLOCK : (c + 1) * BLOCK]) for c in range(own_blocks)],
                index & (BLOCK - 1),
                lax.shift_right_logical(index, 7),
            )

    def fill_rims(step, values):
        fill(rim_out.at[step], values)

    def side_copy(src, dst, send, recv, step, side, q):
        return pltpu.make_async_remote_copy(
            src_ref=src,
            dst_ref=dst,
            send_sem=send.at[step, side],
            recv_sem=recv.at[step, side],
            device_id=place(g, q),
            device_id_type=MESH,
        )

    def rim_copy(step, side, q):
        return side_copy(
            rim_out.at[step, side], rim_in.at[step, side], rim_send, rim_recv, step, side, q
        )

    def lift_copy(layer, side, q):
        target = tables.at[layer] if layer else features
        return side_copy(
            lent.at[layer, side],
            target.at[pl.ds(rows + side * rim, rim)],
            lift_send,
            lift_recv,
            layer,
            side,
            q,
        )

    def flat_copy(step, side, q):
        return side_copy(
            flat_out.at[step], flat_in.at[step, side], flat_send, flat_recv, step, side, q
        )

    def far_copy(step, side, q):
        return side_copy(
            rim_out.at[step, side], far_in.at[step, side], far_send, far_recv, step, side, q
        )

    def list_copy(step, side, q):
        return side_copy(
            lists_out.at[side], lists_in.at[side], list_send, list_recv, step, side, q
        )

    def fixed_copy(step, side, q):
        return side_copy(
            fixed_out.at[side], fixed_in.at[side], fixed_send, fixed_recv, step, side, q
        )

    def start(copy, step, away=1):
        @pl.when(p < n - away)
        def _():
            copy(step, 0, p + away).start()

        @pl.when(p > away - 1)
        def _():
            copy(step, 1, p - away).start()

    def arrive(copy, step, away=1):
        @pl.when(p > away - 1)
        def _():
            copy(step, 0, p - away).wait_recv()

        @pl.when(p < n - away)
        def _():
            copy(step, 1, p + away).wait_recv()

    def gone(copy, step, away=1):
        @pl.when(p < n - away)
        def _():
            copy(step, 0, p + away).wait_send()

        @pl.when(p > away - 1)
        def _():
            copy(step, 1, p - away).wait_send()

    def mark_slots(span):
        width = rows + 2 * rim
        lane = lax.broadcasted_iota(jnp.int32, (rows, width), 1).astype(jnp.int16)
        listing = jnp.concatenate(
            [neighbours[...].astype(F32), jnp.zeros((BLOCK - slots, rows), F32)], axis=0
        ).T.astype(jnp.int32)
        one, none = jnp.ones((rows, width), BF16), jnp.zeros((rows, width), BF16)
        for k in span:
            entry = jnp.broadcast_to(listing[:, k : k + 1], (rows, BLOCK)).astype(jnp.int16)
            entry = jnp.concatenate([entry] * (width // BLOCK), axis=1)
            mark = jnp.where(entry == lane, one, none)
            hot[k % pack, :, k // pack] = mark.reshape(strips, STRIP, width)

    def mark_lent():
        lists = jnp.concatenate(
            [send_rows[...].astype(F32), jnp.zeros((6, rim), F32)], axis=0
        ).T.astype(jnp.int32)
        site = lax.broadcasted_iota(jnp.int32, (rim, rows), 1)
        for side in range(2):
            pick[side * rim : (side + 1) * rim, :] = jnp.where(
                lists[:, side : side + 1] == site, 1.0, 0.0
            ).astype(BF16)

    def spread():
        for number in late[:spread_needs]:
            load(number).wait()
        spread_r = (
            lax.broadcasted_iota(jnp.int32, (channels, radial), 0) % radial
            == lax.broadcasted_iota(jnp.int32, (channels, radial), 1)
        ).astype(F32).astype(BF16)
        spread_c = (
            lax.broadcasted_iota(jnp.int32, (radial, channels), 1) % radial
            == lax.broadcasted_iota(jnp.int32, (radial, channels), 0)
        ).astype(F32).astype(BF16)
        same_in = (
            lax.broadcasted_iota(jnp.int32, (pack * basis, channels), 0) // basis
            == lax.broadcasted_iota(jnp.int32, (pack * basis, channels), 1) // radial
        )
        same_mid = (
            lax.broadcasted_iota(jnp.int32, (channels, channels), 0) // radial
            == lax.broadcasted_iota(jnp.int32, (channels, channels), 1) // radial
        )
        for layer in range(layers):
            flat = jnp.dot(radial_in[layer], spread_c, preferred_element_type=F32)
            wide_in[layer] = jnp.where(
                same_in, jnp.concatenate([0.5 * flat] * pack, axis=0), 0.0
            ).astype(BF16)
            for m in range(2):
                flat = jnp.dot(
                    jnp.dot(spread_r, radial_mid[layer, m], preferred_element_type=F32).astype(
                        BF16
                    ),
                    spread_c,
                    preferred_element_type=F32,
                )
                wide_mid[layer, m] = jnp.where(same_mid, 0.5 * flat, 0.0).astype(BF16)
            for j in range(pack):
                wide_out[layer, j] = jnp.zeros((channels, channels), BF16)
                wide_out[layer, j, j * radial : (j + 1) * radial, :] = radial_out[layer]

    def lend(layer, values):
        picked = jnp.dot(pick[...], values, preferred_element_type=F32).astype(BF16)
        lent[layer] = picked.reshape(2, rim, channels)

    fill_rims(0, own[0:4])

    @pl.when(g == 0)
    def _():
        spot = lax.broadcasted_iota(jnp.int32, (1, rim), 1)
        names = jnp.zeros((1, rim), F32)
        for l in range(listed):
            names = jnp.where(spot == l, blocks[l].astype(F32), names)
        for side in range(2):
            rim_out[0, side, 3:4, :] = names

    @pl.when(p == 0)
    def _():
        for step in range(1 + ROUNDS):
            rim_in[step, 0] = jnp.zeros((4, rim), F32)
        features[rows : rows + rim] = jnp.zeros((rim, channels), BF16)
        for layer in range(1, layers):
            tables[layer, rows : rows + rim] = jnp.zeros((rim, channels), BF16)

    @pl.when(p == n - 1)
    def _():
        for step in range(1 + ROUNDS):
            rim_in[step, 1] = jnp.zeros((4, rim), F32)
        features[rows + rim :] = jnp.zeros((rim, channels), BF16)
        for layer in range(1, layers):
            tables[layer, rows + rim :] = jnp.zeros((rim, channels), BF16)

    def clear(side, away):
        for step in range(1 + ROUNDS):
            far_in[step, side] = jnp.zeros((4, rim), F32)
            if away == 1:
                flat_in[step, side] = jnp.zeros((4, rows), F32)
        if away == 1:
            lists_in[side] = jnp.zeros((slots, rim), jnp.int32)
            fixed_in[side] = jnp.zeros((4, rim), F32)

    @pl.when(g == 1)
    def _():
        flat_out[0] = own[0:4]
        fill(lists_out, neighbours[...])
        for side, ends in enumerate(((0, 1), (n - 1, n - 2))):
            pl.when(p == ends[0])(functools.partial(clear, side, 1))
            pl.when(p == ends[1])(functools.partial(clear, side, 2))

    @pl.when(g == 0)
    def _():
        mark_slots(range(slots // 2))

    sides = [p > 0, p < n - 1, p > 1, p < n - 2]
    pl.semaphore_wait(barrier, n + sum(side.astype(jnp.int32) for side in sides))

    def packet_copy(i):
        return pltpu.make_async_remote_copy(
            src_ref=packet,
            dst_ref=everyone.at[pl.ds(p * own_blocks, own_blocks)],
            send_sem=all_send,
            recv_sem=all_recv,
            device_id=place(other, peer(i)),
            device_id_type=MESH,
        )

    start(rim_copy, 0)

    @pl.loop(0, n, unroll=4)
    def _(i):
        packet_copy(i).start()

    @pl.when(g == 0)
    def _():
        mark_lent()
        spread()
        mark_slots(range(slots // 2, slots))
        lend(0, features[0:rows])

    own_cols[...] = own.T

    def field(targets, source_cols, count):
        x, y, z = (targets[c : c + 1, :] for c in range(3))

        def step(i, sums):
            source = source_cols[pl.ds(pl.multiple_of(i * 8, 8), 8), :]
            rx = x - source[:, 0:1]
            ry = y - source[:, 1:2]
            rz = z - source[:, 2:3]
            w = lax.rsqrt(rx * rx + ry * ry + rz * rz + SMOOTH)
            s = source[:, 3:4] * (w * w * w)
            return (sums[0] + rx * s, sums[1] + ry * s, sums[2] + rz * s)

        zero = jnp.zeros((8, targets.shape[1]), F32)
        sums = lax.fori_loop(0, count // 8, step, (zero, zero, zero), unroll=True)
        return [jnp.sum(s, axis=0, keepdims=True) for s in sums]

    def term_geometry(dipole, part, parts):
        x, y, z = (near_rows[c : c + 1, :] for c in range(3))
        for i in range(part * rows // 8 // parts, (part + 1) * rows // 8 // parts):
            at = slice(i * 8, i * 8 + 8)
            source = own_cols[at, :]
            r = (x - source[:, 0:1], y - source[:, 1:2], z - source[:, 2:3])
            w = lax.rsqrt(r[0] * r[0] + r[1] * r[1] + r[2] * r[2] + SMOOTH)
            w2 = w * w
            w3 = w2 * w
            for c in range(3):
                reach[c, at, :] = r[c] if dipole else r[c] * w3
            if dipole:
                reach[3, at, :] = w3
                reach[4, at, :] = 3.0 * (w3 * w2)

    def send_terms(dipole):
        def step(i, sums):
            at = pl.ds(pl.multiple_of(i * 8, 8), 8)
            d = extra_cols[at, :]
            r = [reach[c, at, :] for c in range(3)]
            if not dipole:
                return tuple(sums[c] + r[c] * d[:, 0:1] for c in range(3))
            w3 = reach[3, at, :]
            d = [d[:, c : c + 1] for c in range(3)]
            s = (r[0] * d[0] + r[1] * d[1] + r[2] * d[2]) * reach[4, at, :]
            return tuple(sums[c] + (r[c] * s - d[c] * w3) for c in range(3))

        zero = jnp.zeros((8, listed * BLOCK), F32)
        sums = lax.fori_loop(0, rows // 8, step, (zero, zero, zero), unroll=True)
        for c in range(3):
            terms[c : c + 1, :] = jnp.sum(sums[c], axis=0, keepdims=True)

    def lent_pieces(side, c, flat, mine, far):
        flat, mine, far = (rows_[c : c + 1, :] for rows_ in (flat, mine, far))
        rims = (far, mine) if side == 0 else (mine, far)
        return [(b, flat[:, b * BLOCK : (b + 1) * BLOCK]) for b in range(own_blocks)] + [
            (own_blocks + i, rims[i]) for i in range(2)
        ]

    def lent_geometry():
        arrive(flat_copy, 0)
        arrive(far_copy, 0, 2)
        arrive(list_copy, 0)
        for side in range(2):
            at = slice(rows + side * rim, rows + (side + 1) * rim)
            index = lists_in[side]
            local = index & (BLOCK - 1)
            chunk = lax.shift_right_logical(index, 7)
            offset = [
                rim_in[0, side, c : c + 1, :]
                - table_gather(
                    lent_pieces(side, c, flat_in[0, side], rim_out[0, 1 - side], far_in[0, side]),
                    local,
                    chunk,
                )
                for c in range(3)
            ]
            w = lax.rsqrt(
                offset[0] * offset[0] + offset[1] * offset[1] + offset[2] * offset[2] + SMOOTH
            )
            w2 = w * w
            w3 = w2 * w
            for c in range(3):
                geometry[c, :, at] = offset[c]
            geometry[3, :, at] = w3
            geometry[4, :, at] = 3.0 * (w3 * w2)

    def edge_index(tile):
        index = neighbours[:, tile * BLOCK : (tile + 1) * BLOCK]
        return index & (BLOCK - 1), lax.shift_right_logical(index, 7)

    def own_edges(count):
        return [
            [
                table_gather(
                    [(b, own_rows[c : c + 1, b * BLOCK : (b + 1) * BLOCK]) for b in range(own_blocks)],
                    *edge_index(tile),
                )
                for c in range(count)
            ]
            for tile in range(own_blocks)
        ]

    def edges(begun):
        for tile in range(own_blocks):
            at = slice(tile * BLOCK, (tile + 1) * BLOCK)
            local, chunk = edge_index(tile)
            picked = [
                table_gather(
                    [(own_blocks + side, rim_in[0, side, c : c + 1, :]) for side in range(2)],
                    local,
                    chunk,
                    value,
                )
                for c, value in enumerate(begun[tile])
            ]
            ox, oy, oz = (own_rows[c : c + 1, at] - picked[c] for c in range(3))
            dist_sq = ox * ox + oy * oy + oz * oz + SMOOTH
            yield at, (ox, oy, oz), dist_sq, picked[-1]

    centre = lax.broadcasted_iota(jnp.int32, (basis, rows), 0).astype(F32) * SPACING

    def waves():
        for q in range(groups):
            parts = []
            for j in range(pack):
                away = jnp.broadcast_to(geometry[0, q * pack + j : q * pack + j + 1, 0:rows], (basis, rows))
                away = away - centre
                parts.append(jnp.exp(-(away * away)))
            turned = jnp.concatenate(parts, axis=0).T
            wave[q * rows : (q + 1) * rows, :] = turned.astype(BF16)

    def radial_net(layer):
        half = groups // 2
        spans = [range(half), range(half, groups)]
        for step in range(3):
            for part, span in enumerate(spans):
                at = slice(span[0] * rows, (span[-1] + 1) * rows)
                if step == 0:
                    source, weight = wave[at, :], wide_in[layer]
                else:
                    source, weight = stage[step - 1, at, :], wide_mid[layer, step - 1]
                h = silu_of_half(jnp.dot(source, weight, preferred_element_type=F32)).astype(BF16)
                if step < 2:
                    stage[step, at, :] = h
                else:
                    for i, q in enumerate(span):
                        third[layer, :, q] = h[i * rows : (i + 1) * rows].reshape(
                            strips, STRIP, channels
                        )

    def edge_part(layer, j):
        edge_weight[j] = jnp.dot(
            third[layer].reshape(groups * rows, channels),
            wide_out[layer, j],
            preferred_element_type=F32,
        ).reshape(strips, groups, STRIP, channels)

    def own_part(layer, beside):
        for j in range(pack):
            beside(j)
            if layer or j >= EARLY:
                edge_part(layer, j)
            gather_part(layer, j, 0, rows)

    def rim_part(layer):
        for j in range(pack):
            gather_part(layer, j, rows, 2 * rim)

    def gather_part(layer, j, first, count):
        source = jnp.dot(
            hot[j, :, :, :, first : first + count].reshape(groups * rows, count),
            tables[layer, first : first + count],
            preferred_element_type=F32,
        )
        product = edge_weight[j] * source.reshape(strips, groups, STRIP, channels)
        total = jnp.sum(product, axis=1)
        if first or j:
            total = acc[...] + total
        acc[...] = total

    @pl.when(g == 0)
    def _():
        begun = own_edges(3)
        arrive(rim_copy, 0)
        start(lift_copy, 0)
        for at, _, dist_sq, _ in edges(begun):
            geometry[0, :, at] = jnp.sqrt(dist_sq)
        waves()
        radial_net(0)

    @pl.when(g == 1)
    def _():
        begun = own_edges(4)
        arrive(rim_copy, 0)
        start(flat_copy, 0)
        start(far_copy, 0, 2)
        start(list_copy, 0)
        for at, offset, dist_sq, source_charge in edges(begun):
            w = lax.rsqrt(dist_sq)
            w2 = w * w
            w3 = w2 * w
            s = source_charge * w3
            for c in range(3):
                geometry[c, :, at] = offset[c]
                extra = jnp.sum(offset[c] * s, axis=0, keepdims=True)
                pairs[c : c + 1, at] = extra
            geometry[3, :, at] = w3
            geometry[4, :, at] = 3.0 * (w3 * w2)

    pltpu.make_async_copy(everyone, everyone, all_recv).wait()
    for l in range(listed):
        tile = everyone[blocks[l]]
        near_rows[:, l * BLOCK : (l + 1) * BLOCK] = tile
        near_cols[l * BLOCK : (l + 1) * BLOCK, :] = jnp.concatenate(
            [tile, jnp.zeros_like(tile)], axis=0
        ).T

    def lent_near():
        names = [
            [jnp.broadcast_to(rim_in[0, side, 3:4, l : l + 1], (4, BLOCK)) for l in range(listed)]
            for side in range(2)
        ]

        def step(b, found):
            tile = everyone[b]
            return tuple(
                tuple(
                    jnp.where(names[side][l] == b.astype(F32), tile, found[side][l])
                    for l in range(listed)
                )
                for side in range(2)
            )

        blank = jnp.zeros((4, BLOCK), F32)
        found = lax.fori_loop(
            0, n * own_blocks, step, ((blank,) * listed,) * 2, unroll=max(8, min(32, n * own_blocks))
        )
        for side in range(2):
            for l in range(listed):
                lent_cols[side, l * BLOCK : (l + 1) * BLOCK, :] = jnp.concatenate(
                    [found[side][l], blank], axis=0
                ).T

    @pl.when(g == 0)
    def _():
        for number in late[spread_needs:]:
            load(number).wait()

        def strength_of(fields):
            fx, fy, fz = fields
            return jnp.sqrt(1.0 + fx * fx + fy * fy + fz * fz)

        def column_of(strength):
            return jnp.broadcast_to(strength, (8, strength.shape[1])).T[:, 0:1]

        def embed(column, at):
            return (features[at].astype(F32) + column * field_gain[...]).astype(BF16)

        def lent_field(side):
            return field(rim_in[0, side], lent_cols.at[side], listed * BLOCK)

        for j in range(EARLY):
            edge_part(0, j)
        strength = strength_of(field(own, near_cols, listed * BLOCK))
        site_result[2:3, :] = strength
        hidden_ref[...] = embed(column_of(strength), slice(0, rows))
        tables[0, 0:rows] = jnp.dot(
            hidden_ref[...], node_in[0], preferred_element_type=F32
        ).astype(BF16)
        fields, columns = [], []

        def lent_lift(j):
            if j == 0:
                lent_near()
            if j < 2:
                fields.append(lent_field(j))
            if j == 2:
                columns.extend(column_of(strength_of(part)) for part in fields)
            if j == pack - 1:
                arrive(lift_copy, 0)
                ends = (p > 0, p < n - 1)
                for side in range(2):
                    at = slice(rows + side * rim, rows + (side + 1) * rim)
                    hidden = embed(columns[side], at)
                    lifted = jnp.dot(hidden, node_in[0], preferred_element_type=F32)
                    tables[0, at] = jnp.where(ends[side], lifted, 0.0).astype(BF16)

        def lift(layer):
            lifted = jnp.dot(
                hidden_ref[...], node_in[layer], preferred_element_type=F32
            ).astype(BF16)
            lend(layer, lifted)
            start(lift_copy, layer)
            tables[layer, 0:rows] = lifted

        for layer in range(layers):
            def beside(j, layer=layer):
                if layer == layers - 1:
                    term_geometry(False, j, pack)

            if layer:
                lift(layer)
                radial_net(layer)
            own_part(layer, beside if layer else lent_lift)
            if layer:
                arrive(lift_copy, layer)
            rim_part(layer)
            message = (acc[...].reshape(rows, channels) * (1.0 / slots)).astype(BF16)
            update = silu_of_half(
                0.5 * jnp.dot(message, node_out[layer], preferred_element_type=F32)
            )
            hidden_ref[...] = (hidden_ref[...].astype(F32) + update).astype(BF16)

        across = (((1,), (1,)), ((), ()))
        extra_cols[:, 0:2] = lax.dot_general(
            hidden_ref[...], readout[...], across, preferred_element_type=F32
        )
        site_result[0:2, :] = lax.dot_general(
            readout[...], hidden_ref[...], across, preferred_element_type=F32
        )
        send_terms(False)
        for layer in range(layers):
            gone(lift_copy, layer)

    @pl.when(g == 1)
    def _():
        out = field(own, near_cols, listed * BLOCK)
        for c in range(3):
            outside[c : c + 1, :] = out[c]
        gain = polar[...]
        outside[...] = outside[...] + pairs[...]
        dipole = [gain * outside[c : c + 1, :] for c in range(3)]

        def induced(at, index, pieces, begun=(None, None, None)):
            local = index & (BLOCK - 1)
            chunk = lax.shift_right_logical(index, 7)
            d = [table_gather(pieces(c), local, chunk, begun[c]) for c in range(3)]
            r = [geometry[c, :, at] for c in range(3)]
            w3 = geometry[3, :, at]
            s = (r[0] * d[0] + r[1] * d[1] + r[2] * d[2]) * geometry[4, :, at]
            return [jnp.sum(r[c] * s - d[c] * w3, axis=0, keepdims=True) for c in range(3)]

        def own_pieces(c, values):
            return [(b, values[c][:, b * BLOCK : (b + 1) * BLOCK]) for b in range(own_blocks)]

        def own_sweep(values, rims, begun):
            fresh = [[], [], []]
            for tile in range(own_blocks):
                at = slice(tile * BLOCK, (tile + 1) * BLOCK)

                def pieces(c):
                    ends = [(own_blocks + side, rims(side, c)) for side in range(2)]
                    return ends if begun else own_pieces(c, values) + ends

                totals = induced(
                    at, neighbours[:, at], pieces, begun[tile] if begun else (None, None, None)
                )
                for c in range(3):
                    fresh[c].append(gain[:, at] * (outside[c : c + 1, at] + totals[c]))
            return [jnp.concatenate(f, axis=1) for f in fresh]

        for sweep in range(ROUNDS):
            step = 1 + sweep
            values = jnp.concatenate(dipole + [jnp.zeros((1, rows), F32)], axis=0)
            fill_rims(step, values)
            start(rim_copy, step)
            start(far_copy, step, 2)
            flat_out[step] = values
            start(flat_copy, step)
            if sweep == 0:
                fill(fixed_out, jnp.concatenate([outside[...], gain], axis=0))
                start(fixed_copy, 0)
            begun = []
            for tile in range(own_blocks):
                index = neighbours[:, tile * BLOCK : (tile + 1) * BLOCK]
                local = index & (BLOCK - 1)
                chunk = lax.shift_right_logical(index, 7)
                begun.append([table_gather(own_pieces(c, dipole), local, chunk) for c in range(3)])
            if sweep == 0:
                lent_geometry()
                term_geometry(True, 0, 1)
            arrive(rim_copy, step)
            arrive(far_copy, step, 2)
            arrive(flat_copy, step)
            if sweep == 0:
                arrive(fixed_copy, 0)
            middle = own_sweep(
                dipole, lambda side, c: rim_in[step, side, c : c + 1, :], begun
            )
            lent_middle = []
            for side in range(2):
                at = slice(rows + side * rim, rows + (side + 1) * rim)
                totals = induced(
                    at,
                    lists_in[side],
                    lambda c: lent_pieces(
                        side, c, flat_in[step, side], rim_out[step, 1 - side], far_in[step, side]
                    ),
                )
                lent_middle.append([
                    fixed_in[side, 3:4, :] * (fixed_in[side, c : c + 1, :] + totals[c])
                    for c in range(3)
                ])
            dipole = own_sweep(middle, lambda side, c: lent_middle[side][c], None)
        for c in range(3):
            site_result[c : c + 1, :] = dipole[c]
        stacked = jnp.concatenate(dipole + [jnp.zeros((5, rows), F32)], axis=0)
        extra_cols[...] = stacked.T
        send_terms(True)
        for step in range(1 + ROUNDS):
            if step:
                gone(rim_copy, step)
            gone(far_copy, step, 2)
            gone(flat_copy, step)
        gone(list_copy, 0)
        gone(fixed_copy, 0)

    @pl.loop(0, n, unroll=min(n, 16))
    def _(q):
        for b in range(own_blocks):
            total = jnp.zeros((3, BLOCK), F32)
            for l in range(listed):
                total = total + jnp.where(
                    blocks[l] == q * own_blocks + b, terms[:, l * BLOCK : (l + 1) * BLOCK], 0.0
                )
            term_out[q, b * 3 : (b + 1) * 3, :] = total

    def term_copy(i):
        return pltpu.make_async_remote_copy(
            src_ref=term_out.at[peer(i)],
            dst_ref=term_in.at[p],
            send_sem=term_send,
            recv_sem=term_recv,
            device_id=place(other, peer(i)),
            device_id_type=MESH,
        )

    @pl.loop(0, n, unroll=4)
    def _(i):
        term_copy(i).start()

    gone(rim_copy, 0)
    pltpu.make_async_copy(everyone, everyone, all_send).wait()
    pltpu.make_async_copy(term_in, term_in, term_recv).wait()

    total = jnp.sum(term_in[...], axis=0)
    for b in range(own_blocks):
        response[:, b * BLOCK : (b + 1) * BLOCK] = total[b * 3 : (b + 1) * 3, :]
    pltpu.make_async_copy(term_in, term_in, term_send).wait()


def local(n_dom, n_sub, *args):
    (
        positions,
        charges,
        polar,
        features,
        neighbours,
        send_rows,
        blocks,
        radial_in,
        radial_mid,
        radial_out,
        node_in,
        node_out,
        field_gain,
        readout,
    ) = args
    n = n_dom * n_sub
    rows = positions.shape[1]
    own_blocks = rows // BLOCK
    slots = neighbours.shape[1]
    listed = blocks.shape[0]
    layers, basis, radial = radial_in.shape
    channels = features.shape[1]
    rim = send_rows.shape[1]
    pack = channels // radial
    dma = pltpu.SemaphoreType.DMA
    operands = (
        positions,
        charges.reshape(1, -1),
        polar.reshape(1, -1),
        features,
        neighbours.T,
        send_rows,
        blocks,
        radial_in,
        radial_mid,
        radial_out,
        node_in,
        node_out,
        field_gain.reshape(1, -1),
        readout.T,
    )
    spaces = [pltpu.VMEM] * INPUTS
    spaces[6] = pltpu.SMEM
    shapes = [a.shape for a in operands]
    shapes[3] = (rows + 2 * rim, channels)
    both = pl.pallas_call(
        functools.partial(kernel, n_dom, n_sub),
        out_shape=jax.ShapeDtypeStruct((2, 3, rows), F32),
        in_specs=[pl.BlockSpec(memory_space=pl.ANY)] * INPUTS,
        out_specs=pl.BlockSpec(memory_space=pltpu.VMEM),
        scratch_shapes=[space(shape, a.dtype) for space, shape, a in zip(spaces, shapes, operands)]
        + [
            dma((INPUTS,)),
            pltpu.VMEM((own_blocks, 4, BLOCK), F32),
            pltpu.VMEM((n * own_blocks, 4, BLOCK), F32),
            pltpu.VMEM((4, listed * BLOCK), F32),
            pltpu.VMEM((listed * BLOCK, 8), F32),
            pltpu.VMEM((8, rows), F32),
            pltpu.VMEM((rows, 8), F32),
            pltpu.VMEM((rows, 8), F32),
            pltpu.VMEM((1 + ROUNDS, 2, 4, rim), F32),
            pltpu.VMEM((1 + ROUNDS, 2, 4, rim), F32),
            pltpu.VMEM((1 + ROUNDS, 4, rows), F32),
            pltpu.VMEM((1 + ROUNDS, 2, 4, rows), F32),
            pltpu.VMEM((1 + ROUNDS, 2, 4, rim), F32),
            pltpu.VMEM((2, slots, rim), jnp.int32),
            pltpu.VMEM((2, slots, rim), jnp.int32),
            pltpu.VMEM((2, 4, rim), F32),
            pltpu.VMEM((2, 4, rim), F32),
            pltpu.VMEM((5, slots, rows + 2 * rim), F32),
            pltpu.VMEM((pack, rows // STRIP, slots // pack, STRIP, rows + 2 * rim), BF16),
            pltpu.VMEM((2 * rim, rows), BF16),
            pltpu.VMEM((slots // pack * rows, pack * basis), BF16),
            pltpu.VMEM((2, slots // pack * rows, channels), BF16),
            pltpu.VMEM((layers, rows // STRIP, slots // pack, STRIP, channels), BF16),
            pltpu.VMEM((pack, rows // STRIP, slots // pack, STRIP, channels), F32),
            pltpu.VMEM((layers, pack * basis, channels), BF16),
            pltpu.VMEM((layers, 2, channels, channels), BF16),
            pltpu.VMEM((layers, pack, channels, channels), BF16),
            pltpu.VMEM((layers, rows + 2 * rim, channels), BF16),
            pltpu.VMEM((layers, 2, rim, channels), BF16),
            pltpu.VMEM((2, listed * BLOCK, 8), F32),
            pltpu.VMEM((5, rows, listed * BLOCK), F32),
            pltpu.VMEM((rows, channels), BF16),
            pltpu.VMEM((rows // STRIP, STRIP, channels), F32),
            pltpu.VMEM((3, rows), F32),
            pltpu.VMEM((3, rows), F32),
            pltpu.VMEM((3, listed * BLOCK), F32),
            pltpu.VMEM((n, own_blocks * 3, BLOCK), F32),
            pltpu.VMEM((n, own_blocks * 3, BLOCK), F32),
            dma(()),
            dma(()),
            dma((1 + ROUNDS, 2)),
            dma((1 + ROUNDS, 2)),
            dma((layers, 2)),
            dma((layers, 2)),
            dma(()),
            dma(()),
            dma((1 + ROUNDS, 2)),
            dma((1 + ROUNDS, 2)),
            dma((1 + ROUNDS, 2)),
            dma((1 + ROUNDS, 2)),
            dma((1, 2)),
            dma((1, 2)),
            dma((1, 2)),
            dma((1, 2)),
        ],
        compiler_params=pltpu.CompilerParams(
            collective_id=0, has_side_effects=True, vmem_limit_bytes=40 * 2**20
        ),
    )(*(pltpu.with_memory_space_constraint(a, pltpu.HBM) for a in operands))
    return both[0], both[1]


def solution(mesh):
    sites = ("grp", "dom", "sub")
    in_specs = (
        P(None, sites),
        P(sites),
        P(sites),
        P(sites, None),
        P(sites, None),
        P(None, sites),
        P(sites),
    ) + (P(),) * 7
    out_specs = (P(None, sites), P(None, sites))
    body = functools.partial(local, mesh.shape["dom"], mesh.shape["sub"])
    return jax.shard_map(body, mesh=mesh, in_specs=in_specs, out_specs=out_specs, check_vma=False)
```

```python
import functools

import jax
import jax.numpy as jnp
from jax import lax
from jax.experimental import pallas as pl
from jax.experimental.pallas import tpu as pltpu
from jax.sharding import PartitionSpec as P

SWEEPS = 4
ROUNDS = SWEEPS // 2
BLOCK = 128
SMOOTH = 1.0
SPACING = 0.75
MESH = pl.DeviceIdType.MESH
INPUTS = 14
STRIP = 16
EARLY = 2
F32 = jnp.float32
BF16 = jnp.bfloat16


def silu_of_half(half):
    return half + half * jnp.tanh(half)


def lane_pick(rows, index):
    shape = index.shape
    return jnp.take_along_axis(
        jnp.broadcast_to(rows, shape), index, axis=1, mode="promise_in_bounds"
    )


def table_gather(pieces, local, chunk, total=None):
    if total is None:
        total = jnp.zeros(local.shape, pieces[0][1].dtype)
    for number, rows in pieces:
        total = jnp.where(chunk == number, lane_pick(rows, local), total)
    return total


def kernel(
    n_dom,
    n_sub,
    *refs,
):
    sources = refs[:INPUTS]
    (
    both,
    positions,
    charges,
    polar,
    features,
    neighbours,
    send_rows,
    blocks,
    radial_in,
    radial_mid,
    radial_out,
    node_in,
    node_out,
    field_gain,
    readout,
    in_sem,
    packet,
    everyone,
    near_rows,
    near_cols,
    own_rows,
    own_cols,
    extra_cols,
    rim_out,
    rim_in,
    flat_out,
    flat_in,
    far_in,
    lists_out,
    lists_in,
    fixed_out,
    fixed_in,
    geometry,
    hot,
    pick,
    wave,
    stage,
    third,
    edge_weight,
    wide_in,
    wide_mid,
    wide_out,
    tables,
    lent,
    lent_cols,
    reach,
    hidden_ref,
    acc,
    outside,
    pairs,
    terms,
    term_out,
    term_in,
    all_send,
    all_recv,
    rim_send,
    rim_recv,
    lift_send,
    lift_recv,
    term_send,
    term_recv,
    flat_send,
    flat_recv,
    far_send,
    far_recv,
    list_send,
    list_recv,
    fixed_send,
    fixed_recv,
    ) = refs[INPUTS:]
    g = lax.axis_index("grp")
    p = lax.axis_index("dom") * n_sub + lax.axis_index("sub")
    site_result, response = both.at[0], both.at[1]
    n = n_dom * n_sub
    rows = positions.shape[1]
    own_blocks = rows // BLOCK
    slots = neighbours.shape[0]
    listed = blocks.shape[0]
    layers, basis, radial = radial_in.shape
    channels = features.shape[1]
    rim = send_rows.shape[1]
    pack = channels // radial
    groups = slots // pack
    strips = rows // STRIP
    other = 1 - g
    held = (
        positions,
        charges,
        polar,
        features,
        neighbours,
        send_rows,
        blocks,
        radial_in,
        radial_mid,
        radial_out,
        node_in,
        node_out,
        field_gain,
        readout,
    )
    early = (0, 1, 2, 4, 5, 6)
    late = (7, 8, 9, 3, 10, 11, 12, 13)
    spread_needs = 4

    def load(number):
        target = held[number]
        if number == 3:
            target = target.at[pl.ds(0, rows)]
        return pltpu.make_async_copy(sources[number], target, in_sem.at[number])

    for number in early:
        load(number).start()

    def place(group, q):
        return (group, lax.div(q, n_sub), lax.rem(q, n_sub))

    def peer(i):
        if n % 4:
            return lax.rem(p + i, n)
        quarter = n // 4
        second = lax.div(2 * p, n)
        turn = lax.div(i, quarter)
        far = second * turn + (1 - second) * (3 - turn)
        return far * quarter + lax.rem(p + i, quarter)

    barrier = pltpu.get_barrier_semaphore()

    @pl.loop(0, n)
    def _(i):
        pl.semaphore_signal(barrier, inc=1, device_id=place(other, peer(i)), device_id_type=MESH)

    @pl.when(p > 0)
    def _():
        pl.semaphore_signal(barrier, inc=1, device_id=place(g, p - 1), device_id_type=MESH)

    @pl.when(p < n - 1)
    def _():
        pl.semaphore_signal(barrier, inc=1, device_id=place(g, p + 1), device_id_type=MESH)

    @pl.when(p > 1)
    def _():
        pl.semaphore_signal(barrier, inc=1, device_id=place(g, p - 2), device_id_type=MESH)

    @pl.when(p < n - 2)
    def _():
        pl.semaphore_signal(barrier, inc=1, device_id=place(g, p + 2), device_id_type=MESH)

    @pl.when(g == 0)
    def _():
        for number in late:
            load(number).start()

    own_rows[...] = jnp.zeros_like(own_rows)
    for number in early:
        load(number).wait()
    own_rows[0:3, :] = positions[...]
    own_rows[3:4, :] = charges[...]
    own = own_rows[...]
    for b in range(own_blocks):
        packet[b] = own[0:4, b * BLOCK : (b + 1) * BLOCK]

    def fill(target, values):
        for side in range(2):
            index = jnp.broadcast_to(send_rows[side : side + 1, :], (values.shape[0], rim))
            target[side] = table_gather(
                [(c, values[:, c * BLOCK : (c + 1) * BLOCK]) for c in range(own_blocks)],
                index & (BLOCK - 1),
                lax.shift_right_logical(index, 7),
            )

    def fill_rims(step, values):
        fill(rim_out.at[step], values)

    def side_copy(src, dst, send, recv, step, side, q):
        return pltpu.make_async_remote_copy(
            src_ref=src,
            dst_ref=dst,
            send_sem=send.at[side],
            recv_sem=recv.at[step, side],
            device_id=place(g, q),
            device_id_type=MESH,
        )

    def rim_copy(step, side, q):
        return side_copy(
            rim_out.at[step, side], rim_in.at[step, side], rim_send, rim_recv, step, side, q
        )

    def lift_copy(layer, side, q):
        target = tables.at[layer] if layer else features
        return side_copy(
            lent.at[layer, side],
            target.at[pl.ds(rows + side * rim, rim)],
            lift_send,
            lift_recv,
            layer,
            side,
            q,
        )

    def flat_copy(step, side, q):
        return side_copy(
            flat_out.at[step], flat_in.at[step, side], flat_send, flat_recv, step, side, q
        )

    def far_copy(step, side, q):
        return side_copy(
            rim_out.at[step, side], far_in.at[step, side], far_send, far_recv, step, side, q
        )

    def list_copy(step, side, q):
        return side_copy(
            lists_out.at[side], lists_in.at[side], list_send, list_recv, step, side, q
        )

    def fixed_copy(step, side, q):
        return side_copy(
            fixed_out.at[side], fixed_in.at[side], fixed_send, fixed_recv, step, side, q
        )

    def start(copy, step, away=1):
        @pl.when(p < n - away)
        def _():
            copy(step, 0, p + away).start()

        @pl.when(p > away - 1)
        def _():
            copy(step, 1, p - away).start()

    def arrive(copy, step, away=1):
        @pl.when(p > away - 1)
        def _():
            copy(step, 0, p - away).wait_recv()

        @pl.when(p < n - away)
        def _():
            copy(step, 1, p + away).wait_recv()

    def gone(copy, step, away=1):
        @pl.when(p < n - away)
        def _():
            copy(step, 0, p + away).wait_send()

        @pl.when(p > away - 1)
        def _():
            copy(step, 1, p - away).wait_send()

    def mark_slots(span):
        width = rows + 2 * rim
        lane = lax.broadcasted_iota(jnp.int32, (rows, width), 1).astype(jnp.int16)
        listing = jnp.concatenate(
            [neighbours[...].astype(F32), jnp.zeros((BLOCK - slots, rows), F32)], axis=0
        ).T.astype(jnp.int32)
        one, none = jnp.ones((rows, width), BF16), jnp.zeros((rows, width), BF16)
        for k in span:
            entry = jnp.broadcast_to(listing[:, k : k + 1], (rows, BLOCK)).astype(jnp.int16)
            entry = jnp.concatenate([entry] * (width // BLOCK), axis=1)
            mark = jnp.where(entry == lane, one, none)
            hot[k % pack, :, k // pack] = mark.reshape(strips, STRIP, width)

    def mark_lent():
        lists = jnp.concatenate(
            [send_rows[...].astype(F32), jnp.zeros((6, rim), F32)], axis=0
        ).T.astype(jnp.int32)
        site = lax.broadcasted_iota(jnp.int32, (rim, rows), 1)
        for side in range(2):
            pick[side * rim : (side + 1) * rim, :] = jnp.where(
                lists[:, side : side + 1] == site, 1.0, 0.0
            ).astype(BF16)

    def spread():
        for number in late[:spread_needs]:
            load(number).wait()
        spread_r = (
            lax.broadcasted_iota(jnp.int32, (channels, radial), 0) % radial
            == lax.broadcasted_iota(jnp.int32, (channels, radial), 1)
        ).astype(F32).astype(BF16)
        spread_c = (
            lax.broadcasted_iota(jnp.int32, (radial, channels), 1) % radial
            == lax.broadcasted_iota(jnp.int32, (radial, channels), 0)
        ).astype(F32).astype(BF16)
        same_in = (
            lax.broadcasted_iota(jnp.int32, (pack * basis, channels), 0) // basis
            == lax.broadcasted_iota(jnp.int32, (pack * basis, channels), 1) // radial
        )
        same_mid = (
            lax.broadcasted_iota(jnp.int32, (channels, channels), 0) // radial
            == lax.broadcasted_iota(jnp.int32, (channels, channels), 1) // radial
        )
        for layer in range(layers):
            flat = jnp.dot(radial_in[layer], spread_c, preferred_element_type=F32)
            wide_in[layer] = jnp.where(
                same_in, jnp.concatenate([0.5 * flat] * pack, axis=0), 0.0
            ).astype(BF16)
            for m in range(2):
                flat = jnp.dot(
                    jnp.dot(spread_r, radial_mid[layer, m], preferred_element_type=F32).astype(
                        BF16
                    ),
                    spread_c,
                    preferred_element_type=F32,
                )
                wide_mid[layer, m] = jnp.where(same_mid, 0.5 * flat, 0.0).astype(BF16)
            for j in range(pack):
                wide_out[layer, j] = jnp.zeros((channels, channels), BF16)
                wide_out[layer, j, j * radial : (j + 1) * radial, :] = radial_out[layer]

    def lend(layer, values):
        picked = jnp.dot(pick[...], values, preferred_element_type=F32).astype(BF16)
        lent[layer] = picked.reshape(2, rim, channels)

    fill_rims(0, own[0:4])

    @pl.when(g == 0)
    def _():
        spot = lax.broadcasted_iota(jnp.int32, (1, rim), 1)
        names = jnp.zeros((1, rim), F32)
        for l in range(listed):
            names = jnp.where(spot == l, blocks[l].astype(F32), names)
        for side in range(2):
            rim_out[0, side, 3:4, :] = names

    @pl.when(p == 0)
    def _():
        for step in range(1 + ROUNDS):
            rim_in[step, 0] = jnp.zeros((4, rim), F32)
        features[rows : rows + rim] = jnp.zeros((rim, channels), BF16)
        for layer in range(1, layers):
            tables[layer, rows : rows + rim] = jnp.zeros((rim, channels), BF16)

    @pl.when(p == n - 1)
    def _():
        for step in range(1 + ROUNDS):
            rim_in[step, 1] = jnp.zeros((4, rim), F32)
        features[rows + rim :] = jnp.zeros((rim, channels), BF16)
        for layer in range(1, layers):
            tables[layer, rows + rim :] = jnp.zeros((rim, channels), BF16)

    def clear(side, away):
        for step in range(1 + ROUNDS):
            far_in[step, side] = jnp.zeros((4, rim), F32)
            if away == 1:
                flat_in[step, side] = jnp.zeros((4, rows), F32)
        if away == 1:
            lists_in[side] = jnp.zeros((slots, rim), jnp.int32)
            fixed_in[side] = jnp.zeros((4, rim), F32)

    @pl.when(g == 1)
    def _():
        flat_out[0] = own[0:4]
        fill(lists_out, neighbours[...])
        for side, ends in enumerate(((0, 1), (n - 1, n - 2))):
            pl.when(p == ends[0])(functools.partial(clear, side, 1))
            pl.when(p == ends[1])(functools.partial(clear, side, 2))

    @pl.when(g == 0)
    def _():
        mark_slots(range(slots // 2))

    sides = [p > 0, p < n - 1, p > 1, p < n - 2]
    pl.semaphore_wait(barrier, n + sum(side.astype(jnp.int32) for side in sides))

    def packet_copy(i):
        return pltpu.make_async_remote_copy(
            src_ref=packet,
            dst_ref=everyone.at[pl.ds(p * own_blocks, own_blocks)],
            send_sem=all_send,
            recv_sem=all_recv,
            device_id=place(other, peer(i)),
            device_id_type=MESH,
        )

    start(rim_copy, 0)

    @pl.loop(0, n, unroll=4)
    def _(i):
        packet_copy(i).start()

    @pl.when(g == 0)
    def _():
        mark_lent()
        spread()
        mark_slots(range(slots // 2, slots))
        lend(0, features[0:rows])

    own_cols[...] = own.T

    def field(targets, source_cols, count):
        x, y, z = (targets[c : c + 1, :] for c in range(3))

        def step(i, sums):
            source = source_cols[pl.ds(pl.multiple_of(i * 8, 8), 8), :]
            rx = x - source[:, 0:1]
            ry = y - source[:, 1:2]
            rz = z - source[:, 2:3]
            w = lax.rsqrt(rx * rx + ry * ry + rz * rz + SMOOTH)
            s = source[:, 3:4] * (w * w * w)
            return (sums[0] + rx * s, sums[1] + ry * s, sums[2] + rz * s)

        zero = jnp.zeros((8, targets.shape[1]), F32)
        sums = lax.fori_loop(0, count // 8, step, (zero, zero, zero), unroll=True)
        return [jnp.sum(s, axis=0, keepdims=True) for s in sums]

    def term_geometry(dipole, part, parts):
        x, y, z = (near_rows[c : c + 1, :] for c in range(3))
        for i in range(part * rows // 8 // parts, (part + 1) * rows // 8 // parts):
            at = slice(i * 8, i * 8 + 8)
            source = own_cols[at, :]
            r = (x - source[:, 0:1], y - source[:, 1:2], z - source[:, 2:3])
            w = lax.rsqrt(r[0] * r[0] + r[1] * r[1] + r[2] * r[2] + SMOOTH)
            w2 = w * w
            w3 = w2 * w
            for c in range(3):
                reach[c, at, :] = r[c] if dipole else r[c] * w3
            if dipole:
                reach[3, at, :] = w3
                reach[4, at, :] = 3.0 * (w3 * w2)

    def send_terms(dipole):
        def step(i, sums):
            at = pl.ds(pl.multiple_of(i * 8, 8), 8)
            d = extra_cols[at, :]
            r = [reach[c, at, :] for c in range(3)]
            if not dipole:
                return tuple(sums[c] + r[c] * d[:, 0:1] for c in range(3))
            w3 = reach[3, at, :]
            d = [d[:, c : c + 1] for c in range(3)]
            s = (r[0] * d[0] + r[1] * d[1] + r[2] * d[2]) * reach[4, at, :]
            return tuple(sums[c] + (r[c] * s - d[c] * w3) for c in range(3))

        zero = jnp.zeros((8, listed * BLOCK), F32)
        sums = lax.fori_loop(0, rows // 8, step, (zero, zero, zero), unroll=True)
        for c in range(3):
            terms[c : c + 1, :] = jnp.sum(sums[c], axis=0, keepdims=True)

    def lent_pieces(side, c, flat, mine, far):
        flat, mine, far = (rows_[c : c + 1, :] for rows_ in (flat, mine, far))
        rims = (far, mine) if side == 0 else (mine, far)
        return [(b, flat[:, b * BLOCK : (b + 1) * BLOCK]) for b in range(own_blocks)] + [
            (own_blocks + i, rims[i]) for i in range(2)
        ]

    def lent_geometry():
        arrive(flat_copy, 0)
        arrive(far_copy, 0, 2)
        arrive(list_copy, 0)
        for side in range(2):
            at = slice(rows + side * rim, rows + (side + 1) * rim)
            index = lists_in[side]
            local = index & (BLOCK - 1)
            chunk = lax.shift_right_logical(index, 7)
            offset = [
                rim_in[0, side, c : c + 1, :]
                - table_gather(
                    lent_pieces(side, c, flat_in[0, side], rim_out[0, 1 - side], far_in[0, side]),
                    local,
                    chunk,
                )
                for c in range(3)
            ]
            w = lax.rsqrt(
                offset[0] * offset[0] + offset[1] * offset[1] + offset[2] * offset[2] + SMOOTH
            )
            w2 = w * w
            w3 = w2 * w
            for c in range(3):
                geometry[c, :, at] = offset[c]
            geometry[3, :, at] = w3
            geometry[4, :, at] = 3.0 * (w3 * w2)

    def edge_index(tile):
        index = neighbours[:, tile * BLOCK : (tile + 1) * BLOCK]
        return index & (BLOCK - 1), lax.shift_right_logical(index, 7)

    def own_edges(count):
        return [
            [
                table_gather(
                    [(b, own_rows[c : c + 1, b * BLOCK : (b + 1) * BLOCK]) for b in range(own_blocks)],
                    *edge_index(tile),
                )
                for c in range(count)
            ]
            for tile in range(own_blocks)
        ]

    def edges(begun):
        for tile in range(own_blocks):
            at = slice(tile * BLOCK, (tile + 1) * BLOCK)
            local, chunk = edge_index(tile)
            picked = [
                table_gather(
                    [(own_blocks + side, rim_in[0, side, c : c + 1, :]) for side in range(2)],
                    local,
                    chunk,
                    value,
                )
                for c, value in enumerate(begun[tile])
            ]
            ox, oy, oz = (own_rows[c : c + 1, at] - picked[c] for c in range(3))
            dist_sq = ox * ox + oy * oy + oz * oz + SMOOTH
            yield at, (ox, oy, oz), dist_sq, picked[-1]

    centre = lax.broadcasted_iota(jnp.int32, (basis, rows), 0).astype(F32) * SPACING

    def waves():
        for q in range(groups):
            parts = []
            for j in range(pack):
                away = jnp.broadcast_to(geometry[0, q * pack + j : q * pack + j + 1, 0:rows], (basis, rows))
                away = away - centre
                parts.append(jnp.exp(-(away * away)))
            turned = jnp.concatenate(parts, axis=0).T
            wave[q * rows : (q + 1) * rows, :] = turned.astype(BF16)

    def radial_net(layer):
        half = groups // 2
        spans = [range(half), range(half, groups)]
        for step in range(3):
            for part, span in enumerate(spans):
                at = slice(span[0] * rows, (span[-1] + 1) * rows)
                if step == 0:
                    source, weight = wave[at, :], wide_in[layer]
                else:
                    source, weight = stage[step - 1, at, :], wide_mid[layer, step - 1]
                h = silu_of_half(jnp.dot(source, weight, preferred_element_type=F32)).astype(BF16)
                if step < 2:
                    stage[step, at, :] = h
                else:
                    for i, q in enumerate(span):
                        third[layer, :, q] = h[i * rows : (i + 1) * rows].reshape(
                            strips, STRIP, channels
                        )

    def edge_part(layer, j):
        edge_weight[j] = jnp.dot(
            third[layer].reshape(groups * rows, channels),
            wide_out[layer, j],
            preferred_element_type=F32,
        ).reshape(strips, groups, STRIP, channels)

    def own_part(layer, beside):
        for j in range(pack):
            beside(j)
            if layer or j >= EARLY:
                edge_part(layer, j)
            gather_part(layer, j, 0, rows)

    def rim_part(layer):
        for j in range(pack):
            gather_part(layer, j, rows, 2 * rim)

    def gather_part(layer, j, first, count):
        source = jnp.dot(
            hot[j, :, :, :, first : first + count].reshape(groups * rows, count),
            tables[layer, first : first + count],
            preferred_element_type=F32,
        )
        product = edge_weight[j] * source.reshape(strips, groups, STRIP, channels)
        total = jnp.sum(product, axis=1)
        if first or j:
            total = acc[...] + total
        acc[...] = total

    @pl.when(g == 0)
    def _():
        begun = own_edges(3)
        arrive(rim_copy, 0)
        start(lift_copy, 0)
        for at, _, dist_sq, _ in edges(begun):
            geometry[0, :, at] = jnp.sqrt(dist_sq)
        waves()
        radial_net(0)

    @pl.when(g == 1)
    def _():
        begun = own_edges(4)
        arrive(rim_copy, 0)
        start(flat_copy, 0)
        start(far_copy, 0, 2)
        start(list_copy, 0)
        for at, offset, dist_sq, source_charge in edges(begun):
            w = lax.rsqrt(dist_sq)
            w2 = w * w
            w3 = w2 * w
            s = source_charge * w3
            for c in range(3):
                geometry[c, :, at] = offset[c]
                extra = jnp.sum(offset[c] * s, axis=0, keepdims=True)
                pairs[c : c + 1, at] = extra
            geometry[3, :, at] = w3
            geometry[4, :, at] = 3.0 * (w3 * w2)

    pltpu.make_async_copy(everyone, everyone, all_recv).wait()
    for l in range(listed):
        tile = everyone[blocks[l]]
        near_rows[:, l * BLOCK : (l + 1) * BLOCK] = tile
        near_cols[l * BLOCK : (l + 1) * BLOCK, :] = jnp.concatenate(
            [tile, jnp.zeros_like(tile)], axis=0
        ).T

    def lent_near():
        names = [
            [jnp.broadcast_to(rim_in[0, side, 3:4, l : l + 1], (4, BLOCK)) for l in range(listed)]
            for side in range(2)
        ]

        def step(b, found):
            tile = everyone[b]
            return tuple(
                tuple(
                    jnp.where(names[side][l] == b.astype(F32), tile, found[side][l])
                    for l in range(listed)
                )
                for side in range(2)
            )

        blank = jnp.zeros((4, BLOCK), F32)
        found = lax.fori_loop(
            0, n * own_blocks, step, ((blank,) * listed,) * 2, unroll=max(8, min(32, n * own_blocks))
        )
        for side in range(2):
            for l in range(listed):
                lent_cols[side, l * BLOCK : (l + 1) * BLOCK, :] = jnp.concatenate(
                    [found[side][l], blank], axis=0
                ).T

    @pl.when(g == 0)
    def _():
        for number in late[spread_needs:]:
            load(number).wait()

        def strength_of(fields):
            fx, fy, fz = fields
            return jnp.sqrt(1.0 + fx * fx + fy * fy + fz * fz)

        def column_of(strength):
            return jnp.broadcast_to(strength, (8, strength.shape[1])).T[:, 0:1]

        def embed(column, at):
            return (features[at].astype(F32) + column * field_gain[...]).astype(BF16)

        def lent_field(side):
            return field(rim_in[0, side], lent_cols.at[side], listed * BLOCK)

        for j in range(EARLY):
            edge_part(0, j)
        strength = strength_of(field(own, near_cols, listed * BLOCK))
        site_result[2:3, :] = strength
        hidden_ref[...] = embed(column_of(strength), slice(0, rows))
        tables[0, 0:rows] = jnp.dot(
            hidden_ref[...], node_in[0], preferred_element_type=F32
        ).astype(BF16)
        fields, columns = [], []

        def lent_lift(j):
            if j == 0:
                lent_near()
            if j < 2:
                fields.append(lent_field(j))
            if j == 2:
                columns.extend(column_of(strength_of(part)) for part in fields)
            if j == pack - 1:
                arrive(lift_copy, 0)
                ends = (p > 0, p < n - 1)
                for side in range(2):
                    at = slice(rows + side * rim, rows + (side + 1) * rim)
                    hidden = embed(columns[side], at)
                    lifted = jnp.dot(hidden, node_in[0], preferred_element_type=F32)
                    tables[0, at] = jnp.where(ends[side], lifted, 0.0).astype(BF16)

        def lift(layer):
            lifted = jnp.dot(
                hidden_ref[...], node_in[layer], preferred_element_type=F32
            ).astype(BF16)
            lend(layer, lifted)
            gone(lift_copy, layer - 1)
            start(lift_copy, layer)
            tables[layer, 0:rows] = lifted

        for layer in range(layers):
            def beside(j, layer=layer):
                if layer == layers - 1:
                    term_geometry(False, j, pack)

            if layer:
                lift(layer)
                radial_net(layer)
            own_part(layer, beside if layer else lent_lift)
            if layer:
                arrive(lift_copy, layer)
            rim_part(layer)
            message = (acc[...].reshape(rows, channels) * (1.0 / slots)).astype(BF16)
            update = silu_of_half(
                0.5 * jnp.dot(message, node_out[layer], preferred_element_type=F32)
            )
            hidden_ref[...] = (hidden_ref[...].astype(F32) + update).astype(BF16)

        across = (((1,), (1,)), ((), ()))
        extra_cols[:, 0:2] = lax.dot_general(
            hidden_ref[...], readout[...], across, preferred_element_type=F32
        )
        site_result[0:2, :] = lax.dot_general(
            readout[...], hidden_ref[...], across, preferred_element_type=F32
        )
        send_terms(False)
        gone(lift_copy, layers - 1)

    @pl.when(g == 1)
    def _():
        out = field(own, near_cols, listed * BLOCK)
        for c in range(3):
            outside[c : c + 1, :] = out[c]
        gain = polar[...]
        outside[...] = outside[...] + pairs[...]
        dipole = [gain * outside[c : c + 1, :] for c in range(3)]

        def induced(at, index, pieces, begun=(None, None, None)):
            local = index & (BLOCK - 1)
            chunk = lax.shift_right_logical(index, 7)
            d = [table_gather(pieces(c), local, chunk, begun[c]) for c in range(3)]
            r = [geometry[c, :, at] for c in range(3)]
            w3 = geometry[3, :, at]
            s = (r[0] * d[0] + r[1] * d[1] + r[2] * d[2]) * geometry[4, :, at]
            return [jnp.sum(r[c] * s - d[c] * w3, axis=0, keepdims=True) for c in range(3)]

        def own_pieces(c, values):
            return [(b, values[c][:, b * BLOCK : (b + 1) * BLOCK]) for b in range(own_blocks)]

        def own_sweep(values, rims, begun):
            fresh = [[], [], []]
            for tile in range(own_blocks):
                at = slice(tile * BLOCK, (tile + 1) * BLOCK)

                def pieces(c):
                    ends = [(own_blocks + side, rims(side, c)) for side in range(2)]
                    return ends if begun else own_pieces(c, values) + ends

                totals = induced(
                    at, neighbours[:, at], pieces, begun[tile] if begun else (None, None, None)
                )
                for c in range(3):
                    fresh[c].append(gain[:, at] * (outside[c : c + 1, at] + totals[c]))
            return [jnp.concatenate(f, axis=1) for f in fresh]

        for sweep in range(ROUNDS):
            step = 1 + sweep
            values = jnp.concatenate(dipole + [jnp.zeros((1, rows), F32)], axis=0)
            fill_rims(step, values)
            gone(rim_copy, step - 1)
            gone(far_copy, step - 1, 2)
            gone(flat_copy, step - 1)
            start(rim_copy, step)
            start(far_copy, step, 2)
            flat_out[step] = values
            start(flat_copy, step)
            if sweep == 0:
                fill(fixed_out, jnp.concatenate([outside[...], gain], axis=0))
                start(fixed_copy, 0)
            begun = []
            for tile in range(own_blocks):
                index = neighbours[:, tile * BLOCK : (tile + 1) * BLOCK]
                local = index & (BLOCK - 1)
                chunk = lax.shift_right_logical(index, 7)
                begun.append([table_gather(own_pieces(c, dipole), local, chunk) for c in range(3)])
            if sweep == 0:
                lent_geometry()
                term_geometry(True, 0, 1)
            arrive(rim_copy, step)
            arrive(far_copy, step, 2)
            arrive(flat_copy, step)
            if sweep == 0:
                arrive(fixed_copy, 0)
            middle = own_sweep(
                dipole, lambda side, c: rim_in[step, side, c : c + 1, :], begun
            )
            lent_middle = []
            for side in range(2):
                at = slice(rows + side * rim, rows + (side + 1) * rim)
                totals = induced(
                    at,
                    lists_in[side],
                    lambda c: lent_pieces(
                        side, c, flat_in[step, side], rim_out[step, 1 - side], far_in[step, side]
                    ),
                )
                lent_middle.append([
                    fixed_in[side, 3:4, :] * (fixed_in[side, c : c + 1, :] + totals[c])
                    for c in range(3)
                ])
            dipole = own_sweep(middle, lambda side, c: lent_middle[side][c], None)
        for c in range(3):
            site_result[c : c + 1, :] = dipole[c]
        stacked = jnp.concatenate(dipole + [jnp.zeros((5, rows), F32)], axis=0)
        extra_cols[...] = stacked.T
        send_terms(True)
        gone(far_copy, ROUNDS, 2)
        gone(flat_copy, ROUNDS)
        gone(list_copy, 0)
        gone(fixed_copy, 0)

    def term_copy(i):
        return pltpu.make_async_remote_copy(
            src_ref=term_out.at[peer(i)],
            dst_ref=term_in.at[p],
            send_sem=term_send,
            recv_sem=term_recv,
            device_id=place(other, peer(i)),
            device_id_type=MESH,
        )

    for first, last in ((0, n // 2), (n // 2, n)):

        @pl.loop(first, last, unroll=min(n // 2, 8))
        def _(i):
            q = peer(i)
            for b in range(own_blocks):
                total = jnp.zeros((3, BLOCK), F32)
                for l in range(listed):
                    total = total + jnp.where(
                        blocks[l] == q * own_blocks + b, terms[:, l * BLOCK : (l + 1) * BLOCK], 0.0
                    )
                term_out[q, b * 3 : (b + 1) * 3, :] = total

        @pl.loop(first, last, unroll=4)
        def _(i):
            term_copy(i).start()

    gone(rim_copy, 0)
    pltpu.make_async_copy(everyone, everyone, all_send).wait()
    pltpu.make_async_copy(term_in, term_in, term_recv).wait()

    total = jnp.sum(term_in[...], axis=0)
    for b in range(own_blocks):
        response[:, b * BLOCK : (b + 1) * BLOCK] = total[b * 3 : (b + 1) * 3, :]
    pltpu.make_async_copy(term_in, term_in, term_send).wait()


def local(n_dom, n_sub, *args):
    (
        positions,
        charges,
        polar,
        features,
        neighbours,
        send_rows,
        blocks,
        radial_in,
        radial_mid,
        radial_out,
        node_in,
        node_out,
        field_gain,
        readout,
    ) = args
    n = n_dom * n_sub
    rows = positions.shape[1]
    own_blocks = rows // BLOCK
    slots = neighbours.shape[1]
    listed = blocks.shape[0]
    layers, basis, radial = radial_in.shape
    channels = features.shape[1]
    rim = send_rows.shape[1]
    pack = channels // radial
    dma = pltpu.SemaphoreType.DMA
    operands = (
        positions,
        charges.reshape(1, -1),
        polar.reshape(1, -1),
        features,
        neighbours.T,
        send_rows,
        blocks,
        radial_in,
        radial_mid,
        radial_out,
        node_in,
        node_out,
        field_gain.reshape(1, -1),
        readout.T,
    )
    spaces = [pltpu.VMEM] * INPUTS
    spaces[6] = pltpu.SMEM
    shapes = [a.shape for a in operands]
    shapes[3] = (rows + 2 * rim, channels)
    both = pl.pallas_call(
        functools.partial(kernel, n_dom, n_sub),
        out_shape=jax.ShapeDtypeStruct((2, 3, rows), F32),
        in_specs=[pl.BlockSpec(memory_space=pl.ANY)] * INPUTS,
        out_specs=pl.BlockSpec(memory_space=pltpu.VMEM),
        scratch_shapes=[space(shape, a.dtype) for space, shape, a in zip(spaces, shapes, operands)]
        + [
            dma((INPUTS,)),
            pltpu.VMEM((own_blocks, 4, BLOCK), F32),
            pltpu.VMEM((n * own_blocks, 4, BLOCK), F32),
            pltpu.VMEM((4, listed * BLOCK), F32),
            pltpu.VMEM((listed * BLOCK, 8), F32),
            pltpu.VMEM((8, rows), F32),
            pltpu.VMEM((rows, 8), F32),
            pltpu.VMEM((rows, 8), F32),
            pltpu.VMEM((1 + ROUNDS, 2, 4, rim), F32),
            pltpu.VMEM((1 + ROUNDS, 2, 4, rim), F32),
            pltpu.VMEM((1 + ROUNDS, 4, rows), F32),
            pltpu.VMEM((1 + ROUNDS, 2, 4, rows), F32),
            pltpu.VMEM((1 + ROUNDS, 2, 4, rim), F32),
            pltpu.VMEM((2, slots, rim), jnp.int32),
            pltpu.VMEM((2, slots, rim), jnp.int32),
            pltpu.VMEM((2, 4, rim), F32),
            pltpu.VMEM((2, 4, rim), F32),
            pltpu.VMEM((5, slots, rows + 2 * rim), F32),
            pltpu.VMEM((pack, rows // STRIP, slots // pack, STRIP, rows + 2 * rim), BF16),
            pltpu.VMEM((2 * rim, rows), BF16),
            pltpu.VMEM((slots // pack * rows, pack * basis), BF16),
            pltpu.VMEM((2, slots // pack * rows, channels), BF16),
            pltpu.VMEM((layers, rows // STRIP, slots // pack, STRIP, channels), BF16),
            pltpu.VMEM((pack, rows // STRIP, slots // pack, STRIP, channels), F32),
            pltpu.VMEM((layers, pack * basis, channels), BF16),
            pltpu.VMEM((layers, 2, channels, channels), BF16),
            pltpu.VMEM((layers, pack, channels, channels), BF16),
            pltpu.VMEM((layers, rows + 2 * rim, channels), BF16),
            pltpu.VMEM((layers, 2, rim, channels), BF16),
            pltpu.VMEM((2, listed * BLOCK, 8), F32),
            pltpu.VMEM((5, rows, listed * BLOCK), F32),
            pltpu.VMEM((rows, channels), BF16),
            pltpu.VMEM((rows // STRIP, STRIP, channels), F32),
            pltpu.VMEM((3, rows), F32),
            pltpu.VMEM((3, rows), F32),
            pltpu.VMEM((3, listed * BLOCK), F32),
            pltpu.VMEM((n, own_blocks * 3, BLOCK), F32),
            pltpu.VMEM((n, own_blocks * 3, BLOCK), F32),
            dma(()),
            dma(()),
            dma((2,)),
            dma((1 + ROUNDS, 2)),
            dma((2,)),
            dma((layers, 2)),
            dma(()),
            dma(()),
            dma((2,)),
            dma((1 + ROUNDS, 2)),
            dma((2,)),
            dma((1 + ROUNDS, 2)),
            dma((2,)),
            dma((1, 2)),
            dma((2,)),
            dma((1, 2)),
        ],
        compiler_params=pltpu.CompilerParams(
            collective_id=0, has_side_effects=True, vmem_limit_bytes=40 * 2**20
        ),
    )(*(pltpu.with_memory_space_constraint(a, pltpu.HBM) for a in operands))
    return both[0], both[1]


def solution(mesh):
    sites = ("grp", "dom", "sub")
    in_specs = (
        P(None, sites),
        P(sites),
        P(sites),
        P(sites, None),
        P(sites, None),
        P(None, sites),
        P(sites),
    ) + (P(),) * 7
    out_specs = (P(None, sites), P(None, sites))
    body = functools.partial(local, mesh.shape["dom"], mesh.shape["sub"])
    return jax.shard_map(body, mesh=mesh, in_specs=in_specs, out_specs=out_specs, check_vma=False)
```

```python
import functools

import jax
import jax.numpy as jnp
from jax import lax
from jax.experimental import pallas as pl
from jax.experimental.pallas import tpu as pltpu
from jax.sharding import PartitionSpec as P

SWEEPS = 4
ROUNDS = SWEEPS // 2
BLOCK = 128
SMOOTH = 1.0
SPACING = 0.75
MESH = pl.DeviceIdType.MESH
INPUTS = 14
STRIP = 16
EARLY = 3
F32 = jnp.float32
BF16 = jnp.bfloat16


def silu_of_half(half):
    return half + half * jnp.tanh(half)


def lane_pick(rows, index):
    shape = index.shape
    return jnp.take_along_axis(
        jnp.broadcast_to(rows, shape), index, axis=1, mode="promise_in_bounds"
    )


def table_gather(pieces, local, chunk, total=None):
    if total is None:
        total = jnp.zeros(local.shape, pieces[0][1].dtype)
    for number, rows in pieces:
        total = jnp.where(chunk == number, lane_pick(rows, local), total)
    return total


def kernel(
    n_dom,
    n_sub,
    *refs,
):
    sources = refs[:INPUTS]
    (
    both,
    positions,
    charges,
    polar,
    features,
    neighbours,
    send_rows,
    blocks,
    radial_in,
    radial_mid,
    radial_out,
    node_in,
    node_out,
    field_gain,
    readout,
    in_sem,
    packet,
    everyone,
    near_rows,
    near_cols,
    own_rows,
    own_cols,
    extra_cols,
    rim_out,
    rim_in,
    flat_out,
    flat_in,
    far_in,
    lists_out,
    lists_in,
    fixed_out,
    fixed_in,
    geometry,
    hot,
    pick,
    wave,
    stage,
    third,
    edge_weight,
    wide_in,
    wide_mid,
    wide_out,
    tables,
    lent,
    lent_cols,
    reach,
    hidden_ref,
    acc,
    outside,
    pairs,
    terms,
    term_out,
    term_in,
    all_send,
    all_recv,
    rim_send,
    rim_recv,
    lift_send,
    lift_recv,
    term_send,
    term_recv,
    flat_send,
    flat_recv,
    far_send,
    far_recv,
    list_send,
    list_recv,
    fixed_send,
    fixed_recv,
    ) = refs[INPUTS:]
    g = lax.axis_index("grp")
    p = lax.axis_index("dom") * n_sub + lax.axis_index("sub")
    site_result, response = both.at[0], both.at[1]
    n = n_dom * n_sub
    rows = positions.shape[1]
    own_blocks = rows // BLOCK
    slots = neighbours.shape[0]
    listed = blocks.shape[0]
    layers, basis, radial = radial_in.shape
    channels = features.shape[1]
    rim = send_rows.shape[1]
    pack = channels // radial
    groups = slots // pack
    strips = rows // STRIP
    other = 1 - g
    held = (
        positions,
        charges,
        polar,
        features,
        neighbours,
        send_rows,
        blocks,
        radial_in,
        radial_mid,
        radial_out,
        node_in,
        node_out,
        field_gain,
        readout,
    )
    early = (0, 1, 2, 4, 5, 6)
    late = (7, 8, 9, 3, 10, 11, 12, 13)
    spread_needs = 4

    def load(number):
        target = held[number]
        if number == 3:
            target = target.at[pl.ds(0, rows)]
        return pltpu.make_async_copy(sources[number], target, in_sem.at[number])

    for number in early:
        load(number).start()

    def place(group, q):
        return (group, lax.div(q, n_sub), lax.rem(q, n_sub))

    def peer(i):
        if n % 4:
            return lax.rem(p + i, n)
        quarter = n // 4
        second = lax.div(2 * p, n)
        turn = lax.div(i, quarter)
        far = second * turn + (1 - second) * (3 - turn)
        return far * quarter + lax.rem(p + i, quarter)

    barrier = pltpu.get_barrier_semaphore()

    @pl.loop(0, n)
    def _(i):
        pl.semaphore_signal(barrier, inc=1, device_id=place(other, peer(i)), device_id_type=MESH)

    @pl.when(p > 0)
    def _():
        pl.semaphore_signal(barrier, inc=1, device_id=place(g, p - 1), device_id_type=MESH)

    @pl.when(p < n - 1)
    def _():
        pl.semaphore_signal(barrier, inc=1, device_id=place(g, p + 1), device_id_type=MESH)

    @pl.when(p > 1)
    def _():
        pl.semaphore_signal(barrier, inc=1, device_id=place(g, p - 2), device_id_type=MESH)

    @pl.when(p < n - 2)
    def _():
        pl.semaphore_signal(barrier, inc=1, device_id=place(g, p + 2), device_id_type=MESH)

    @pl.when(g == 0)
    def _():
        for number in late:
            load(number).start()

    own_rows[...] = jnp.zeros_like(own_rows)
    for number in early:
        load(number).wait()
    own_rows[0:3, :] = positions[...]
    own_rows[3:4, :] = charges[...]
    own = own_rows[...]
    for b in range(own_blocks):
        packet[b] = own[0:4, b * BLOCK : (b + 1) * BLOCK]

    def fill(target, values):
        for side in range(2):
            index = jnp.broadcast_to(send_rows[side : side + 1, :], (values.shape[0], rim))
            target[side] = table_gather(
                [(c, values[:, c * BLOCK : (c + 1) * BLOCK]) for c in range(own_blocks)],
                index & (BLOCK - 1),
                lax.shift_right_logical(index, 7),
            )

    def fill_rims(step, values):
        fill(rim_out.at[step], values)

    def side_copy(src, dst, send, recv, step, side, q):
        return pltpu.make_async_remote_copy(
            src_ref=src,
            dst_ref=dst,
            send_sem=send.at[side],
            recv_sem=recv.at[step, side],
            device_id=place(g, q),
            device_id_type=MESH,
        )

    def rim_copy(step, side, q):
        return side_copy(
            rim_out.at[step, side], rim_in.at[step, side], rim_send, rim_recv, step, side, q
        )

    def lift_copy(layer, side, q):
        target = tables.at[layer] if layer else features
        return side_copy(
            lent.at[layer, side],
            target.at[pl.ds(rows + side * rim, rim)],
            lift_send,
            lift_recv,
            layer,
            side,
            q,
        )

    def flat_copy(step, side, q):
        return side_copy(
            flat_out.at[step], flat_in.at[step, side], flat_send, flat_recv, step, side, q
        )

    def far_copy(step, side, q):
        return side_copy(
            rim_out.at[step, side], far_in.at[step, side], far_send, far_recv, step, side, q
        )

    def list_copy(step, side, q):
        return side_copy(
            lists_out.at[side], lists_in.at[side], list_send, list_recv, step, side, q
        )

    def fixed_copy(step, side, q):
        return side_copy(
            fixed_out.at[side], fixed_in.at[side], fixed_send, fixed_recv, step, side, q
        )

    def start(copy, step, away=1):
        @pl.when(p < n - away)
        def _():
            copy(step, 0, p + away).start()

        @pl.when(p > away - 1)
        def _():
            copy(step, 1, p - away).start()

    def arrive(copy, step, away=1):
        @pl.when(p > away - 1)
        def _():
            copy(step, 0, p - away).wait_recv()

        @pl.when(p < n - away)
        def _():
            copy(step, 1, p + away).wait_recv()

    def gone(copy, step, away=1):
        @pl.when(p < n - away)
        def _():
            copy(step, 0, p + away).wait_send()

        @pl.when(p > away - 1)
        def _():
            copy(step, 1, p - away).wait_send()

    def mark_slots(span):
        width = rows + 2 * rim
        lane = lax.broadcasted_iota(jnp.int32, (rows, width), 1).astype(jnp.int16)
        listing = jnp.concatenate(
            [neighbours[...].astype(F32), jnp.zeros((BLOCK - slots, rows), F32)], axis=0
        ).T.astype(jnp.int32)
        one, none = jnp.ones((rows, width), BF16), jnp.zeros((rows, width), BF16)
        for k in span:
            entry = jnp.broadcast_to(listing[:, k : k + 1], (rows, BLOCK)).astype(jnp.int16)
            entry = jnp.concatenate([entry] * (width // BLOCK), axis=1)
            mark = jnp.where(entry == lane, one, none)
            hot[k % pack, :, k // pack] = mark.reshape(strips, STRIP, width)

    def mark_lent():
        lists = jnp.concatenate(
            [send_rows[...].astype(F32), jnp.zeros((6, rim), F32)], axis=0
        ).T.astype(jnp.int32)
        site = lax.broadcasted_iota(jnp.int32, (rim, rows), 1)
        for side in range(2):
            pick[side * rim : (side + 1) * rim, :] = jnp.where(
                lists[:, side : side + 1] == site, 1.0, 0.0
            ).astype(BF16)

    def spread():
        for number in late[:spread_needs]:
            load(number).wait()
        spread_r = (
            lax.broadcasted_iota(jnp.int32, (channels, radial), 0) % radial
            == lax.broadcasted_iota(jnp.int32, (channels, radial), 1)
        ).astype(F32).astype(BF16)
        spread_c = (
            lax.broadcasted_iota(jnp.int32, (radial, channels), 1) % radial
            == lax.broadcasted_iota(jnp.int32, (radial, channels), 0)
        ).astype(F32).astype(BF16)
        same_in = (
            lax.broadcasted_iota(jnp.int32, (pack * basis, channels), 0) // basis
            == lax.broadcasted_iota(jnp.int32, (pack * basis, channels), 1) // radial
        )
        same_mid = (
            lax.broadcasted_iota(jnp.int32, (channels, channels), 0) // radial
            == lax.broadcasted_iota(jnp.int32, (channels, channels), 1) // radial
        )
        for layer in range(layers):
            flat = jnp.dot(radial_in[layer], spread_c, preferred_element_type=F32)
            wide_in[layer] = jnp.where(
                same_in, jnp.concatenate([0.5 * flat] * pack, axis=0), 0.0
            ).astype(BF16)
            for m in range(2):
                flat = jnp.dot(
                    jnp.dot(spread_r, radial_mid[layer, m], preferred_element_type=F32).astype(
                        BF16
                    ),
                    spread_c,
                    preferred_element_type=F32,
                )
                wide_mid[layer, m] = jnp.where(same_mid, 0.5 * flat, 0.0).astype(BF16)
            for j in range(pack):
                wide_out[layer, j] = jnp.zeros((channels, channels), BF16)
                wide_out[layer, j, j * radial : (j + 1) * radial, :] = radial_out[layer]

    def lend(layer, values):
        picked = jnp.dot(pick[...], values, preferred_element_type=F32).astype(BF16)
        lent[layer] = picked.reshape(2, rim, channels)

    fill_rims(0, own[0:4])

    @pl.when(g == 0)
    def _():
        spot = lax.broadcasted_iota(jnp.int32, (1, rim), 1)
        names = jnp.zeros((1, rim), F32)
        for l in range(listed):
            names = jnp.where(spot == l, blocks[l].astype(F32), names)
        for side in range(2):
            rim_out[0, side, 3:4, :] = names

    @pl.when(p == 0)
    def _():
        for step in range(1 + ROUNDS):
            rim_in[step, 0] = jnp.zeros((4, rim), F32)
        features[rows : rows + rim] = jnp.zeros((rim, channels), BF16)
        for layer in range(1, layers):
            tables[layer, rows : rows + rim] = jnp.zeros((rim, channels), BF16)

    @pl.when(p == n - 1)
    def _():
        for step in range(1 + ROUNDS):
            rim_in[step, 1] = jnp.zeros((4, rim), F32)
        features[rows + rim :] = jnp.zeros((rim, channels), BF16)
        for layer in range(1, layers):
            tables[layer, rows + rim :] = jnp.zeros((rim, channels), BF16)

    def clear(side, away):
        for step in range(1 + ROUNDS):
            far_in[step, side] = jnp.zeros((4, rim), F32)
            if away == 1:
                flat_in[step, side] = jnp.zeros((4, rows), F32)
        if away == 1:
            lists_in[side] = jnp.zeros((slots, rim), jnp.int32)
            fixed_in[side] = jnp.zeros((4, rim), F32)

    @pl.when(g == 1)
    def _():
        flat_out[0] = own[0:4]
        fill(lists_out, neighbours[...])
        for side, ends in enumerate(((0, 1), (n - 1, n - 2))):
            pl.when(p == ends[0])(functools.partial(clear, side, 1))
            pl.when(p == ends[1])(functools.partial(clear, side, 2))

    @pl.when(g == 0)
    def _():
        mark_slots(range(slots // 2))

    sides = [p > 0, p < n - 1, p > 1, p < n - 2]
    pl.semaphore_wait(barrier, n + sum(side.astype(jnp.int32) for side in sides))

    def packet_copy(i):
        return pltpu.make_async_remote_copy(
            src_ref=packet,
            dst_ref=everyone.at[pl.ds(p * own_blocks, own_blocks)],
            send_sem=all_send,
            recv_sem=all_recv,
            device_id=place(other, peer(i)),
            device_id_type=MESH,
        )

    start(rim_copy, 0)

    @pl.loop(0, n, unroll=4)
    def _(i):
        packet_copy(i).start()

    @pl.when(g == 0)
    def _():
        mark_lent()
        spread()
        mark_slots(range(slots // 2, slots))
        lend(0, features[0:rows])

    own_cols[...] = own.T

    def field(targets, source_cols, count):
        x, y, z = (targets[c : c + 1, :] for c in range(3))

        def step(i, sums):
            source = source_cols[pl.ds(pl.multiple_of(i * 8, 8), 8), :]
            rx = x - source[:, 0:1]
            ry = y - source[:, 1:2]
            rz = z - source[:, 2:3]
            w = lax.rsqrt(rx * rx + ry * ry + rz * rz + SMOOTH)
            s = source[:, 3:4] * (w * w * w)
            return (sums[0] + rx * s, sums[1] + ry * s, sums[2] + rz * s)

        zero = jnp.zeros((8, targets.shape[1]), F32)
        sums = lax.fori_loop(0, count // 8, step, (zero, zero, zero), unroll=True)
        return [jnp.sum(s, axis=0, keepdims=True) for s in sums]

    def term_geometry(dipole, part, parts):
        x, y, z = (near_rows[c : c + 1, :] for c in range(3))
        for i in range(part * rows // 8 // parts, (part + 1) * rows // 8 // parts):
            at = slice(i * 8, i * 8 + 8)
            source = own_cols[at, :]
            r = (x - source[:, 0:1], y - source[:, 1:2], z - source[:, 2:3])
            w = lax.rsqrt(r[0] * r[0] + r[1] * r[1] + r[2] * r[2] + SMOOTH)
            w2 = w * w
            w3 = w2 * w
            for c in range(3):
                reach[c, at, :] = r[c] if dipole else r[c] * w3
            if dipole:
                reach[3, at, :] = w3
                reach[4, at, :] = 3.0 * (w3 * w2)

    def send_terms(dipole):
        def step(i, sums):
            at = pl.ds(pl.multiple_of(i * 8, 8), 8)
            d = extra_cols[at, :]
            r = [reach[c, at, :] for c in range(3)]
            if not dipole:
                return tuple(sums[c] + r[c] * d[:, 0:1] for c in range(3))
            w3 = reach[3, at, :]
            d = [d[:, c : c + 1] for c in range(3)]
            s = (r[0] * d[0] + r[1] * d[1] + r[2] * d[2]) * reach[4, at, :]
            return tuple(sums[c] + (r[c] * s - d[c] * w3) for c in range(3))

        zero = jnp.zeros((8, listed * BLOCK), F32)
        sums = lax.fori_loop(0, rows // 8, step, (zero, zero, zero), unroll=True)
        for c in range(3):
            terms[c : c + 1, :] = jnp.sum(sums[c], axis=0, keepdims=True)

    def lent_pieces(side, c, flat, mine, far):
        flat, mine, far = (rows_[c : c + 1, :] for rows_ in (flat, mine, far))
        rims = (far, mine) if side == 0 else (mine, far)
        return [(b, flat[:, b * BLOCK : (b + 1) * BLOCK]) for b in range(own_blocks)] + [
            (own_blocks + i, rims[i]) for i in range(2)
        ]

    def lent_geometry():
        arrive(flat_copy, 0)
        arrive(far_copy, 0, 2)
        arrive(list_copy, 0)
        for side in range(2):
            at = slice(rows + side * rim, rows + (side + 1) * rim)
            index = lists_in[side]
            local = index & (BLOCK - 1)
            chunk = lax.shift_right_logical(index, 7)
            offset = [
                rim_in[0, side, c : c + 1, :]
                - table_gather(
                    lent_pieces(side, c, flat_in[0, side], rim_out[0, 1 - side], far_in[0, side]),
                    local,
                    chunk,
                )
                for c in range(3)
            ]
            w = lax.rsqrt(
                offset[0] * offset[0] + offset[1] * offset[1] + offset[2] * offset[2] + SMOOTH
            )
            w2 = w * w
            w3 = w2 * w
            for c in range(3):
                geometry[c, :, at] = offset[c]
            geometry[3, :, at] = w3
            geometry[4, :, at] = 3.0 * (w3 * w2)

    def edge_index(tile):
        index = neighbours[:, tile * BLOCK : (tile + 1) * BLOCK]
        return index & (BLOCK - 1), lax.shift_right_logical(index, 7)

    def own_edges(count):
        return [
            [
                table_gather(
                    [(b, own_rows[c : c + 1, b * BLOCK : (b + 1) * BLOCK]) for b in range(own_blocks)],
                    *edge_index(tile),
                )
                for c in range(count)
            ]
            for tile in range(own_blocks)
        ]

    def edges(begun):
        for tile in range(own_blocks):
            at = slice(tile * BLOCK, (tile + 1) * BLOCK)
            local, chunk = edge_index(tile)
            picked = [
                table_gather(
                    [(own_blocks + side, rim_in[0, side, c : c + 1, :]) for side in range(2)],
                    local,
                    chunk,
                    value,
                )
                for c, value in enumerate(begun[tile])
            ]
            ox, oy, oz = (own_rows[c : c + 1, at] - picked[c] for c in range(3))
            dist_sq = ox * ox + oy * oy + oz * oz + SMOOTH
            yield at, (ox, oy, oz), dist_sq, picked[-1]

    centre = lax.broadcasted_iota(jnp.int32, (basis, rows), 0).astype(F32) * SPACING

    def waves():
        for q in range(groups):
            parts = []
            for j in range(pack):
                away = jnp.broadcast_to(geometry[0, q * pack + j : q * pack + j + 1, 0:rows], (basis, rows))
                away = away - centre
                parts.append(jnp.exp(-(away * away)))
            turned = jnp.concatenate(parts, axis=0).T
            wave[q * rows : (q + 1) * rows, :] = turned.astype(BF16)

    def radial_net(layer):
        half = groups // 2
        spans = [range(half), range(half, groups)]
        for step in range(3):
            for part, span in enumerate(spans):
                at = slice(span[0] * rows, (span[-1] + 1) * rows)
                if step == 0:
                    source, weight = wave[at, :], wide_in[layer]
                else:
                    source, weight = stage[step - 1, at, :], wide_mid[layer, step - 1]
                h = silu_of_half(jnp.dot(source, weight, preferred_element_type=F32)).astype(BF16)
                if step < 2:
                    stage[step, at, :] = h
                else:
                    for i, q in enumerate(span):
                        third[layer, :, q] = h[i * rows : (i + 1) * rows].reshape(
                            strips, STRIP, channels
                        )

    def edge_part(layer, j):
        edge_weight[j] = jnp.dot(
            third[layer].reshape(groups * rows, channels),
            wide_out[layer, j],
            preferred_element_type=F32,
        ).reshape(strips, groups, STRIP, channels)

    def own_part(layer, beside):
        for j in range(pack):
            beside(j)
            if layer or j >= EARLY:
                edge_part(layer, j)
            gather_part(layer, j, 0, rows)

    def rim_part(layer):
        for j in range(pack):
            gather_part(layer, j, rows, 2 * rim)

    def gather_part(layer, j, first, count):
        source = jnp.dot(
            hot[j, :, :, :, first : first + count].reshape(groups * rows, count),
            tables[layer, first : first + count],
            preferred_element_type=F32,
        )
        product = edge_weight[j] * source.reshape(strips, groups, STRIP, channels)
        total = jnp.sum(product, axis=1)
        if first or j:
            total = acc[...] + total
        acc[...] = total

    @pl.when(g == 0)
    def _():
        begun = own_edges(3)
        start(lift_copy, 0)
        arrive(rim_copy, 0)
        for at, _, dist_sq, _ in edges(begun):
            geometry[0, :, at] = jnp.sqrt(dist_sq)
        waves()
        radial_net(0)

    @pl.when(g == 1)
    def _():
        begun = own_edges(4)
        arrive(rim_copy, 0)
        start(flat_copy, 0)
        start(far_copy, 0, 2)
        start(list_copy, 0)
        for at, offset, dist_sq, source_charge in edges(begun):
            w = lax.rsqrt(dist_sq)
            w2 = w * w
            w3 = w2 * w
            s = source_charge * w3
            for c in range(3):
                geometry[c, :, at] = offset[c]
                extra = jnp.sum(offset[c] * s, axis=0, keepdims=True)
                pairs[c : c + 1, at] = extra
            geometry[3, :, at] = w3
            geometry[4, :, at] = 3.0 * (w3 * w2)

    pltpu.make_async_copy(everyone, everyone, all_recv).wait()
    for l in range(listed):
        tile = everyone[blocks[l]]
        near_rows[:, l * BLOCK : (l + 1) * BLOCK] = tile
        near_cols[l * BLOCK : (l + 1) * BLOCK, :] = jnp.concatenate(
            [tile, jnp.zeros_like(tile)], axis=0
        ).T

    def lent_near():
        names = [
            [jnp.broadcast_to(rim_in[0, side, 3:4, l : l + 1], (4, BLOCK)) for l in range(listed)]
            for side in range(2)
        ]

        def step(b, found):
            tile = everyone[b]
            return tuple(
                tuple(
                    jnp.where(names[side][l] == b.astype(F32), tile, found[side][l])
                    for l in range(listed)
                )
                for side in range(2)
            )

        blank = jnp.zeros((4, BLOCK), F32)
        found = lax.fori_loop(
            0, n * own_blocks, step, ((blank,) * listed,) * 2, unroll=max(8, min(32, n * own_blocks))
        )
        for side in range(2):
            for l in range(listed):
                lent_cols[side, l * BLOCK : (l + 1) * BLOCK, :] = jnp.concatenate(
                    [found[side][l], blank], axis=0
                ).T

    @pl.when(g == 0)
    def _():
        for number in late[spread_needs:]:
            load(number).wait()

        def strength_of(fields):
            fx, fy, fz = fields
            return jnp.sqrt(1.0 + fx * fx + fy * fy + fz * fz)

        def column_of(strength):
            return jnp.broadcast_to(strength, (8, strength.shape[1])).T[:, 0:1]

        def embed(column, at):
            return (features[at].astype(F32) + column * field_gain[...]).astype(BF16)

        def lent_field(side):
            return field(rim_in[0, side], lent_cols.at[side], listed * BLOCK)

        for j in range(EARLY):
            edge_part(0, j)
        strength = strength_of(field(own, near_cols, listed * BLOCK))
        site_result[2:3, :] = strength
        hidden_ref[...] = embed(column_of(strength), slice(0, rows))
        tables[0, 0:rows] = jnp.dot(
            hidden_ref[...], node_in[0], preferred_element_type=F32
        ).astype(BF16)
        fields, columns = [], []

        def lent_lift(j):
            if j == 0:
                lent_near()
            if j < 2:
                fields.append(lent_field(j))
            if j == 2:
                columns.extend(column_of(strength_of(part)) for part in fields)
            if j == pack - 1:
                arrive(lift_copy, 0)
                ends = (p > 0, p < n - 1)
                for side in range(2):
                    at = slice(rows + side * rim, rows + (side + 1) * rim)
                    hidden = embed(columns[side], at)
                    lifted = jnp.dot(hidden, node_in[0], preferred_element_type=F32)
                    tables[0, at] = jnp.where(ends[side], lifted, 0.0).astype(BF16)

        def lift(layer):
            lifted = jnp.dot(
                hidden_ref[...], node_in[layer], preferred_element_type=F32
            ).astype(BF16)
            lend(layer, lifted)
            gone(lift_copy, layer - 1)
            start(lift_copy, layer)
            tables[layer, 0:rows] = lifted

        for layer in range(layers):
            def beside(j, layer=layer):
                if layer == layers - 1:
                    term_geometry(False, j, pack)

            if layer:
                lift(layer)
                radial_net(layer)
            own_part(layer, beside if layer else lent_lift)
            if layer:
                arrive(lift_copy, layer)
            rim_part(layer)
            message = (acc[...].reshape(rows, channels) * (1.0 / slots)).astype(BF16)
            update = silu_of_half(
                0.5 * jnp.dot(message, node_out[layer], preferred_element_type=F32)
            )
            hidden_ref[...] = (hidden_ref[...].astype(F32) + update).astype(BF16)

        across = (((1,), (1,)), ((), ()))
        extra_cols[:, 0:2] = lax.dot_general(
            hidden_ref[...], readout[...], across, preferred_element_type=F32
        )
        site_result[0:2, :] = lax.dot_general(
            readout[...], hidden_ref[...], across, preferred_element_type=F32
        )
        send_terms(False)
        gone(lift_copy, layers - 1)

    @pl.when(g == 1)
    def _():
        out = field(own, near_cols, listed * BLOCK)
        for c in range(3):
            outside[c : c + 1, :] = out[c]
        gain = polar[...]
        outside[...] = outside[...] + pairs[...]
        dipole = [gain * outside[c : c + 1, :] for c in range(3)]

        def induced(at, index, pieces, begun=(None, None, None)):
            local = index & (BLOCK - 1)
            chunk = lax.shift_right_logical(index, 7)
            d = [table_gather(pieces(c), local, chunk, begun[c]) for c in range(3)]
            r = [geometry[c, :, at] for c in range(3)]
            w3 = geometry[3, :, at]
            s = (r[0] * d[0] + r[1] * d[1] + r[2] * d[2]) * geometry[4, :, at]
            return [jnp.sum(r[c] * s - d[c] * w3, axis=0, keepdims=True) for c in range(3)]

        def own_pieces(c, values):
            return [(b, values[c][:, b * BLOCK : (b + 1) * BLOCK]) for b in range(own_blocks)]

        def own_sweep(values, rims, begun):
            fresh = [[], [], []]
            for tile in range(own_blocks):
                at = slice(tile * BLOCK, (tile + 1) * BLOCK)

                def pieces(c):
                    ends = [(own_blocks + side, rims(side, c)) for side in range(2)]
                    return ends if begun else own_pieces(c, values) + ends

                totals = induced(
                    at, neighbours[:, at], pieces, begun[tile] if begun else (None, None, None)
                )
                for c in range(3):
                    fresh[c].append(gain[:, at] * (outside[c : c + 1, at] + totals[c]))
            return [jnp.concatenate(f, axis=1) for f in fresh]

        for sweep in range(ROUNDS):
            step = 1 + sweep
            values = jnp.concatenate(dipole + [jnp.zeros((1, rows), F32)], axis=0)
            fill_rims(step, values)
            gone(rim_copy, step - 1)
            gone(far_copy, step - 1, 2)
            gone(flat_copy, step - 1)
            start(rim_copy, step)
            start(far_copy, step, 2)
            flat_out[step] = values
            start(flat_copy, step)
            if sweep == 0:
                fill(fixed_out, jnp.concatenate([outside[...], gain], axis=0))
                start(fixed_copy, 0)
            begun = []
            for tile in range(own_blocks):
                index = neighbours[:, tile * BLOCK : (tile + 1) * BLOCK]
                local = index & (BLOCK - 1)
                chunk = lax.shift_right_logical(index, 7)
                begun.append([table_gather(own_pieces(c, dipole), local, chunk) for c in range(3)])
            if sweep == 0:
                lent_geometry()
                term_geometry(True, 0, 1)
            arrive(rim_copy, step)
            arrive(far_copy, step, 2)
            arrive(flat_copy, step)
            if sweep == 0:
                arrive(fixed_copy, 0)
            middle = own_sweep(
                dipole, lambda side, c: rim_in[step, side, c : c + 1, :], begun
            )
            lent_middle = []
            for side in range(2):
                at = slice(rows + side * rim, rows + (side + 1) * rim)
                totals = induced(
                    at,
                    lists_in[side],
                    lambda c: lent_pieces(
                        side, c, flat_in[step, side], rim_out[step, 1 - side], far_in[step, side]
                    ),
                )
                lent_middle.append([
                    fixed_in[side, 3:4, :] * (fixed_in[side, c : c + 1, :] + totals[c])
                    for c in range(3)
                ])
            dipole = own_sweep(middle, lambda side, c: lent_middle[side][c], None)
        for c in range(3):
            site_result[c : c + 1, :] = dipole[c]
        stacked = jnp.concatenate(dipole + [jnp.zeros((5, rows), F32)], axis=0)
        extra_cols[...] = stacked.T
        send_terms(True)
        gone(far_copy, ROUNDS, 2)
        gone(flat_copy, ROUNDS)
        gone(list_copy, 0)
        gone(fixed_copy, 0)

    def term_copy(i):
        return pltpu.make_async_remote_copy(
            src_ref=term_out.at[peer(i)],
            dst_ref=term_in.at[p],
            send_sem=term_send,
            recv_sem=term_recv,
            device_id=place(other, peer(i)),
            device_id_type=MESH,
        )

    for first, last in ((0, n // 2), (n // 2, n)):

        @pl.loop(first, last, unroll=min(n // 2, 8))
        def _(i):
            q = peer(i)
            for b in range(own_blocks):
                total = jnp.zeros((3, BLOCK), F32)
                for l in range(listed):
                    total = total + jnp.where(
                        blocks[l] == q * own_blocks + b, terms[:, l * BLOCK : (l + 1) * BLOCK], 0.0
                    )
                term_out[q, b * 3 : (b + 1) * 3, :] = total

        @pl.loop(first, last, unroll=4)
        def _(i):
            term_copy(i).start()

    gone(rim_copy, 0)
    pltpu.make_async_copy(everyone, everyone, all_send).wait()
    pltpu.make_async_copy(term_in, term_in, term_recv).wait()

    total = jnp.sum(term_in[...], axis=0)
    for b in range(own_blocks):
        response[:, b * BLOCK : (b + 1) * BLOCK] = total[b * 3 : (b + 1) * 3, :]
    pltpu.make_async_copy(term_in, term_in, term_send).wait()


def local(n_dom, n_sub, *args):
    (
        positions,
        charges,
        polar,
        features,
        neighbours,
        send_rows,
        blocks,
        radial_in,
        radial_mid,
        radial_out,
        node_in,
        node_out,
        field_gain,
        readout,
    ) = args
    n = n_dom * n_sub
    rows = positions.shape[1]
    own_blocks = rows // BLOCK
    slots = neighbours.shape[1]
    listed = blocks.shape[0]
    layers, basis, radial = radial_in.shape
    channels = features.shape[1]
    rim = send_rows.shape[1]
    pack = channels // radial
    dma = pltpu.SemaphoreType.DMA
    operands = (
        positions,
        charges.reshape(1, -1),
        polar.reshape(1, -1),
        features,
        neighbours.T,
        send_rows,
        blocks,
        radial_in,
        radial_mid,
        radial_out,
        node_in,
        node_out,
        field_gain.reshape(1, -1),
        readout.T,
    )
    spaces = [pltpu.VMEM] * INPUTS
    spaces[6] = pltpu.SMEM
    shapes = [a.shape for a in operands]
    shapes[3] = (rows + 2 * rim, channels)
    both = pl.pallas_call(
        functools.partial(kernel, n_dom, n_sub),
        out_shape=jax.ShapeDtypeStruct((2, 3, rows), F32),
        in_specs=[pl.BlockSpec(memory_space=pl.ANY)] * INPUTS,
        out_specs=pl.BlockSpec(memory_space=pltpu.VMEM),
        scratch_shapes=[space(shape, a.dtype) for space, shape, a in zip(spaces, shapes, operands)]
        + [
            dma((INPUTS,)),
            pltpu.VMEM((own_blocks, 4, BLOCK), F32),
            pltpu.VMEM((n * own_blocks, 4, BLOCK), F32),
            pltpu.VMEM((4, listed * BLOCK), F32),
            pltpu.VMEM((listed * BLOCK, 8), F32),
            pltpu.VMEM((8, rows), F32),
            pltpu.VMEM((rows, 8), F32),
            pltpu.VMEM((rows, 8), F32),
            pltpu.VMEM((1 + ROUNDS, 2, 4, rim), F32),
            pltpu.VMEM((1 + ROUNDS, 2, 4, rim), F32),
            pltpu.VMEM((1 + ROUNDS, 4, rows), F32),
            pltpu.VMEM((1 + ROUNDS, 2, 4, rows), F32),
            pltpu.VMEM((1 + ROUNDS, 2, 4, rim), F32),
            pltpu.VMEM((2, slots, rim), jnp.int32),
            pltpu.VMEM((2, slots, rim), jnp.int32),
            pltpu.VMEM((2, 4, rim), F32),
            pltpu.VMEM((2, 4, rim), F32),
            pltpu.VMEM((5, slots, rows + 2 * rim), F32),
            pltpu.VMEM((pack, rows // STRIP, slots // pack, STRIP, rows + 2 * rim), BF16),
            pltpu.VMEM((2 * rim, rows), BF16),
            pltpu.VMEM((slots // pack * rows, pack * basis), BF16),
            pltpu.VMEM((2, slots // pack * rows, channels), BF16),
            pltpu.VMEM((layers, rows // STRIP, slots // pack, STRIP, channels), BF16),
            pltpu.VMEM((pack, rows // STRIP, slots // pack, STRIP, channels), F32),
            pltpu.VMEM((layers, pack * basis, channels), BF16),
            pltpu.VMEM((layers, 2, channels, channels), BF16),
            pltpu.VMEM((layers, pack, channels, channels), BF16),
            pltpu.VMEM((layers, rows + 2 * rim, channels), BF16),
            pltpu.VMEM((layers, 2, rim, channels), BF16),
            pltpu.VMEM((2, listed * BLOCK, 8), F32),
            pltpu.VMEM((5, rows, listed * BLOCK), F32),
            pltpu.VMEM((rows, channels), BF16),
            pltpu.VMEM((rows // STRIP, STRIP, channels), F32),
            pltpu.VMEM((3, rows), F32),
            pltpu.VMEM((3, rows), F32),
            pltpu.VMEM((3, listed * BLOCK), F32),
            pltpu.VMEM((n, own_blocks * 3, BLOCK), F32),
            pltpu.VMEM((n, own_blocks * 3, BLOCK), F32),
            dma(()),
            dma(()),
            dma((2,)),
            dma((1 + ROUNDS, 2)),
            dma((2,)),
            dma((layers, 2)),
            dma(()),
            dma(()),
            dma((2,)),
            dma((1 + ROUNDS, 2)),
            dma((2,)),
            dma((1 + ROUNDS, 2)),
            dma((2,)),
            dma((1, 2)),
            dma((2,)),
            dma((1, 2)),
        ],
        compiler_params=pltpu.CompilerParams(
            collective_id=0, has_side_effects=True, vmem_limit_bytes=40 * 2**20
        ),
    )(*(pltpu.with_memory_space_constraint(a, pltpu.HBM) for a in operands))
    return both[0], both[1]


def solution(mesh):
    sites = ("grp", "dom", "sub")
    in_specs = (
        P(None, sites),
        P(sites),
        P(sites),
        P(sites, None),
        P(sites, None),
        P(None, sites),
        P(sites),
    ) + (P(),) * 7
    out_specs = (P(None, sites), P(None, sites))
    body = functools.partial(local, mesh.shape["dom"], mesh.shape["sub"])
    return jax.shard_map(body, mesh=mesh, in_specs=in_specs, out_specs=out_specs, check_vma=False)
```

```python
import functools

import jax
import jax.numpy as jnp
from jax import lax
from jax.experimental import pallas as pl
from jax.experimental.pallas import tpu as pltpu
from jax.sharding import PartitionSpec as P

SWEEPS = 4
ROUNDS = SWEEPS // 2
BLOCK = 128
SMOOTH = 1.0
SPACING = 0.75
MESH = pl.DeviceIdType.MESH
INPUTS = 14
STRIP = 16
EARLY = 3
F32 = jnp.float32
BF16 = jnp.bfloat16


def silu_of_half(half):
    return half + half * jnp.tanh(half)


def lane_pick(rows, index):
    shape = index.shape
    return jnp.take_along_axis(
        jnp.broadcast_to(rows, shape), index, axis=1, mode="promise_in_bounds"
    )


def table_gather(pieces, local, chunk, total=None):
    if total is None:
        total = jnp.zeros(local.shape, pieces[0][1].dtype)
    for number, rows in pieces:
        total = jnp.where(chunk == number, lane_pick(rows, local), total)
    return total


def kernel(
    n_dom,
    n_sub,
    *refs,
):
    sources = refs[:INPUTS]
    (
    both,
    positions,
    charges,
    polar,
    features,
    neighbours,
    send_rows,
    blocks,
    radial_in,
    radial_mid,
    radial_out,
    node_in,
    node_out,
    field_gain,
    readout,
    in_sem,
    packet,
    everyone,
    near_rows,
    near_cols,
    own_rows,
    own_cols,
    extra_cols,
    rim_out,
    rim_in,
    flat_out,
    flat_in,
    far_in,
    lists_out,
    lists_in,
    fixed_out,
    fixed_in,
    geometry,
    hot,
    pick,
    wave,
    stage,
    third,
    edge_weight,
    wide_in,
    wide_mid,
    wide_out,
    tables,
    lent,
    lent_cols,
    reach,
    hidden_ref,
    acc,
    outside,
    pairs,
    terms,
    term_out,
    term_in,
    all_send,
    all_recv,
    rim_send,
    rim_recv,
    lift_send,
    lift_recv,
    term_send,
    term_recv,
    flat_send,
    flat_recv,
    far_send,
    far_recv,
    list_send,
    list_recv,
    fixed_send,
    fixed_recv,
    ) = refs[INPUTS:]
    g = lax.axis_index("grp")
    p = lax.axis_index("dom") * n_sub + lax.axis_index("sub")
    site_result, response = both.at[0], both.at[1]
    n = n_dom * n_sub
    rows = positions.shape[1]
    own_blocks = rows // BLOCK
    slots = neighbours.shape[0]
    listed = blocks.shape[0]
    layers, basis, radial = radial_in.shape
    channels = features.shape[1]
    rim = send_rows.shape[1]
    pack = channels // radial
    groups = slots // pack
    strips = rows // STRIP
    other = 1 - g
    held = (
        positions,
        charges,
        polar,
        features,
        neighbours,
        send_rows,
        blocks,
        radial_in,
        radial_mid,
        radial_out,
        node_in,
        node_out,
        field_gain,
        readout,
    )
    early = (0, 1, 2, 4, 5, 6)
    late = (7, 8, 9, 3, 10, 11, 12, 13)
    spread_needs = 4

    def load(number):
        target = held[number]
        if number == 3:
            target = target.at[pl.ds(0, rows)]
        return pltpu.make_async_copy(sources[number], target, in_sem.at[number])

    for number in early:
        load(number).start()

    def place(group, q):
        return (group, lax.div(q, n_sub), lax.rem(q, n_sub))

    def peer(i):
        if n % 4:
            return lax.rem(p + i, n)
        quarter = n // 4
        second = lax.div(2 * p, n)
        turn = lax.div(i, quarter)
        far = second * turn + (1 - second) * (3 - turn)
        return far * quarter + lax.rem(p + i, quarter)

    barrier = pltpu.get_barrier_semaphore()

    @pl.loop(0, n)
    def _(i):
        pl.semaphore_signal(barrier, inc=1, device_id=place(other, peer(i)), device_id_type=MESH)

    @pl.when(p > 0)
    def _():
        pl.semaphore_signal(barrier, inc=1, device_id=place(g, p - 1), device_id_type=MESH)

    @pl.when(p < n - 1)
    def _():
        pl.semaphore_signal(barrier, inc=1, device_id=place(g, p + 1), device_id_type=MESH)

    @pl.when(p > 1)
    def _():
        pl.semaphore_signal(barrier, inc=1, device_id=place(g, p - 2), device_id_type=MESH)

    @pl.when(p < n - 2)
    def _():
        pl.semaphore_signal(barrier, inc=1, device_id=place(g, p + 2), device_id_type=MESH)

    @pl.when(g == 0)
    def _():
        for number in late:
            load(number).start()

    own_rows[...] = jnp.zeros_like(own_rows)
    for number in early:
        load(number).wait()
    own_rows[0:3, :] = positions[...]
    own_rows[3:4, :] = charges[...]
    own = own_rows[...]
    for b in range(own_blocks):
        packet[b] = own[0:4, b * BLOCK : (b + 1) * BLOCK]

    def fill(target, values):
        for side in range(2):
            index = jnp.broadcast_to(send_rows[side : side + 1, :], (values.shape[0], rim))
            target[side] = table_gather(
                [(c, values[:, c * BLOCK : (c + 1) * BLOCK]) for c in range(own_blocks)],
                index & (BLOCK - 1),
                lax.shift_right_logical(index, 7),
            )

    def fill_rims(step, values):
        fill(rim_out.at[step], values)

    def side_copy(src, dst, send, recv, step, side, q):
        return pltpu.make_async_remote_copy(
            src_ref=src,
            dst_ref=dst,
            send_sem=send.at[side],
            recv_sem=recv.at[step, side],
            device_id=place(g, q),
            device_id_type=MESH,
        )

    def rim_copy(step, side, q):
        return side_copy(
            rim_out.at[step, side], rim_in.at[step, side], rim_send, rim_recv, step, side, q
        )

    def lift_copy(layer, side, q):
        target = tables.at[layer] if layer else features
        return side_copy(
            lent.at[layer, side],
            target.at[pl.ds(rows + side * rim, rim)],
            lift_send,
            lift_recv,
            layer,
            side,
            q,
        )

    def flat_copy(step, side, q):
        return side_copy(
            flat_out.at[step], flat_in.at[step, side], flat_send, flat_recv, step, side, q
        )

    def far_copy(step, side, q):
        return side_copy(
            rim_out.at[step, side], far_in.at[step, side], far_send, far_recv, step, side, q
        )

    def list_copy(step, side, q):
        return side_copy(
            lists_out.at[side], lists_in.at[side], list_send, list_recv, step, side, q
        )

    def fixed_copy(step, side, q):
        return side_copy(
            fixed_out.at[side], fixed_in.at[side], fixed_send, fixed_recv, step, side, q
        )

    def start(copy, step, away=1):
        @pl.when(p < n - away)
        def _():
            copy(step, 0, p + away).start()

        @pl.when(p > away - 1)
        def _():
            copy(step, 1, p - away).start()

    def arrive(copy, step, away=1):
        @pl.when(p > away - 1)
        def _():
            copy(step, 0, p - away).wait_recv()

        @pl.when(p < n - away)
        def _():
            copy(step, 1, p + away).wait_recv()

    def gone(copy, step, away=1):
        @pl.when(p < n - away)
        def _():
            copy(step, 0, p + away).wait_send()

        @pl.when(p > away - 1)
        def _():
            copy(step, 1, p - away).wait_send()

    def mark_slots(span):
        width = rows + 2 * rim
        lane = lax.broadcasted_iota(jnp.int32, (rows, width), 1).astype(jnp.int16)
        listing = jnp.concatenate(
            [neighbours[...].astype(F32), jnp.zeros((BLOCK - slots, rows), F32)], axis=0
        ).T.astype(jnp.int32)
        one, none = jnp.ones((rows, width), BF16), jnp.zeros((rows, width), BF16)
        for k in span:
            entry = jnp.broadcast_to(listing[:, k : k + 1], (rows, BLOCK)).astype(jnp.int16)
            entry = jnp.concatenate([entry] * (width // BLOCK), axis=1)
            mark = jnp.where(entry == lane, one, none)
            hot[k % pack, :, k // pack] = mark.reshape(strips, STRIP, width)

    def mark_lent():
        lists = jnp.concatenate(
            [send_rows[...].astype(F32), jnp.zeros((6, rim), F32)], axis=0
        ).T.astype(jnp.int32)
        site = lax.broadcasted_iota(jnp.int32, (rim, rows), 1)
        for side in range(2):
            pick[side * rim : (side + 1) * rim, :] = jnp.where(
                lists[:, side : side + 1] == site, 1.0, 0.0
            ).astype(BF16)

    def spread():
        for number in late[:spread_needs]:
            load(number).wait()
        spread_r = (
            lax.broadcasted_iota(jnp.int32, (channels, radial), 0) % radial
            == lax.broadcasted_iota(jnp.int32, (channels, radial), 1)
        ).astype(F32).astype(BF16)
        spread_c = (
            lax.broadcasted_iota(jnp.int32, (radial, channels), 1) % radial
            == lax.broadcasted_iota(jnp.int32, (radial, channels), 0)
        ).astype(F32).astype(BF16)
        same_in = (
            lax.broadcasted_iota(jnp.int32, (pack * basis, channels), 0) // basis
            == lax.broadcasted_iota(jnp.int32, (pack * basis, channels), 1) // radial
        )
        same_mid = (
            lax.broadcasted_iota(jnp.int32, (channels, channels), 0) // radial
            == lax.broadcasted_iota(jnp.int32, (channels, channels), 1) // radial
        )
        for layer in range(layers):
            flat = jnp.dot(radial_in[layer], spread_c, preferred_element_type=F32)
            wide_in[layer] = jnp.where(
                same_in, jnp.concatenate([0.5 * flat] * pack, axis=0), 0.0
            ).astype(BF16)
            for m in range(2):
                flat = jnp.dot(
                    jnp.dot(spread_r, radial_mid[layer, m], preferred_element_type=F32).astype(
                        BF16
                    ),
                    spread_c,
                    preferred_element_type=F32,
                )
                wide_mid[layer, m] = jnp.where(same_mid, 0.5 * flat, 0.0).astype(BF16)
            for j in range(pack):
                wide_out[layer, j] = jnp.zeros((channels, channels), BF16)
                wide_out[layer, j, j * radial : (j + 1) * radial, :] = radial_out[layer]

    def lend(layer, values):
        picked = jnp.dot(pick[...], values, preferred_element_type=F32).astype(BF16)
        lent[layer] = picked.reshape(2, rim, channels)

    fill_rims(0, own[0:4])

    @pl.when(g == 0)
    def _():
        spot = lax.broadcasted_iota(jnp.int32, (1, rim), 1)
        names = jnp.zeros((1, rim), F32)
        for l in range(listed):
            names = jnp.where(spot == l, blocks[l].astype(F32), names)
        for side in range(2):
            rim_out[0, side, 3:4, :] = names

    @pl.when(p == 0)
    def _():
        for step in range(1 + ROUNDS):
            rim_in[step, 0] = jnp.zeros((4, rim), F32)
        features[rows : rows + rim] = jnp.zeros((rim, channels), BF16)
        for layer in range(1, layers):
            tables[layer, rows : rows + rim] = jnp.zeros((rim, channels), BF16)

    @pl.when(p == n - 1)
    def _():
        for step in range(1 + ROUNDS):
            rim_in[step, 1] = jnp.zeros((4, rim), F32)
        features[rows + rim :] = jnp.zeros((rim, channels), BF16)
        for layer in range(1, layers):
            tables[layer, rows + rim :] = jnp.zeros((rim, channels), BF16)

    def clear(side, away):
        for step in range(1 + ROUNDS):
            far_in[step, side] = jnp.zeros((4, rim), F32)
            if away == 1:
                flat_in[step, side] = jnp.zeros((4, rows), F32)
        if away == 1:
            lists_in[side] = jnp.zeros((slots, rim), jnp.int32)
            fixed_in[side] = jnp.zeros((4, rim), F32)

    @pl.when(g == 1)
    def _():
        flat_out[0] = own[0:4]
        fill(lists_out, neighbours[...])
        for side, ends in enumerate(((0, 1), (n - 1, n - 2))):
            pl.when(p == ends[0])(functools.partial(clear, side, 1))
            pl.when(p == ends[1])(functools.partial(clear, side, 2))

    @pl.when(g == 0)
    def _():
        mark_slots(range(slots // 2))

    sides = [p > 0, p < n - 1, p > 1, p < n - 2]
    pl.semaphore_wait(barrier, n + sum(side.astype(jnp.int32) for side in sides))

    def packet_copy(i):
        return pltpu.make_async_remote_copy(
            src_ref=packet,
            dst_ref=everyone.at[pl.ds(p * own_blocks, own_blocks)],
            send_sem=all_send,
            recv_sem=all_recv,
            device_id=place(other, peer(i)),
            device_id_type=MESH,
        )

    start(rim_copy, 0)

    @pl.loop(0, n, unroll=4)
    def _(i):
        packet_copy(i).start()

    @pl.when(g == 0)
    def _():
        mark_lent()
        spread()
        mark_slots(range(slots // 2, slots))
        lend(0, features[0:rows])

    own_cols[...] = own.T

    def field(targets, source_cols, count):
        x, y, z = (targets[c : c + 1, :] for c in range(3))

        def step(i, sums):
            source = source_cols[pl.ds(pl.multiple_of(i * 8, 8), 8), :]
            rx = x - source[:, 0:1]
            ry = y - source[:, 1:2]
            rz = z - source[:, 2:3]
            w = lax.rsqrt(rx * rx + ry * ry + rz * rz + SMOOTH)
            s = source[:, 3:4] * (w * w * w)
            return (sums[0] + rx * s, sums[1] + ry * s, sums[2] + rz * s)

        zero = jnp.zeros((8, targets.shape[1]), F32)
        sums = lax.fori_loop(0, count // 8, step, (zero, zero, zero), unroll=True)
        return [jnp.sum(s, axis=0, keepdims=True) for s in sums]

    def term_geometry(dipole, part, parts):
        x, y, z = (near_rows[c : c + 1, :] for c in range(3))
        for i in range(part * rows // 8 // parts, (part + 1) * rows // 8 // parts):
            at = slice(i * 8, i * 8 + 8)
            source = own_cols[at, :]
            r = (x - source[:, 0:1], y - source[:, 1:2], z - source[:, 2:3])
            w = lax.rsqrt(r[0] * r[0] + r[1] * r[1] + r[2] * r[2] + SMOOTH)
            w2 = w * w
            w3 = w2 * w
            for c in range(3):
                reach[c, at, :] = r[c] if dipole else r[c] * w3
            if dipole:
                reach[3, at, :] = w3
                reach[4, at, :] = 3.0 * (w3 * w2)

    def send_terms(dipole):
        def step(i, sums):
            at = pl.ds(pl.multiple_of(i * 8, 8), 8)
            d = extra_cols[at, :]
            r = [reach[c, at, :] for c in range(3)]
            if not dipole:
                return tuple(sums[c] + r[c] * d[:, 0:1] for c in range(3))
            w3 = reach[3, at, :]
            d = [d[:, c : c + 1] for c in range(3)]
            s = (r[0] * d[0] + r[1] * d[1] + r[2] * d[2]) * reach[4, at, :]
            return tuple(sums[c] + (r[c] * s - d[c] * w3) for c in range(3))

        zero = jnp.zeros((8, listed * BLOCK), F32)
        sums = lax.fori_loop(0, rows // 8, step, (zero, zero, zero), unroll=True)
        for c in range(3):
            terms[c : c + 1, :] = jnp.sum(sums[c], axis=0, keepdims=True)

    def lent_pieces(side, c, flat, mine, far):
        flat, mine, far = (rows_[c : c + 1, :] for rows_ in (flat, mine, far))
        rims = (far, mine) if side == 0 else (mine, far)
        return [(b, flat[:, b * BLOCK : (b + 1) * BLOCK]) for b in range(own_blocks)] + [
            (own_blocks + i, rims[i]) for i in range(2)
        ]

    def lent_geometry():
        arrive(flat_copy, 0)
        arrive(far_copy, 0, 2)
        arrive(list_copy, 0)
        for side in range(2):
            at = slice(rows + side * rim, rows + (side + 1) * rim)
            index = lists_in[side]
            local = index & (BLOCK - 1)
            chunk = lax.shift_right_logical(index, 7)
            offset = [
                rim_in[0, side, c : c + 1, :]
                - table_gather(
                    lent_pieces(side, c, flat_in[0, side], rim_out[0, 1 - side], far_in[0, side]),
                    local,
                    chunk,
                )
                for c in range(3)
            ]
            w = lax.rsqrt(
                offset[0] * offset[0] + offset[1] * offset[1] + offset[2] * offset[2] + SMOOTH
            )
            w2 = w * w
            w3 = w2 * w
            for c in range(3):
                geometry[c, :, at] = offset[c]
            geometry[3, :, at] = w3
            geometry[4, :, at] = 3.0 * (w3 * w2)

    def edge_index(tile):
        index = neighbours[:, tile * BLOCK : (tile + 1) * BLOCK]
        return index & (BLOCK - 1), lax.shift_right_logical(index, 7)

    def own_edges(count):
        return [
            [
                table_gather(
                    [(b, own_rows[c : c + 1, b * BLOCK : (b + 1) * BLOCK]) for b in range(own_blocks)],
                    *edge_index(tile),
                )
                for c in range(count)
            ]
            for tile in range(own_blocks)
        ]

    def edges(begun):
        for tile in range(own_blocks):
            at = slice(tile * BLOCK, (tile + 1) * BLOCK)
            local, chunk = edge_index(tile)
            picked = [
                table_gather(
                    [(own_blocks + side, rim_in[0, side, c : c + 1, :]) for side in range(2)],
                    local,
                    chunk,
                    value,
                )
                for c, value in enumerate(begun[tile])
            ]
            ox, oy, oz = (own_rows[c : c + 1, at] - picked[c] for c in range(3))
            dist_sq = ox * ox + oy * oy + oz * oz + SMOOTH
            yield at, (ox, oy, oz), dist_sq, picked[-1]

    centre = lax.broadcasted_iota(jnp.int32, (basis, rows), 0).astype(F32) * SPACING

    def waves():
        for q in range(groups):
            parts = []
            for j in range(pack):
                away = jnp.broadcast_to(geometry[0, q * pack + j : q * pack + j + 1, 0:rows], (basis, rows))
                away = away - centre
                parts.append(jnp.exp(-(away * away)))
            turned = jnp.concatenate(parts, axis=0).T
            wave[q * rows : (q + 1) * rows, :] = turned.astype(BF16)

    def radial_net(layer):
        quarter = max(groups // 4, 1)
        spans = [range(q, q + quarter) for q in range(0, groups, quarter)]
        for step in range(3):
            for part, span in enumerate(spans):
                at = slice(span[0] * rows, (span[-1] + 1) * rows)
                if step == 0:
                    source, weight = wave[at, :], wide_in[layer]
                else:
                    source, weight = stage[step - 1, at, :], wide_mid[layer, step - 1]
                h = silu_of_half(jnp.dot(source, weight, preferred_element_type=F32)).astype(BF16)
                if step < 2:
                    stage[step, at, :] = h
                else:
                    for i, q in enumerate(span):
                        third[layer, :, q] = h[i * rows : (i + 1) * rows].reshape(
                            strips, STRIP, channels
                        )

    def edge_part(layer, j):
        edge_weight[j] = jnp.dot(
            third[layer].reshape(groups * rows, channels),
            wide_out[layer, j],
            preferred_element_type=F32,
        ).reshape(strips, groups, STRIP, channels)

    def own_part(layer, beside):
        for j in range(pack):
            beside(j)
            if layer or j >= EARLY:
                edge_part(layer, j)
            gather_part(layer, j, 0, rows)

    def rim_part(layer):
        for j in range(pack):
            gather_part(layer, j, rows, 2 * rim)

    def gather_part(layer, j, first, count):
        source = jnp.dot(
            hot[j, :, :, :, first : first + count].reshape(groups * rows, count),
            tables[layer, first : first + count],
            preferred_element_type=F32,
        )
        product = edge_weight[j] * source.reshape(strips, groups, STRIP, channels)
        total = jnp.sum(product, axis=1)
        if first or j:
            total = acc[...] + total
        acc[...] = total

    @pl.when(g == 0)
    def _():
        begun = own_edges(3)
        start(lift_copy, 0)
        arrive(rim_copy, 0)
        for at, _, dist_sq, _ in edges(begun):
            geometry[0, :, at] = jnp.sqrt(dist_sq)
        waves()
        radial_net(0)

    @pl.when(g == 1)
    def _():
        begun = own_edges(4)
        arrive(rim_copy, 0)
        start(flat_copy, 0)
        start(far_copy, 0, 2)
        start(list_copy, 0)
        for at, offset, dist_sq, source_charge in edges(begun):
            w = lax.rsqrt(dist_sq)
            w2 = w * w
            w3 = w2 * w
            s = source_charge * w3
            for c in range(3):
                geometry[c, :, at] = offset[c]
                extra = jnp.sum(offset[c] * s, axis=0, keepdims=True)
                pairs[c : c + 1, at] = extra
            geometry[3, :, at] = w3
            geometry[4, :, at] = 3.0 * (w3 * w2)

    pltpu.make_async_copy(everyone, everyone, all_recv).wait()
    for l in range(listed):
        tile = everyone[blocks[l]]
        near_rows[:, l * BLOCK : (l + 1) * BLOCK] = tile
        near_cols[l * BLOCK : (l + 1) * BLOCK, :] = jnp.concatenate(
            [tile, jnp.zeros_like(tile)], axis=0
        ).T

    def lent_near():
        names = [
            [jnp.broadcast_to(rim_in[0, side, 3:4, l : l + 1], (4, BLOCK)) for l in range(listed)]
            for side in range(2)
        ]

        def step(b, found):
            tile = everyone[b]
            return tuple(
                tuple(
                    jnp.where(names[side][l] == b.astype(F32), tile, found[side][l])
                    for l in range(listed)
                )
                for side in range(2)
            )

        blank = jnp.zeros((4, BLOCK), F32)
        found = lax.fori_loop(
            0, n * own_blocks, step, ((blank,) * listed,) * 2, unroll=max(8, min(32, n * own_blocks))
        )
        for side in range(2):
            for l in range(listed):
                lent_cols[side, l * BLOCK : (l + 1) * BLOCK, :] = jnp.concatenate(
                    [found[side][l], blank], axis=0
                ).T

    @pl.when(g == 0)
    def _():
        for number in late[spread_needs:]:
            load(number).wait()

        def strength_of(fields):
            fx, fy, fz = fields
            return jnp.sqrt(1.0 + fx * fx + fy * fy + fz * fz)

        def column_of(strength):
            return jnp.broadcast_to(strength, (8, strength.shape[1])).T[:, 0:1]

        def embed(column, at):
            return (features[at].astype(F32) + column * field_gain[...]).astype(BF16)

        def lent_field(side):
            return field(rim_in[0, side], lent_cols.at[side], listed * BLOCK)

        for j in range(EARLY):
            edge_part(0, j)
        strength = strength_of(field(own, near_cols, listed * BLOCK))
        site_result[2:3, :] = strength
        hidden_ref[...] = embed(column_of(strength), slice(0, rows))
        tables[0, 0:rows] = jnp.dot(
            hidden_ref[...], node_in[0], preferred_element_type=F32
        ).astype(BF16)
        fields, columns = [], []

        def lent_lift(j):
            if j == 0:
                lent_near()
            if j < 2:
                fields.append(lent_field(j))
            if j == 2:
                columns.extend(column_of(strength_of(part)) for part in fields)
            if j == pack - 1:
                arrive(lift_copy, 0)
                ends = (p > 0, p < n - 1)
                for side in range(2):
                    at = slice(rows + side * rim, rows + (side + 1) * rim)
                    hidden = embed(columns[side], at)
                    lifted = jnp.dot(hidden, node_in[0], preferred_element_type=F32)
                    tables[0, at] = jnp.where(ends[side], lifted, 0.0).astype(BF16)

        def lift(layer):
            lifted = jnp.dot(
                hidden_ref[...], node_in[layer], preferred_element_type=F32
            ).astype(BF16)
            lend(layer, lifted)
            gone(lift_copy, layer - 1)
            start(lift_copy, layer)
            tables[layer, 0:rows] = lifted

        for layer in range(layers):
            def beside(j, layer=layer):
                if layer == layers - 1:
                    term_geometry(False, j, pack)

            if layer:
                lift(layer)
                radial_net(layer)
            own_part(layer, beside if layer else lent_lift)
            if layer:
                arrive(lift_copy, layer)
            rim_part(layer)
            message = (acc[...].reshape(rows, channels) * (1.0 / slots)).astype(BF16)
            update = silu_of_half(
                0.5 * jnp.dot(message, node_out[layer], preferred_element_type=F32)
            )
            hidden_ref[...] = (hidden_ref[...].astype(F32) + update).astype(BF16)

        across = (((1,), (1,)), ((), ()))
        extra_cols[:, 0:2] = lax.dot_general(
            hidden_ref[...], readout[...], across, preferred_element_type=F32
        )
        site_result[0:2, :] = lax.dot_general(
            readout[...], hidden_ref[...], across, preferred_element_type=F32
        )
        send_terms(False)
        gone(lift_copy, layers - 1)

    @pl.when(g == 1)
    def _():
        out = field(own, near_cols, listed * BLOCK)
        for c in range(3):
            outside[c : c + 1, :] = out[c]
        gain = polar[...]
        outside[...] = outside[...] + pairs[...]
        dipole = [gain * outside[c : c + 1, :] for c in range(3)]

        def induced(at, index, pieces, begun=(None, None, None)):
            local = index & (BLOCK - 1)
            chunk = lax.shift_right_logical(index, 7)
            d = [table_gather(pieces(c), local, chunk, begun[c]) for c in range(3)]
            r = [geometry[c, :, at] for c in range(3)]
            w3 = geometry[3, :, at]
            s = (r[0] * d[0] + r[1] * d[1] + r[2] * d[2]) * geometry[4, :, at]
            return [jnp.sum(r[c] * s - d[c] * w3, axis=0, keepdims=True) for c in range(3)]

        def own_pieces(c, values):
            return [(b, values[c][:, b * BLOCK : (b + 1) * BLOCK]) for b in range(own_blocks)]

        def own_sweep(values, rims, begun):
            fresh = [[], [], []]
            for tile in range(own_blocks):
                at = slice(tile * BLOCK, (tile + 1) * BLOCK)

                def pieces(c):
                    ends = [(own_blocks + side, rims(side, c)) for side in range(2)]
                    return ends if begun else own_pieces(c, values) + ends

                totals = induced(
                    at, neighbours[:, at], pieces, begun[tile] if begun else (None, None, None)
                )
                for c in range(3):
                    fresh[c].append(gain[:, at] * (outside[c : c + 1, at] + totals[c]))
            return [jnp.concatenate(f, axis=1) for f in fresh]

        for sweep in range(ROUNDS):
            step = 1 + sweep
            values = jnp.concatenate(dipole + [jnp.zeros((1, rows), F32)], axis=0)
            fill_rims(step, values)
            gone(rim_copy, step - 1)
            gone(far_copy, step - 1, 2)
            gone(flat_copy, step - 1)
            start(rim_copy, step)
            start(far_copy, step, 2)
            flat_out[step] = values
            start(flat_copy, step)
            if sweep == 0:
                fill(fixed_out, jnp.concatenate([outside[...], gain], axis=0))
                start(fixed_copy, 0)
            begun = []
            for tile in range(own_blocks):
                index = neighbours[:, tile * BLOCK : (tile + 1) * BLOCK]
                local = index & (BLOCK - 1)
                chunk = lax.shift_right_logical(index, 7)
                begun.append([table_gather(own_pieces(c, dipole), local, chunk) for c in range(3)])
            if sweep == 0:
                lent_geometry()
                term_geometry(True, 0, 1)
            arrive(rim_copy, step)
            arrive(far_copy, step, 2)
            arrive(flat_copy, step)
            if sweep == 0:
                arrive(fixed_copy, 0)
            middle = own_sweep(
                dipole, lambda side, c: rim_in[step, side, c : c + 1, :], begun
            )
            lent_middle = []
            for side in range(2):
                at = slice(rows + side * rim, rows + (side + 1) * rim)
                totals = induced(
                    at,
                    lists_in[side],
                    lambda c: lent_pieces(
                        side, c, flat_in[step, side], rim_out[step, 1 - side], far_in[step, side]
                    ),
                )
                lent_middle.append([
                    fixed_in[side, 3:4, :] * (fixed_in[side, c : c + 1, :] + totals[c])
                    for c in range(3)
                ])
            dipole = own_sweep(middle, lambda side, c: lent_middle[side][c], None)
        for c in range(3):
            site_result[c : c + 1, :] = dipole[c]
        stacked = jnp.concatenate(dipole + [jnp.zeros((5, rows), F32)], axis=0)
        extra_cols[...] = stacked.T
        send_terms(True)
        gone(far_copy, ROUNDS, 2)
        gone(flat_copy, ROUNDS)
        gone(list_copy, 0)
        gone(fixed_copy, 0)

    def term_copy(i):
        return pltpu.make_async_remote_copy(
            src_ref=term_out.at[peer(i)],
            dst_ref=term_in.at[p],
            send_sem=term_send,
            recv_sem=term_recv,
            device_id=place(other, peer(i)),
            device_id_type=MESH,
        )

    for first, last in ((0, n // 2), (n // 2, n)):

        @pl.loop(first, last, unroll=min(n // 2, 8))
        def _(i):
            q = peer(i)
            for b in range(own_blocks):
                total = jnp.zeros((3, BLOCK), F32)
                for l in range(listed):
                    total = total + jnp.where(
                        blocks[l] == q * own_blocks + b, terms[:, l * BLOCK : (l + 1) * BLOCK], 0.0
                    )
                term_out[q, b * 3 : (b + 1) * 3, :] = total

        @pl.loop(first, last, unroll=4)
        def _(i):
            term_copy(i).start()

    gone(rim_copy, 0)
    pltpu.make_async_copy(everyone, everyone, all_send).wait()
    pltpu.make_async_copy(term_in, term_in, term_recv).wait()

    total = jnp.sum(term_in[...], axis=0)
    for b in range(own_blocks):
        response[:, b * BLOCK : (b + 1) * BLOCK] = total[b * 3 : (b + 1) * 3, :]
    pltpu.make_async_copy(term_in, term_in, term_send).wait()


def local(n_dom, n_sub, *args):
    (
        positions,
        charges,
        polar,
        features,
        neighbours,
        send_rows,
        blocks,
        radial_in,
        radial_mid,
        radial_out,
        node_in,
        node_out,
        field_gain,
        readout,
    ) = args
    n = n_dom * n_sub
    rows = positions.shape[1]
    own_blocks = rows // BLOCK
    slots = neighbours.shape[1]
    listed = blocks.shape[0]
    layers, basis, radial = radial_in.shape
    channels = features.shape[1]
    rim = send_rows.shape[1]
    pack = channels // radial
    dma = pltpu.SemaphoreType.DMA
    operands = (
        positions,
        charges.reshape(1, -1),
        polar.reshape(1, -1),
        features,
        neighbours.T,
        send_rows,
        blocks,
        radial_in,
        radial_mid,
        radial_out,
        node_in,
        node_out,
        field_gain.reshape(1, -1),
        readout.T,
    )
    spaces = [pltpu.VMEM] * INPUTS
    spaces[6] = pltpu.SMEM
    shapes = [a.shape for a in operands]
    shapes[3] = (rows + 2 * rim, channels)
    both = pl.pallas_call(
        functools.partial(kernel, n_dom, n_sub),
        out_shape=jax.ShapeDtypeStruct((2, 3, rows), F32),
        in_specs=[pl.BlockSpec(memory_space=pl.ANY)] * INPUTS,
        out_specs=pl.BlockSpec(memory_space=pltpu.VMEM),
        scratch_shapes=[space(shape, a.dtype) for space, shape, a in zip(spaces, shapes, operands)]
        + [
            dma((INPUTS,)),
            pltpu.VMEM((own_blocks, 4, BLOCK), F32),
            pltpu.VMEM((n * own_blocks, 4, BLOCK), F32),
            pltpu.VMEM((4, listed * BLOCK), F32),
            pltpu.VMEM((listed * BLOCK, 8), F32),
            pltpu.VMEM((8, rows), F32),
            pltpu.VMEM((rows, 8), F32),
            pltpu.VMEM((rows, 8), F32),
            pltpu.VMEM((1 + ROUNDS, 2, 4, rim), F32),
            pltpu.VMEM((1 + ROUNDS, 2, 4, rim), F32),
            pltpu.VMEM((1 + ROUNDS, 4, rows), F32),
            pltpu.VMEM((1 + ROUNDS, 2, 4, rows), F32),
            pltpu.VMEM((1 + ROUNDS, 2, 4, rim), F32),
            pltpu.VMEM((2, slots, rim), jnp.int32),
            pltpu.VMEM((2, slots, rim), jnp.int32),
            pltpu.VMEM((2, 4, rim), F32),
            pltpu.VMEM((2, 4, rim), F32),
            pltpu.VMEM((5, slots, rows + 2 * rim), F32),
            pltpu.VMEM((pack, rows // STRIP, slots // pack, STRIP, rows + 2 * rim), BF16),
            pltpu.VMEM((2 * rim, rows), BF16),
            pltpu.VMEM((slots // pack * rows, pack * basis), BF16),
            pltpu.VMEM((2, slots // pack * rows, channels), BF16),
            pltpu.VMEM((layers, rows // STRIP, slots // pack, STRIP, channels), BF16),
            pltpu.VMEM((pack, rows // STRIP, slots // pack, STRIP, channels), F32),
            pltpu.VMEM((layers, pack * basis, channels), BF16),
            pltpu.VMEM((layers, 2, channels, channels), BF16),
            pltpu.VMEM((layers, pack, channels, channels), BF16),
            pltpu.VMEM((layers, rows + 2 * rim, channels), BF16),
            pltpu.VMEM((layers, 2, rim, channels), BF16),
            pltpu.VMEM((2, listed * BLOCK, 8), F32),
            pltpu.VMEM((5, rows, listed * BLOCK), F32),
            pltpu.VMEM((rows, channels), BF16),
            pltpu.VMEM((rows // STRIP, STRIP, channels), F32),
            pltpu.VMEM((3, rows), F32),
            pltpu.VMEM((3, rows), F32),
            pltpu.VMEM((3, listed * BLOCK), F32),
            pltpu.VMEM((n, own_blocks * 3, BLOCK), F32),
            pltpu.VMEM((n, own_blocks * 3, BLOCK), F32),
            dma(()),
            dma(()),
            dma((2,)),
            dma((1 + ROUNDS, 2)),
            dma((2,)),
            dma((layers, 2)),
            dma(()),
            dma(()),
            dma((2,)),
            dma((1 + ROUNDS, 2)),
            dma((2,)),
            dma((1 + ROUNDS, 2)),
            dma((2,)),
            dma((1, 2)),
            dma((2,)),
            dma((1, 2)),
        ],
        compiler_params=pltpu.CompilerParams(
            collective_id=0, has_side_effects=True, vmem_limit_bytes=40 * 2**20
        ),
    )(*(pltpu.with_memory_space_constraint(a, pltpu.HBM) for a in operands))
    return both[0], both[1]


def solution(mesh):
    sites = ("grp", "dom", "sub")
    in_specs = (
        P(None, sites),
        P(sites),
        P(sites),
        P(sites, None),
        P(sites, None),
        P(None, sites),
        P(sites),
    ) + (P(),) * 7
    out_specs = (P(None, sites), P(None, sites))
    body = functools.partial(local, mesh.shape["dom"], mesh.shape["sub"])
    return jax.shard_map(body, mesh=mesh, in_specs=in_specs, out_specs=out_specs, check_vma=False)
```
